128 devices in a mesh: gx: 8 (over y, core), gy: 16 (over x, z).
Axes of the slice: x: 4, y: 4, z: 4, core: 2. Of those that a mesh axis runs over, the one named last changes fastest.
Arguments:
- density: float32 [262144, 256], P(('gx', 'gy')), may hold values from -6 to 6
- cell_index: int32 [262144], P(('gx', 'gy')), may hold values from 0 to 32767
- live_batches: int32 [128], P(('gx', 'gy')), may hold values from 0 to 32, as said below
- propagator: float32 [256, 768], replicated
- dipoles: float32 [2, 256], replicated, may hold values from -0.375 to 0.375
- electric_x: float32 [1024, 4096], P('gx', 'gy'), may hold values from -6 to 6
- electric_y: float32 [1024, 4096], P('gx', 'gy'), may hold values from -6 to 6
- magnetic_z: float32 [1024, 4096], P('gx', 'gy'), may hold values from -6 to 6
Outputs:
- evolved_density: float32 [262144, 256], P(('gx', 'gy'))
- evolved_x: float32 [1024, 4096], P('gx', 'gy')
- evolved_y: float32 [1024, 4096], P('gx', 'gy')
- evolved_z: float32 [1024, 4096], P('gx', 'gy')
The draws below stay inside these ranges and needn't reach their ends.
Inputs may be any that keep to these rules, and one draw needn't show every extreme that they name: `live_batches`: each entry is a multiple of 16; the 16 entries of devices that share a gx index sum to 256, and among them one is 32 and one is 0.
All inputs are finite; a program needn't handle non-finite values.
Results may differ from the reference program's by a relative error of at most 0.0003.
Values sent between devices are 32-bit elements; how exact they have to be, the bound alone decides.
No kernel may reach another device: no remote copies, remote signals or barrier semaphores. Data moves between devices by JAX's collectives and lax.ppermute only.
A program may use at most 128 MiB of HBM per device.

```python
import jax
import jax.numpy as jnp
from jax import lax

S2 = 256
CX = 128
CY = 256
BATCH = 64
SB = 32
STEPS = 3
SLOTS = 2048
MOLS = 262144
NX = 1024
NY = 4096
N_GX = 8
N_GY = 16
DEVICES = 128


def draw_live_batches(key, part):
    largest = SB // N_GY
    half = N_GY // 2

    def one_row(subkey):
        first, second = jax.random.split(subkey)
        picks = jax.random.randint(first, (half,), 0, largest + 1)
        picks = picks.at[0].set(0)
        paired = jnp.concatenate([picks, largest - picks])
        order = jax.random.permutation(second, N_GY)
        return paired[order] * N_GY
    return jax.vmap(one_row)(jax.random.split(key, N_GX)).reshape(-1).astype(jnp.int32)


def draw_propagator(key, part):
    noise = jax.random.normal(key, (S2, 3 * S2), jnp.float32)
    blocks = noise * (0.5 / jnp.sqrt(jnp.float32(S2)))
    blocks = blocks.at[:, :S2].add(0.7 * jnp.eye(S2, dtype=jnp.float32))
    return blocks.astype(jnp.float32)


def touch_ends(result, own_key, smallest, high):
    longest = result.shape.index(max(result.shape))
    spots = []
    for shift in (0, 1):
        where = [jax.random.randint(jax.random.fold_in(own_key, axis), (), 0, length) for axis, length in enumerate(result.shape)]
        where[longest] = (where[longest] + shift) % result.shape[longest]
        spots.append(tuple(where))
    return result.at[spots[0]].set(smallest).at[spots[1]].set(high)


def block_scale(stream_key, extent, pieces, smallest, high):
    gain = 1.0
    for dim, parts in pieces:
        heights = jax.random.uniform(jax.random.fold_in(jax.random.fold_in(stream_key, 6), dim), (parts,), jnp.float32, smallest / len(pieces), high / len(pieces))
        gain = gain * jnp.repeat(jnp.exp(heights), extent[dim] // parts).reshape((-1,) + (1,) * (len(extent) - 1 - dim))
    return gain


def normal_values(key, extent, scale, bound, shards=(), held_as=jnp.bfloat16):
    drawn = jax.random.normal(key, extent, jnp.float32) * scale
    if len(shards) > 0:
        drawn = block_scale(key, extent, shards, -0.22, 0.18) * drawn
    return jnp.clip(drawn, min=-bound, max=bound).astype(held_as)


def setup_inputs(seed: int = 0) -> dict:
    key_of = jax.random.split(jax.random.key(seed), 9)
    return {
        "density": normal_values(key_of[0], (MOLS, S2), 1.0, 6.0, ((0, 128),), jnp.float32),
        "cell_index": touch_ends(jax.random.randint(key_of[1], (MOLS,), 0, CX * CY), jax.random.fold_in(key_of[1], 1), 0, (CX * CY) - 1).astype(jnp.int32),
        "live_batches": draw_live_batches(jax.random.fold_in(key_of[8], 71), 0),
        "propagator": draw_propagator(jax.random.fold_in(key_of[8], 71), 0),
        "dipoles": normal_values(key_of[4], (2, S2), S2 ** -0.5, 0.375, (), jnp.float32),
        "electric_x": normal_values(key_of[5], (NX, NY), 1.0, 6.0, ((0, 8), (1, 16)), jnp.float32),
        "electric_y": normal_values(key_of[6], (NX, NY), 1.0, 6.0, ((0, 8), (1, 16)), jnp.float32),
        "magnetic_z": normal_values(key_of[7], (NX, NY), 1.0, 6.0, ((0, 8), (1, 16)), jnp.float32),
    }


COURANT = 0.5


def molecule_step(block, propagator, dipoles):
    states, sample_x, sample_y, alive = block
    product = jnp.dot(states, propagator, precision=lax.Precision.HIGHEST, preferred_element_type=jnp.float32)
    updated = product[:, :S2] + sample_x[:, None] * product[:, S2:2 * S2] + sample_y[:, None] * product[:, 2 * S2:]
    updated = jnp.where(alive[:, None], updated, states)
    emission = lax.dot_general(dipoles, updated - states, (((1,), (1,)), ((), ())), precision=lax.Precision.HIGHEST)
    return updated, emission


def reference(density, cell_index, live_batches, propagator, dipoles, electric_x, electric_y, magnetic_z):
    rows = jnp.arange(MOLS, dtype=jnp.int32)
    owner = rows // SLOTS
    row_block = owner // N_GY
    col_block = owner % N_GY
    cells = ((row_block * CX + cell_index // CY) * NY + col_block * CY + cell_index % CY).astype(jnp.int32)
    alive = ((rows % SLOTS) // BATCH) < live_batches[owner]
    for repeat in range(STEPS):
        sample_x = electric_x.reshape(-1)[cells]
        sample_y = electric_y.reshape(-1)[cells]
        updated, emission = lax.map(
            lambda block: molecule_step(block, propagator, dipoles),
            (density.reshape(DEVICES, SLOTS, S2), sample_x.reshape(DEVICES, SLOTS),
             sample_y.reshape(DEVICES, SLOTS), alive.reshape(DEVICES, SLOTS)))
        density = updated.reshape(MOLS, S2)
        current = jnp.transpose(emission, (1, 0, 2)).reshape(2, MOLS)
        source = jnp.zeros((2, NX * NY), jnp.float32).at[:, cells].add(current).reshape(2, NX, NY)
        magnetic_z = magnetic_z - COURANT * ((jnp.roll(electric_y, -1, 0) - electric_y) - (jnp.roll(electric_x, -1, 1) - electric_x))
        electric_x = electric_x + COURANT * (magnetic_z - jnp.roll(magnetic_z, 1, 1)) - source[0]
        electric_y = electric_y - COURANT * (magnetic_z - jnp.roll(magnetic_z, 1, 0)) - source[1]
    return density, electric_x, electric_y, magnetic_z
```

```python
import jax
import jax.numpy as jnp
from jax import lax
from jax.experimental import pallas as pl
from jax.experimental.pallas import tpu as pltpu
from jax.sharding import PartitionSpec as P

BATCH = 64
STEPS = 3
TILE = 256
COURANT = 0.5
CX = 128
CY = 256
S2 = 256
ROWS = 3 * S2 + 16
F32 = jnp.float32
BF16 = jnp.bfloat16


def halves(x):
    hi = x.astype(BF16)
    return hi, (x - hi.astype(F32)).astype(BF16)


def prepare(prop_ref, dip_ref, table_ref):
    for b in range(3):
        hi, lo = halves(prop_ref[:, b * S2 : (b + 1) * S2].T)
        rows = pl.ds(b * S2, S2)
        table_ref[rows, 0:S2] = hi
        table_ref[rows, S2 : 2 * S2] = hi
        table_ref[rows, 2 * S2 :] = lo
    dipoles = dip_ref[...]
    padded = jnp.concatenate([dipoles, jnp.zeros((6, S2), F32)], axis=0)
    reads = [
        lax.dot_general(
            padded,
            prop_ref[:, b * S2 : (b + 1) * S2],
            (((1,), (1,)), ((), ())),
            precision=lax.Precision.HIGHEST,
            preferred_element_type=F32,
        )[0:2]
        for b in range(3)
    ]
    stacked = jnp.concatenate(
        [reads[0] - dipoles, reads[1], reads[2], jnp.zeros((10, S2), F32)], axis=0
    )
    hi, lo = halves(stacked)
    rows = pl.ds(3 * S2, 16)
    table_ref[rows, 0:S2] = hi
    table_ref[rows, S2 : 2 * S2] = hi
    table_ref[rows, 2 * S2 :] = lo


def tile_step(t, cells_ref, fields, table, state, source_ref):
    cell = jnp.concatenate(
        [cells_ref[pl.ds(t * (TILE // 128) + j, 1), :] for j in range(TILE // 128)], axis=1
    )
    row = cell >> 8
    col = cell & (CY - 1)
    hot_col = jnp.where(lax.broadcasted_iota(jnp.int32, (CY, TILE), 0) == col, 1.0, 0.0).astype(BF16)
    mask = lax.broadcasted_iota(jnp.int32, (CX, TILE), 0) == row
    lines = jnp.dot(fields, hot_col, preferred_element_type=F32)
    sample_x = jnp.sum(
        jnp.where(mask, lines[0:CX] + lines[CX : 2 * CX], 0.0), axis=0, keepdims=True
    )
    sample_y = jnp.sum(
        jnp.where(mask, lines[2 * CX : 3 * CX] + lines[3 * CX :], 0.0), axis=0, keepdims=True
    )
    hi, lo = state
    product = jnp.dot(table, jnp.concatenate([hi, lo, hi], axis=0), preferred_element_type=F32)
    updated = (
        product[0:S2] + sample_x * product[S2 : 2 * S2] + sample_y * product[2 * S2 : 3 * S2]
    )
    reads = product[3 * S2 : 3 * S2 + 8]
    current_x = reads[0:1] + sample_x * reads[2:3] + sample_y * reads[4:5]
    current_y = reads[1:2] + sample_x * reads[3:4] + sample_y * reads[5:6]
    parts = []
    for current in (current_x, current_y):
        hi, lo = halves(current)
        for part in (hi, lo):
            parts.append(jnp.where(mask, part.astype(F32), 0.0).astype(BF16))
    source_ref[...] += lax.dot_general(
        jnp.concatenate(parts, axis=0), hot_col, (((1,), (1,)), ((), ())), preferred_element_type=F32
    )
    return updated


def split_fields(ex_ref, ey_ref):
    xh, xl = halves(ex_ref[...])
    yh, yl = halves(ey_ref[...])
    return jnp.concatenate([xh, xl, yh, yl], axis=0)


def first_kernel(
    live_ref, cells_ref, ex_ref, ey_ref, prop_ref, dip_ref, dens_ref,
    table_ref, state_ref, out_ref, buf, acc, fld, sems,
):
    count = live_ref[0] * BATCH // TILE

    def copy(t):
        rows = pl.ds(t * TILE, TILE)
        return pltpu.make_async_copy(dens_ref.at[rows, :], buf.at[rows, :], sems.at[t])

    def start(t, carry):
        copy(t).start()
        return carry

    lax.fori_loop(0, count, start, 0)
    prepare(prop_ref, dip_ref, table_ref)
    fld[...] = split_fields(ex_ref, ey_ref)
    acc[...] = jnp.zeros_like(acc)

    def step(t, carry):
        copy(t).wait()
        state = halves(buf[pl.ds(t * TILE, TILE), :].T)
        updated = tile_step(t, cells_ref, fld[...], table_ref[...], state, acc)
        hi, lo = halves(updated)
        cols = pl.ds(pl.multiple_of(t * TILE, TILE), TILE)
        state_ref[0:S2, cols] = hi
        state_ref[S2:, cols] = lo
        return carry

    lax.fori_loop(0, count, step, 0)
    finish(acc, out_ref)


def finish(acc, out_ref):
    out_ref[0:CX] = acc[0:CX] + acc[CX : 2 * CX]
    out_ref[CX:] = acc[2 * CX : 3 * CX] + acc[3 * CX :]


def load_state(old_ref, t):
    cols = pl.ds(pl.multiple_of(t * TILE, TILE), TILE)
    return old_ref[0:S2, cols], old_ref[S2:, cols]


def middle_kernel(live_ref, cells_ref, ex_ref, ey_ref, table_ref, old_ref, state_ref, out_ref, acc, fld):
    count = live_ref[0] * BATCH // TILE
    fld[...] = split_fields(ex_ref, ey_ref)
    acc[...] = jnp.zeros_like(acc)

    def step(t, carry):
        updated = tile_step(t, cells_ref, fld[...], table_ref[...], load_state(old_ref, t), acc)
        hi, lo = halves(updated)
        cols = pl.ds(pl.multiple_of(t * TILE, TILE), TILE)
        state_ref[0:S2, cols] = hi
        state_ref[S2:, cols] = lo
        return carry

    lax.fori_loop(0, count, step, 0)
    finish(acc, out_ref)


def last_kernel(
    live_ref, cells_ref, ex_ref, ey_ref, table_ref, old_ref, dens_ref,
    evolved_ref, out_ref, buf, acc, fld, sems,
):
    count = live_ref[0] * BATCH // TILE
    total = dens_ref.shape[0] // TILE

    def keep(t):
        rows = pl.ds(t * TILE, TILE)
        return pltpu.make_async_copy(dens_ref.at[rows, :], evolved_ref.at[rows, :], sems.at[t])

    def write(t):
        rows = pl.ds(t * TILE, TILE)
        return pltpu.make_async_copy(buf.at[rows, :], evolved_ref.at[rows, :], sems.at[t])

    def start_keep(t, carry):
        keep(t).start()
        return carry

    lax.fori_loop(count, total, start_keep, 0)
    fld[...] = split_fields(ex_ref, ey_ref)
    acc[...] = jnp.zeros_like(acc)

    def step(t, carry):
        updated = tile_step(t, cells_ref, fld[...], table_ref[...], load_state(old_ref, t), acc)
        buf[pl.ds(t * TILE, TILE), :] = updated.T
        write(t).start()
        return carry

    lax.fori_loop(0, count, step, 0)
    finish(acc, out_ref)

    def wait_write(t, carry):
        write(t).wait()
        return carry

    def wait_keep(t, carry):
        keep(t).wait()
        return carry

    lax.fori_loop(0, count, wait_write, 0)
    lax.fori_loop(count, total, wait_keep, 0)


def diagonal():
    shape = (CX, CX)
    return lax.broadcasted_iota(jnp.int32, shape, 0) == lax.broadcasted_iota(jnp.int32, shape, 1)


def to_row(column):
    return jnp.sum(jnp.where(diagonal(), column, 0.0), axis=0, keepdims=True)


def to_column(row):
    return jnp.sum(jnp.where(diagonal(), row, 0.0), axis=1, keepdims=True)


def emit_edges(ex, ey, mz, edge_refs):
    west, east, south, north, corner_a, corner_b = edge_refs
    west[...] = ey[0:8]
    pad = jnp.zeros((5, CY), F32)
    last = CX - 1
    east[...] = jnp.concatenate([mz[last:], ex[last:], ey[last:], pad], axis=0)
    wide = jnp.zeros((7, CX), F32)
    south[...] = jnp.concatenate([to_row(ex[:, 0:1]), wide], axis=0)
    end = CY - 1
    north[...] = jnp.concatenate(
        [to_row(mz[:, end:]), to_row(ex[:, end:]), to_row(ey[:, end:]), jnp.zeros((5, CX), F32)],
        axis=0,
    )
    corner_a[...] = ex[CX - 8 :, 0:128]
    corner_b[...] = ey[0:8, CY - 128 :]


def edges_kernel(ex_ref, ey_ref, mz_ref, *edge_refs):
    emit_edges(ex_ref[...], ey_ref[...], mz_ref[...], edge_refs)


def field_kernel(
    ex_ref, ey_ref, mz_ref, source_ref, own_south_ref,
    up_ref, down_ref, right_ref, left_ref, down_right_ref, up_left_ref,
    new_x_ref, new_y_ref, new_z_ref, *edge_refs,
):
    ex = ex_ref[...]
    ey = ey_ref[...]
    mz = mz_ref[...]
    shape = (CX, CY)
    line = lax.broadcasted_iota(jnp.int32, shape, 0)
    place = lax.broadcasted_iota(jnp.int32, shape, 1)
    ey_next = jnp.where(line == CX - 1, up_ref[0:1, :], pltpu.roll(ey, CX - 1, 0))
    ex_next = jnp.where(place == CY - 1, to_column(right_ref[0:1, :]), pltpu.roll(ex, CY - 1, 1))
    magnet = mz - COURANT * ((ey_next - ey) - (ex_next - ex))
    down = down_ref[...]
    across = down[1:2]
    lane = lax.broadcasted_iota(jnp.int32, (1, CY), 1)
    corner = down_right_ref[7:8, 0:1]
    across_next = jnp.where(lane == CY - 1, corner, pltpu.roll(across, CY - 1, 1))
    magnet_down = down[0:1] - COURANT * ((ey[0:1] - down[2:3]) - (across_next - across))
    left = left_ref[...]
    along = left[2:3]
    lane = lax.broadcasted_iota(jnp.int32, (1, CX), 1)
    corner = up_left_ref[0:1, 127:128]
    along_next = jnp.where(lane == CX - 1, corner, pltpu.roll(along, CX - 1, 1))
    magnet_left = left[0:1] - COURANT * ((along_next - along) - (own_south_ref[0:1] - left[1:2]))
    before_y = jnp.where(place == 0, to_column(magnet_left), pltpu.roll(magnet, 1, 1))
    before_x = jnp.where(line == 0, magnet_down, pltpu.roll(magnet, 1, 0))
    new_x = ex + COURANT * (magnet - before_y) - source_ref[0:CX]
    new_y = ey - COURANT * (magnet - before_x) - source_ref[CX:]
    new_x_ref[...] = new_x
    new_y_ref[...] = new_y
    new_z_ref[...] = magnet
    if edge_refs:
        emit_edges(new_x, new_y, magnet, edge_refs)


VMEM = pl.BlockSpec(memory_space=pltpu.VMEM)
SMEM = pl.BlockSpec(memory_space=pltpu.SMEM)
ANY = pl.BlockSpec(memory_space=pl.ANY)


def shaped(shape, dtype=F32):
    return jax.ShapeDtypeStruct(shape, dtype)


EDGES = tuple(shaped((8, n)) for n in (CY, CY, CX, CX, 128, 128))
FIELDS = tuple(shaped((CX, CY)) for _ in range(3))


def exchange(edges):
    gx = lax.axis_size("gx")
    gy = lax.axis_size("gy")

    def send(value, dx, dy):
        pairs = []
        for a in range(gx):
            for b in range(gy):
                pairs.append((a * gy + b, (a + dx) % gx * gy + (b + dy) % gy))
        return lax.ppermute(value, ("gx", "gy"), pairs)

    west, east, south, north, corner_a, corner_b = edges
    return (
        send(west, -1, 0),
        send(east, 1, 0),
        send(south, 0, -1),
        send(north, 0, 1),
        send(corner_a, 1, -1),
        send(corner_b, -1, 1),
    )


def shards(density, cell_index, live_batches, propagator, dipoles, ex, ey, mz):
    slots = density.shape[0]
    tiles = slots // TILE
    cells = cell_index.reshape(slots // 128, 128)
    edges = pl.pallas_call(
        edges_kernel, out_shape=EDGES, in_specs=[VMEM] * 3, out_specs=(VMEM,) * 6, name="edges"
    )(ex, ey, mz)
    work = [pltpu.VMEM((4 * CX, CY), F32), pltpu.VMEM((4 * CX, CY), BF16)]
    buffer = pltpu.VMEM((slots, S2), F32)
    sems = pltpu.SemaphoreType.DMA((tiles,))
    table_shape = shaped((ROWS, 3 * S2), BF16)
    state_shape = shaped((2 * S2, slots), BF16)
    source_shape = shaped((2 * CX, CY))
    for step in range(STEPS):
        halo = exchange(edges)
        if step == 0:
            table, state, source = pl.pallas_call(
                first_kernel,
                out_shape=(table_shape, state_shape, source_shape),
                in_specs=[SMEM, VMEM, VMEM, VMEM, VMEM, VMEM, ANY],
                out_specs=(VMEM,) * 3,
                scratch_shapes=[buffer, *work, sems],
                name="first",
            )(live_batches, cells, ex, ey, propagator, dipoles, density)
        elif step < STEPS - 1:
            state, source = pl.pallas_call(
                middle_kernel,
                out_shape=(state_shape, source_shape),
                in_specs=[SMEM, VMEM, VMEM, VMEM, VMEM, VMEM],
                out_specs=(VMEM,) * 2,
                scratch_shapes=work,
                name="middle",
            )(live_batches, cells, ex, ey, table, state)
        else:
            evolved, source = pl.pallas_call(
                last_kernel,
                out_shape=(shaped((slots, S2)), source_shape),
                in_specs=[SMEM, VMEM, VMEM, VMEM, VMEM, VMEM, ANY],
                out_specs=(ANY, VMEM),
                scratch_shapes=[buffer, *work, sems],
                name="last",
            )(live_batches, cells, ex, ey, table, state, density)
        shapes = FIELDS + (EDGES if step < STEPS - 1 else ())
        ex, ey, mz, *edges = pl.pallas_call(
            field_kernel,
            out_shape=shapes,
            in_specs=[VMEM] * 11,
            out_specs=(VMEM,) * len(shapes),
            name="fields",
        )(ex, ey, mz, source, edges[2], *halo)
    return evolved, ex, ey, mz


def solution(mesh):
    placed = (
        P(("gx", "gy"), None),
        P(("gx", "gy")),
        P(("gx", "gy")),
        P(),
        P(),
        P("gx", "gy"),
        P("gx", "gy"),
        P("gx", "gy"),
    )
    return jax.shard_map(
        shards,
        mesh=mesh,
        in_specs=placed,
        out_specs=(P(("gx", "gy"), None), P("gx", "gy"), P("gx", "gy"), P("gx", "gy")),
        check_vma=False,
    )
```

```python
import jax
import jax.numpy as jnp
from jax import lax
from jax.experimental import pallas as pl
from jax.experimental.pallas import tpu as pltpu
from jax.sharding import PartitionSpec as P

BATCH = 64
STEPS = 3
TILE = 256
COURANT = 0.5
CX = 128
CY = 256
S2 = 256
ROWS = 3 * S2 + 16
FIRST = 6
ORDERS = 24
LINES = 56
TALL = CX + 16
WIDE = CY + 256
F32 = jnp.float32
BF16 = jnp.bfloat16
NT = (((1,), (1,)), ((), ()))


def halves(x):
    hi = x.astype(BF16)
    return hi, (x - hi.astype(F32)).astype(BF16)


def exact_nt(a, b):
    return lax.dot_general(
        a, b, NT, precision=lax.Precision.HIGHEST, preferred_element_type=F32
    )


def fast_nt(a, b):
    return lax.dot_general(a, b, NT, preferred_element_type=F32)


def prepare(prop_ref, dip_ref, table_ref):
    def put(rows, value):
        hi, lo = halves(value)
        table_ref[rows, 0:S2] = hi
        table_ref[rows, S2 : 2 * S2] = hi
        table_ref[rows, 2 * S2 :] = lo

    blocks = [prop_ref[:, b * S2 : (b + 1) * S2] for b in range(3)]
    for b in range(3):
        put(pl.ds(b * S2, S2), blocks[b].T)
    dipoles = dip_ref[...]
    padded = jnp.concatenate([dipoles, jnp.zeros((6, S2), F32)], axis=0)
    reads = [exact_nt(padded, block)[0:2] for block in blocks]
    first = jnp.concatenate(
        [reads[0] - dipoles, reads[1], reads[2], jnp.zeros((2, S2), F32)], axis=0
    )
    put(pl.ds(3 * S2, 16), jnp.concatenate([first, jnp.zeros((8, S2), F32)], axis=0))
    second = [exact_nt(first, block)[0:FIRST] for block in blocks]
    return jnp.concatenate([first[0:FIRST], *second, jnp.zeros((8, S2), F32)], axis=0)


def cells_of(cells_ref, t):
    cell = jnp.concatenate(
        [cells_ref[pl.ds(t * (TILE // 128) + j, 1), :] for j in range(TILE // 128)], axis=1
    )
    return cell >> 8, cell & (CY - 1)


def matches(index, size):
    return lax.broadcasted_iota(jnp.int32, (size, TILE), 0) == index


def one_hot(index, size):
    return jnp.where(matches(index, size), 1.0, 0.0).astype(BF16)


def count_of(live_ref):
    return live_ref[0] * BATCH // TILE


def tile_rows(t):
    return pl.ds(pl.multiple_of(t * TILE, TILE), TILE)


def sweep(lower, upper, body):
    def wrapped(t, carry):
        body(t)
        return carry

    lax.fori_loop(lower, upper, wrapped, 0)


def coefficient_kernel(
    live_ref, cells_ref, ex_ref, ey_ref, mz_ref, prop_ref, dip_ref, dens_ref,
    table_ref, low_ref, high_ref, west_ref, east_ref, buf, by_row, by_col, sems,
):
    count = count_of(live_ref)

    def copy(t):
        return pltpu.make_async_copy(dens_ref.at[tile_rows(t), :], buf.at[tile_rows(t), :], sems.at[t])

    sweep(0, count, lambda t: copy(t).start())
    functionals = prepare(prop_ref, dip_ref, table_ref)
    fh, fl = halves(functionals)
    stacked = jnp.concatenate([fh, fl], axis=0)
    by_row[...] = jnp.zeros_like(by_row)
    by_col[...] = jnp.zeros_like(by_col)

    def picked(index, near, far, parts):
        out = []
        for place, rows in ((near[0], ORDERS), (near[1], ORDERS), (far[0], 8), (far[1], 8)):
            for part in parts:
                out.append(jnp.where(index == place, part[0:rows], 0.0))
        return jnp.concatenate(out, axis=0).astype(BF16)

    def body(t):
        copy(t).wait()
        dh, dl = halves(buf[tile_rows(t), :])
        wide = fast_nt(stacked, dh)
        values = wide[0:32] + wide[32:64] + fast_nt(fh, dl)
        vh, vl = halves(values)
        parts = (vh.astype(F32), vl.astype(F32))
        row, col = cells_of(cells_ref, t)
        by_row[...] += fast_nt(picked(row, (0, CX - 1), (1, CX - 2), parts), one_hot(col, CY))
        by_col[...] += fast_nt(picked(col, (0, CY - 1), (1, CY - 2), parts), one_hot(row, CX))

    sweep(0, count, body)

    def side(ref, which):
        near = 2 * ORDERS * which
        far = 4 * ORDERS + 16 * which
        return (
            ref[near : near + ORDERS] + ref[near + ORDERS : near + 2 * ORDERS],
            ref[far : far + 8] + ref[far + 8 : far + 16],
        )

    for which, ref, rows in ((0, low_ref, slice(0, 8)), (1, high_ref, slice(CX - 8, CX))):
        near, far = side(by_row, which)
        ref[0:8] = mz_ref[rows, :]
        ref[8:16] = ex_ref[rows, :]
        ref[16:24] = ey_ref[rows, :]
        ref[24:48] = near
        ref[48:56] = far
    for which, ref in ((0, west_ref), (1, east_ref)):
        near, far = side(by_col, which)
        ref[0:ORDERS] = near
        ref[ORDERS:] = far


def tile_step(t, cells_ref, fields, table, state, source_ref):
    row, col = cells_of(cells_ref, t)
    hot_col = one_hot(col, CY)
    mask = matches(row, CX)
    lines = jnp.dot(fields, hot_col, preferred_element_type=F32)
    sample_x = jnp.sum(
        jnp.where(mask, lines[0:CX] + lines[CX : 2 * CX], 0.0), axis=0, keepdims=True
    )
    sample_y = jnp.sum(
        jnp.where(mask, lines[2 * CX : 3 * CX] + lines[3 * CX :], 0.0), axis=0, keepdims=True
    )
    hi, lo = state
    product = jnp.dot(table, jnp.concatenate([hi, lo, hi], axis=0), preferred_element_type=F32)
    updated = (
        product[0:S2] + sample_x * product[S2 : 2 * S2] + sample_y * product[2 * S2 : 3 * S2]
    )
    reads = product[3 * S2 : 3 * S2 + 8]
    current_x = reads[0:1] + sample_x * reads[2:3] + sample_y * reads[4:5]
    current_y = reads[1:2] + sample_x * reads[3:4] + sample_y * reads[5:6]
    parts = []
    for current in (current_x, current_y):
        for part in halves(current):
            parts.append(jnp.where(mask, part.astype(F32), 0.0).astype(BF16))
    source_ref[...] += fast_nt(jnp.concatenate(parts, axis=0), hot_col)
    return updated


def split_fields(ex, ey):
    xh, xl = halves(ex)
    yh, yl = halves(ey)
    return jnp.concatenate([xh, xl, yh, yl], axis=0)


def save_state(state_ref, t, updated):
    hi, lo = halves(updated)
    state_ref[0:S2, tile_rows(t)] = hi
    state_ref[S2:, tile_rows(t)] = lo


def load_state(state_ref, t):
    return state_ref[0:S2, tile_rows(t)], state_ref[S2:, tile_rows(t)]


def first_kernel(
    live_ref, cells_ref, ex_ref, ey_ref, table_ref, dens_ref,
    state_ref, acc, buf, fld, sems,
):
    count = count_of(live_ref)

    def copy(t):
        return pltpu.make_async_copy(dens_ref.at[tile_rows(t), :], buf.at[tile_rows(t), :], sems.at[t])

    sweep(0, count, lambda t: copy(t).start())
    fld[...] = split_fields(ex_ref[...], ey_ref[...])
    acc[...] = jnp.zeros_like(acc)

    def body(t):
        copy(t).wait()
        state = halves(buf[tile_rows(t), :].T)
        updated = tile_step(t, cells_ref, fld[...], table_ref[...], state, acc)
        save_state(state_ref, t, updated)

    sweep(0, count, body)


def corner_kernel(
    ex_ref, ey_ref, mz_ref, west_ref, east_ref, top_ref, bottom_ref, left_ref, right_ref
):
    tops = top_ref[...]
    bottoms = bottom_ref[...]
    lane = lax.broadcasted_iota(jnp.int32, (TALL, 128), 1)
    for side, ref, coefs_ref in ((0, left_ref, west_ref), (1, right_ref, east_ref)):
        half = slice(128 * side, 128 * side + 128)

        def tall(k, field_ref):
            rows = slice(8 * k, 8 * k + 8)
            return jnp.concatenate([tops[rows, half], field_ref[:, half], bottoms[rows, half]], axis=0)

        shift = 8 * side
        m = tall(0, mz_ref)
        if shift:
            m = pltpu.roll(m, shift, 1)
        x = pltpu.roll(tall(1, ex_ref), 8 + shift, 1)
        y = pltpu.roll(tall(2, ey_ref), 16 + shift, 1)
        ref[0:TALL] = jnp.where(lane < 8, m, jnp.where(lane < 16, x, y))
        coefs = coefs_ref[...]
        wide = pltpu.roll(jnp.concatenate([coefs, jnp.zeros_like(coefs)], axis=1), 8, 1)
        lower = wide[:, 0:128]
        upper = wide[:, 128:256]
        place = lax.broadcasted_iota(jnp.int32, (32, 128), 1)
        gap = jnp.zeros((16, 128), F32)

        def both(lines, near_from, far_from, near_to, far_to, base):
            near = lines[24:48, half]
            far = lines[48:56, half]
            at_near = jnp.concatenate(
                [
                    pltpu.roll(near, (near_to - near_from) % 128, 1),
                    pltpu.roll(near[0:8], (near_to - far_from) % 128, 1),
                ],
                axis=0,
            )
            at_far = jnp.concatenate(
                [
                    pltpu.roll(far, (far_to - near_from) % 128, 1),
                    gap,
                    pltpu.roll(far, (far_to - far_from) % 128, 1),
                ],
                axis=0,
            )
            return jnp.where(place == near_to, at_near, jnp.where(place == far_to, at_far, base))

        near_from, far_from = (127, 126) if side else (0, 1)
        ref[TALL : TALL + 32] = both(tops, near_from, far_from, 7, 6, lower)
        ref[TALL + 32 :] = both(bottoms, near_from, far_from, 8, 9, upper)


def linear(coefs, x, y):
    return (
        coefs[0:1] + x * coefs[2:3] + y * coefs[4:5],
        coefs[1:2] + x * coefs[3:4] + y * coefs[5:6],
    )


def quadratic(coefs, x0, y0, x1, y1):
    terms = [linear(coefs[FIRST * (c + 1) : FIRST * (c + 2)], x1, y1) for c in range(3)]
    return tuple(terms[0][k] + x0 * terms[1][k] + y0 * terms[2][k] for k in range(2))


def turned(value):
    rows, lanes = value.shape
    if rows < 128:
        value = jnp.concatenate([value, jnp.zeros((128 - rows, lanes), F32)], axis=0)
    elif rows < 256:
        value = jnp.concatenate([value, jnp.zeros((256 - rows, lanes), F32)], axis=0)
    return value.T


def advance(x, y, z, source_x, source_y):
    y_next = pltpu.roll(y, TALL - 1, 0)
    x_next = pltpu.roll(x, WIDE - 1, 1)
    z = z - COURANT * ((y_next - y) - (x_next - x))
    x = x + COURANT * (z - pltpu.roll(z, 1, 1)) - source_x
    y = y - COURANT * (z - pltpu.roll(z, 1, 0)) - source_y
    return x, y, z


OWN = slice(128, 128 + CY)


def main_kernel(
    live_ref, cells_ref, ex_ref, ey_ref, mz_ref, acc_ref, table_ref, old_ref,
    top_ref, bottom_ref, left_ref, right_ref, dens_ref,
    evolved_ref, out_x, out_y, out_z, state, buf, acc, fld, xs, ys, zs, sems,
):
    count = count_of(live_ref)
    total = dens_ref.shape[0] // TILE

    def fetch(t):
        return pltpu.make_async_copy(dens_ref.at[tile_rows(t), :], buf.at[tile_rows(t), :], sems.at[t])

    def write(t):
        return pltpu.make_async_copy(buf.at[tile_rows(t), :], evolved_ref.at[tile_rows(t), :], sems.at[t])

    sweep(count, total, lambda t: fetch(t).start())

    left = left_ref[...]
    right = right_ref[...]

    def extended(k, field_ref):
        rows = slice(8 * k, 8 * k + 8)
        middle = jnp.concatenate([top_ref[rows, :], field_ref[...], bottom_ref[rows, :]], axis=0)
        before = pltpu.roll(left[0:TALL], 120 - 8 * k, 1)
        after = right[0:TALL]
        if k:
            after = pltpu.roll(after, 128 - 8 * k, 1)
        return jnp.concatenate([before, middle, after], axis=1)

    zs[...] = extended(0, mz_ref)
    xs[...] = extended(1, ex_ref)
    ys[...] = extended(2, ey_ref)

    sides = []
    for package, near, far in ((left, 7, 6), (right, 0, 1)):
        lines = turned(package[0:TALL])
        coefs = jnp.concatenate([package[TALL : TALL + 32], package[TALL + 32 :]], axis=1)
        near_x, near_y = lines[8 + near : 9 + near], lines[16 + near : 17 + near]
        far_x, far_y = lines[8 + far : 9 + far], lines[16 + far : 17 + far]
        sides.append(
            (
                coefs,
                near_x,
                near_y,
                linear(coefs[0:FIRST], near_x, near_y),
                linear(coefs[ORDERS : ORDERS + FIRST], far_x, far_y),
            )
        )
    lane = lax.broadcasted_iota(jnp.int32, (TALL, 128), 1)
    line = lax.broadcasted_iota(jnp.int32, (8, CY), 0)

    def assembled(tops, rows, bottoms, before, after):
        middle = jnp.concatenate([tops, rows, bottoms], axis=0)
        return jnp.concatenate([before, middle, after], axis=1)

    (lc, lx0, ly0, lnear, lfar), (rc, rx0, ry0, rnear, rfar) = sides
    columns = turned(
        jnp.concatenate(
            [lfar[0], lnear[0], lfar[1], lnear[1], rnear[0], rfar[0], rnear[1], rfar[1]], axis=0
        )
    )[0:TALL]
    zero_line = jnp.zeros((8, CY), F32)
    starts = []
    top_lines = []
    bottom_lines = []
    for lines_ref, near, far, out in (
        (top_ref, 7, 6, top_lines),
        (bottom_ref, 0, 1, bottom_lines),
    ):
        near_x, near_y = lines_ref[8 + near : 9 + near, :], lines_ref[16 + near : 17 + near, :]
        far_x, far_y = lines_ref[8 + far : 9 + far, :], lines_ref[16 + far : 17 + far, :]
        starts.append((near_x, near_y))
        at_near = linear(lines_ref[24 : 24 + FIRST, :], near_x, near_y)
        at_far = linear(lines_ref[48 : 48 + FIRST, :], far_x, far_y)
        for k in range(2):
            out.append(
                jnp.where(line == near, at_near[k], jnp.where(line == far, at_far[k], zero_line))
            )

    def own(ref, k):
        return ref[2 * k * CX : (2 * k + 1) * CX] + ref[(2 * k + 1) * CX : (2 * k + 2) * CX]

    sources = []
    for k in range(2):
        before = jnp.where(lane >= 126, pltpu.roll(columns, 126 - 2 * k, 1), 0.0)
        after = jnp.where(lane < 2, pltpu.roll(columns, 124 - 2 * k, 1), 0.0)
        sources.append(assembled(top_lines[k], own(acc_ref, k), bottom_lines[k], before, after))
    x, y, z = advance(xs[...], ys[...], zs[...], *sources)
    xs[...] = x
    ys[...] = y
    zs[...] = z

    def flush(t):
        fetch(t).wait()
        write(t).start()

    sweep(count, total, flush)

    def prime():
        fld[...] = split_fields(xs[8 : 8 + CX, OWN], ys[8 : 8 + CX, OWN])
        acc[...] = jnp.zeros_like(acc)

    prime()

    def second(t):
        updated = tile_step(t, cells_ref, fld[...], table_ref[...], load_state(old_ref, t), acc)
        save_state(state, t, updated)

    sweep(0, count, second)

    x = xs[...]
    y = ys[...]
    xl, yl = x[:, 0:128], y[:, 0:128]
    xr, yr = x[:, 384:512], y[:, 384:512]
    edge = jnp.where(
        lane == 127,
        xl,
        jnp.where(
            lane == 126,
            pltpu.roll(yl, 127, 1),
            jnp.where(lane == 0, xr, jnp.where(lane == 1, pltpu.roll(yr, 1, 1), 0.0)),
        ),
    )
    rows = turned(edge)
    ends_l = quadratic(lc, lx0, ly0, rows[127:128], rows[126:127])
    ends_r = quadratic(rc, rx0, ry0, rows[0:1], rows[1:2])
    columns = turned(
        jnp.concatenate([ends_l[0], ends_l[1], ends_r[0], ends_r[1], jnp.zeros((4, CY), F32)], axis=0)
    )[0:TALL]
    lines = []
    for (x0, y0), lines_ref, near, at in (
        (starts[0], top_ref, 7, 7),
        (starts[1], bottom_ref, 0, 8 + CX),
    ):
        ends = quadratic(
            lines_ref[24:48, :], x0, y0, x[at : at + 1, OWN], y[at : at + 1, OWN]
        )
        lines.append([jnp.where(line == near, ends[k], zero_line) for k in range(2)])
    sources = []
    for k in range(2):
        before = jnp.where(lane == 127, pltpu.roll(columns, 127 - k, 1), 0.0)
        after = jnp.where(lane == 0, pltpu.roll(columns, 126 - k, 1), 0.0)
        sources.append(assembled(lines[0][k], own(acc, k), lines[1][k], before, after))
    x, y, z = advance(x, y, zs[...], *sources)
    xs[...] = x
    ys[...] = y
    zs[...] = z
    prime()

    def third(t):
        updated = tile_step(t, cells_ref, fld[...], table_ref[...], load_state(state, t), acc)
        buf[tile_rows(t), :] = updated.T
        write(t).start()

    sweep(0, count, third)
    blank = jnp.zeros((TALL, 128), F32)
    sources = [assembled(zero_line, own(acc, k), zero_line, blank, blank) for k in range(2)]
    x, y, z = advance(xs[...], ys[...], zs[...], *sources)
    out_x[...] = x[8 : 8 + CX, OWN]
    out_y[...] = y[8 : 8 + CX, OWN]
    out_z[...] = z[8 : 8 + CX, OWN]
    sweep(0, total, lambda t: write(t).wait())


VMEM = pl.BlockSpec(memory_space=pltpu.VMEM)
SMEM = pl.BlockSpec(memory_space=pltpu.SMEM)
ANY = pl.BlockSpec(memory_space=pl.ANY)


def shaped(shape, dtype=F32):
    return jax.ShapeDtypeStruct(shape, dtype)


def ring(axis, step):
    count = lax.axis_size(axis)
    return [(i, (i + step) % count) for i in range(count)]


def shards(density, cell_index, live_batches, propagator, dipoles, ex, ey, mz):
    slots = density.shape[0]
    tiles = slots // TILE
    cells = cell_index.reshape(slots // 128, 128)
    buffer = pltpu.VMEM((slots, S2), F32)
    sems = pltpu.SemaphoreType.DMA((tiles,))
    sums = (4 * CX, CY)
    halved = pltpu.VMEM((4 * CX, CY), BF16)
    table, low, high, west, east = pl.pallas_call(
        coefficient_kernel,
        out_shape=(
            shaped((ROWS, 3 * S2), BF16),
            shaped((LINES, CY)),
            shaped((LINES, CY)),
            shaped((32, CX)),
            shaped((32, CX)),
        ),
        in_specs=[SMEM] + [VMEM] * 6 + [ANY],
        out_specs=(VMEM,) * 5,
        scratch_shapes=[buffer, pltpu.VMEM((128, CY), F32), pltpu.VMEM((128, CX), F32), sems],
        name="coefficients",
    )(live_batches, cells, ex, ey, mz, propagator, dipoles, density)
    bottom = lax.ppermute(low, "gx", ring("gx", -1))
    top = lax.ppermute(high, "gx", ring("gx", 1))
    state, source = pl.pallas_call(
        first_kernel,
        out_shape=(shaped((2 * S2, slots), BF16), shaped(sums)),
        in_specs=[SMEM] + [VMEM] * 4 + [ANY],
        out_specs=(VMEM,) * 2,
        scratch_shapes=[buffer, halved, sems],
        name="first",
    )(live_batches, cells, ex, ey, table, density)
    package = shaped((TALL + 64, 128))
    to_left, to_right = pl.pallas_call(
        corner_kernel,
        out_shape=(package, package),
        in_specs=[VMEM] * 7,
        out_specs=(VMEM,) * 2,
        name="corners",
    )(ex, ey, mz, west, east, top, bottom)
    right = lax.ppermute(to_left, "gy", ring("gy", -1))
    left = lax.ppermute(to_right, "gy", ring("gy", 1))
    field = shaped((CX, CY))
    tall = pltpu.VMEM((TALL, WIDE), F32)
    return pl.pallas_call(
        main_kernel,
        out_shape=(shaped((slots, S2)), field, field, field),
        in_specs=[SMEM] + [VMEM] * 11 + [ANY],
        out_specs=(ANY,) + (VMEM,) * 3,
        scratch_shapes=[
            pltpu.VMEM((2 * S2, slots), BF16), buffer, pltpu.VMEM(sums, F32), halved,
            tall, tall, tall, sems,
        ],
        name="main",
    )(live_batches, cells, ex, ey, mz, source, table, state, top, bottom, left, right, density)


def solution(mesh):
    placed = (
        P(("gx", "gy"), None),
        P(("gx", "gy")),
        P(("gx", "gy")),
        P(),
        P(),
        P("gx", "gy"),
        P("gx", "gy"),
        P("gx", "gy"),
    )
    return jax.shard_map(
        shards,
        mesh=mesh,
        in_specs=placed,
        out_specs=(P(("gx", "gy"), None), P("gx", "gy"), P("gx", "gy"), P("gx", "gy")),
        check_vma=False,
    )
```

```python
import jax
import jax.numpy as jnp
from jax import lax
from jax.experimental import pallas as pl
from jax.experimental.pallas import tpu as pltpu
from jax.sharding import PartitionSpec as P

BATCH = 64
STEPS = 3
TILE = 1024
COURANT = 0.5
CX = 128
CY = 256
S2 = 256
ROWS = 3 * S2 + 16
FIRST = 6
ORDERS = 24
LINES = 56
TALL = CX + 16
WIDE = CY + 256
F32 = jnp.float32
BF16 = jnp.bfloat16
NT = (((1,), (1,)), ((), ()))


def halves(x):
    hi = x.astype(BF16)
    return hi, (x - hi.astype(F32)).astype(BF16)


def exact_nt(a, b):
    return lax.dot_general(
        a, b, NT, precision=lax.Precision.HIGHEST, preferred_element_type=F32
    )


def fast_nt(a, b):
    return lax.dot_general(a, b, NT, preferred_element_type=F32)


def functionals_of(prop_ref, dip_ref):
    blocks = [prop_ref[:, b * S2 : (b + 1) * S2] for b in range(3)]
    dipoles = dip_ref[...]
    padded = jnp.concatenate([dipoles, jnp.zeros((6, S2), F32)], axis=0)
    reads = [exact_nt(padded, block)[0:2] for block in blocks]
    first = jnp.concatenate(
        [reads[0] - dipoles, reads[1], reads[2], jnp.zeros((2, S2), F32)], axis=0
    )
    second = [exact_nt(first, block)[0:FIRST] for block in blocks]
    return jnp.concatenate([first[0:FIRST], *second, jnp.zeros((8, S2), F32)], axis=0)


def table_kernel(prop_ref, readout_ref, table_ref):
    def put(rows, value):
        hi, lo = halves(value)
        table_ref[rows, 0:S2] = hi
        table_ref[rows, S2 : 2 * S2] = hi
        table_ref[rows, 2 * S2 :] = lo

    for b in range(3):
        put(pl.ds(b * S2, S2), prop_ref[:, b * S2 : (b + 1) * S2].T)
    put(pl.ds(3 * S2, 16), jnp.concatenate([readout_ref[...], jnp.zeros((8, S2), F32)], axis=0))


def cells_of(cells_ref, t):
    cell = jnp.concatenate(
        [cells_ref[pl.ds(t * (TILE // 128) + j, 1), :] for j in range(TILE // 128)], axis=1
    )
    return cell >> 8, cell & (CY - 1)


def matches(index, size):
    return lax.broadcasted_iota(jnp.int32, (size, TILE), 0) == index


def one_hot(index, size):
    return jnp.where(matches(index, size), 1.0, 0.0).astype(BF16)


def count_of(live_ref):
    return live_ref[0] * BATCH // TILE


def tile_rows(t):
    return pl.ds(pl.multiple_of(t * TILE, TILE), TILE)


def sweep(lower, upper, body):
    def wrapped(t, carry):
        body(t)
        return carry

    lax.fori_loop(lower, upper, wrapped, 0)


def coefficient_kernel(
    live_ref, cells_hbm, ex_hbm, ey_hbm, mz_hbm, prop_hbm, dip_hbm, dens_hbm,
    readout_ref, low_ref, high_ref, west_ref, east_ref, hi_ref, lo_ref,
    buf, by_row, by_col, prop_ref, dip_ref, cells_ref, sems, loads,
):
    count = count_of(live_ref)

    def copy(t):
        return pltpu.make_async_copy(dens_hbm.at[tile_rows(t), :], buf.at[tile_rows(t), :], sems.at[t])

    pairs = [(dip_hbm, dip_ref), (prop_hbm, prop_ref), (cells_hbm, cells_ref)]
    for ref, start in ((low_ref, 0), (high_ref, CX - 8)):
        for k, field in enumerate((mz_hbm, ex_hbm, ey_hbm)):
            pairs.append((field.at[pl.ds(start, 8), :], ref.at[pl.ds(8 * k, 8), :]))
    moves = [pltpu.make_async_copy(src, dst, loads.at[k]) for k, (src, dst) in enumerate(pairs)]
    for move in moves[:3]:
        move.start()
    sweep(0, count, lambda t: copy(t).start())
    for move in moves[3:]:
        move.start()
    for move in moves[:2]:
        move.wait()
    functionals = functionals_of(prop_ref, dip_ref)
    readout_ref[...] = functionals[0:8]
    fh, fl = halves(functionals)
    stacked = jnp.concatenate([fh, fl], axis=0)
    by_row[...] = jnp.zeros_like(by_row)
    by_col[...] = jnp.zeros_like(by_col)

    def picked(index, near, far, parts):
        out = []
        for place, rows in ((near[0], ORDERS), (near[1], ORDERS), (far[0], 8), (far[1], 8)):
            for part in parts:
                out.append(jnp.where(index == place, part[0:rows], 0.0))
        return jnp.concatenate(out, axis=0).astype(BF16)

    def body(t):
        copy(t).wait()
        dh, dl = halves(buf[tile_rows(t), :])
        hi_ref[tile_rows(t), :] = dh
        lo_ref[tile_rows(t), :] = dl
        wide = fast_nt(stacked, dh)
        values = wide[0:32] + wide[32:64] + fast_nt(fh, dl)
        vh, vl = halves(values)
        parts = (vh.astype(F32), vl.astype(F32))
        row, col = cells_of(cells_ref, t)
        by_row[...] += fast_nt(picked(row, (0, CX - 1), (1, CX - 2), parts), one_hot(col, CY))
        by_col[...] += fast_nt(picked(col, (0, CY - 1), (1, CY - 2), parts), one_hot(row, CX))

    for move in moves[2:]:
        move.wait()
    sweep(0, count, body)

    def side(ref, which):
        near = 2 * ORDERS * which
        far = 4 * ORDERS + 16 * which
        return (
            ref[near : near + ORDERS] + ref[near + ORDERS : near + 2 * ORDERS],
            ref[far : far + 8] + ref[far + 8 : far + 16],
        )

    for which, ref in ((0, low_ref), (1, high_ref)):
        near, far = side(by_row, which)
        ref[24:48] = near
        ref[48:56] = far
    for which, ref in ((0, west_ref), (1, east_ref)):
        near, far = side(by_col, which)
        ref[0:ORDERS] = near
        ref[ORDERS:] = far


def tile_step(t, cells_ref, fields, table, state, source_ref):
    row, col = cells_of(cells_ref, t)
    hot_col = one_hot(col, CY)
    mask = matches(row, CX)
    lines = jnp.dot(fields, hot_col, preferred_element_type=F32)
    sample_x = jnp.sum(
        jnp.where(mask, lines[0:CX] + lines[CX : 2 * CX], 0.0), axis=0, keepdims=True
    )
    sample_y = jnp.sum(
        jnp.where(mask, lines[2 * CX : 3 * CX] + lines[3 * CX :], 0.0), axis=0, keepdims=True
    )
    product = state(table)
    updated = (
        product[0:S2] + sample_x * product[S2 : 2 * S2] + sample_y * product[2 * S2 : 3 * S2]
    )
    reads = product[3 * S2 : 3 * S2 + 8]
    current_x = reads[0:1] + sample_x * reads[2:3] + sample_y * reads[4:5]
    current_y = reads[1:2] + sample_x * reads[3:4] + sample_y * reads[5:6]
    parts = []
    for current in (current_x, current_y):
        for part in halves(current):
            parts.append(jnp.where(mask, part.astype(F32), 0.0).astype(BF16))
    source_ref[...] += fast_nt(jnp.concatenate(parts, axis=0), hot_col)
    return updated


def split_fields(ex, ey):
    xh, xl = halves(ex)
    yh, yl = halves(ey)
    return jnp.concatenate([xh, xl, yh, yl], axis=0)


def save_state(state_ref, t, updated):
    hi, lo = halves(updated)
    state_ref[0:S2, tile_rows(t)] = hi
    state_ref[S2:, tile_rows(t)] = lo


def stored(state_ref, t):
    def product(table):
        hi, lo = state_ref[0:S2, tile_rows(t)], state_ref[S2:, tile_rows(t)]
        return jnp.dot(table, jnp.concatenate([hi, lo, hi], axis=0), preferred_element_type=F32)

    return product


def first_kernel(
    live_ref, cells_ref, ex_ref, ey_ref, table_ref, hi_ref, lo_ref, state_ref, acc, fld
):
    fld[...] = split_fields(ex_ref[...], ey_ref[...])
    acc[...] = jnp.zeros_like(acc)

    def body(t):
        def product(table):
            hi, lo = hi_ref[tile_rows(t), :], lo_ref[tile_rows(t), :]
            return fast_nt(table, jnp.concatenate([hi, lo, hi], axis=1))

        updated = tile_step(t, cells_ref, fld[...], table_ref[...], product, acc)
        save_state(state_ref, t, updated)

    sweep(0, count_of(live_ref), body)


def corner_kernel(
    ex_ref, ey_ref, mz_ref, west_ref, east_ref, top_ref, bottom_ref, after_ref, left_ref, right_ref
):
    tops = top_ref[...]
    bottoms = bottom_ref[...]
    lane = lax.broadcasted_iota(jnp.int32, (TALL, 128), 1)
    for side, ref, coefs_ref in ((0, left_ref, west_ref), (1, right_ref, east_ref)):
        half = slice(128 * side, 128 * side + 128)

        def tall(k, field_ref):
            rows = slice(8 * k, 8 * k + 8)
            return jnp.concatenate([tops[rows, half], field_ref[:, half], bottoms[rows, half]], axis=0)

        shift = 8 * side
        m = tall(0, mz_ref)
        if shift:
            m = pltpu.roll(m, shift, 1)
        x = pltpu.roll(tall(1, ex_ref), 8 + shift, 1)
        y = pltpu.roll(tall(2, ey_ref), 16 + shift, 1)
        ref[0:TALL] = jnp.where(lane < 8, m, jnp.where(lane < 16, x, y))
        coefs = coefs_ref[...]
        wide = pltpu.roll(jnp.concatenate([coefs, jnp.zeros_like(coefs)], axis=1), 8, 1)
        lower = wide[:, 0:128]
        upper = wide[:, 128:256]
        place = lax.broadcasted_iota(jnp.int32, (32, 128), 1)
        gap = jnp.zeros((16, 128), F32)

        def both(lines, near_from, far_from, near_to, far_to, base):
            near = lines[24:48, half]
            far = lines[48:56, half]
            at_near = jnp.concatenate(
                [
                    pltpu.roll(near, (near_to - near_from) % 128, 1),
                    pltpu.roll(near[0:8], (near_to - far_from) % 128, 1),
                ],
                axis=0,
            )
            at_far = jnp.concatenate(
                [
                    pltpu.roll(far, (far_to - near_from) % 128, 1),
                    gap,
                    pltpu.roll(far, (far_to - far_from) % 128, 1),
                ],
                axis=0,
            )
            return jnp.where(place == near_to, at_near, jnp.where(place == far_to, at_far, base))

        near_from, far_from = (127, 126) if side else (0, 1)
        ref[TALL : TALL + 32] = both(tops, near_from, far_from, 7, 6, lower)
        ref[TALL + 32 :] = both(bottoms, near_from, far_from, 8, 9, upper)


def linear(coefs, x, y):
    return (
        coefs[0:1] + x * coefs[2:3] + y * coefs[4:5],
        coefs[1:2] + x * coefs[3:4] + y * coefs[5:6],
    )


def quadratic(coefs, x0, y0, x1, y1):
    terms = [linear(coefs[FIRST * (c + 1) : FIRST * (c + 2)], x1, y1) for c in range(3)]
    return tuple(terms[0][k] + x0 * terms[1][k] + y0 * terms[2][k] for k in range(2))


def turned(value):
    rows, lanes = value.shape
    if rows < 128:
        value = jnp.concatenate([value, jnp.zeros((128 - rows, lanes), F32)], axis=0)
    elif rows < 256:
        value = jnp.concatenate([value, jnp.zeros((256 - rows, lanes), F32)], axis=0)
    return value.T


def advance(x, y, z, source_x, source_y):
    y_next = pltpu.roll(y, TALL - 1, 0)
    x_next = pltpu.roll(x, WIDE - 1, 1)
    z = z - COURANT * ((y_next - y) - (x_next - x))
    x = x + COURANT * (z - pltpu.roll(z, 1, 1)) - source_x
    y = y - COURANT * (z - pltpu.roll(z, 1, 0)) - source_y
    return x, y, z


OWN = slice(128, 128 + CY)


def main_kernel(
    live_ref, cells_ref, ex_ref, ey_ref, mz_ref, acc_ref, table_ref, old_ref,
    top_ref, bottom_ref, left_ref, right_ref, dens_ref,
    evolved_ref, out_x, out_y, out_z, state, buf, acc, fld, xs, ys, zs, sems,
):
    count = count_of(live_ref)
    total = dens_ref.shape[0] // TILE

    def fetch(t):
        return pltpu.make_async_copy(dens_ref.at[tile_rows(t), :], buf.at[tile_rows(t), :], sems.at[t])

    def write(t):
        return pltpu.make_async_copy(buf.at[tile_rows(t), :], evolved_ref.at[tile_rows(t), :], sems.at[t])

    sweep(count, total, lambda t: fetch(t).start())

    left = left_ref[...]
    right = right_ref[...]

    def extended(k, field_ref):
        rows = slice(8 * k, 8 * k + 8)
        middle = jnp.concatenate([top_ref[rows, :], field_ref[...], bottom_ref[rows, :]], axis=0)
        before = pltpu.roll(left[0:TALL], 120 - 8 * k, 1)
        after = right[0:TALL]
        if k:
            after = pltpu.roll(after, 128 - 8 * k, 1)
        return jnp.concatenate([before, middle, after], axis=1)

    zs[...] = extended(0, mz_ref)
    xs[...] = extended(1, ex_ref)
    ys[...] = extended(2, ey_ref)

    sides = []
    for package, near, far in ((left, 7, 6), (right, 0, 1)):
        lines = turned(package[0:TALL])
        coefs = jnp.concatenate([package[TALL : TALL + 32], package[TALL + 32 :]], axis=1)
        near_x, near_y = lines[8 + near : 9 + near], lines[16 + near : 17 + near]
        far_x, far_y = lines[8 + far : 9 + far], lines[16 + far : 17 + far]
        sides.append(
            (
                coefs,
                near_x,
                near_y,
                linear(coefs[0:FIRST], near_x, near_y),
                linear(coefs[ORDERS : ORDERS + FIRST], far_x, far_y),
            )
        )
    lane = lax.broadcasted_iota(jnp.int32, (TALL, 128), 1)
    line = lax.broadcasted_iota(jnp.int32, (8, CY), 0)

    def assembled(tops, rows, bottoms, before, after):
        middle = jnp.concatenate([tops, rows, bottoms], axis=0)
        return jnp.concatenate([before, middle, after], axis=1)

    (lc, lx0, ly0, lnear, lfar), (rc, rx0, ry0, rnear, rfar) = sides
    columns = turned(
        jnp.concatenate(
            [lfar[0], lnear[0], lfar[1], lnear[1], rnear[0], rfar[0], rnear[1], rfar[1]], axis=0
        )
    )[0:TALL]
    zero_line = jnp.zeros((8, CY), F32)
    starts = []
    top_lines = []
    bottom_lines = []
    for lines_ref, near, far, out in (
        (top_ref, 7, 6, top_lines),
        (bottom_ref, 0, 1, bottom_lines),
    ):
        near_x, near_y = lines_ref[8 + near : 9 + near, :], lines_ref[16 + near : 17 + near, :]
        far_x, far_y = lines_ref[8 + far : 9 + far, :], lines_ref[16 + far : 17 + far, :]
        starts.append((near_x, near_y))
        at_near = linear(lines_ref[24 : 24 + FIRST, :], near_x, near_y)
        at_far = linear(lines_ref[48 : 48 + FIRST, :], far_x, far_y)
        for k in range(2):
            out.append(
                jnp.where(line == near, at_near[k], jnp.where(line == far, at_far[k], zero_line))
            )

    def own(ref, k):
        return ref[2 * k * CX : (2 * k + 1) * CX] + ref[(2 * k + 1) * CX : (2 * k + 2) * CX]

    sources = []
    for k in range(2):
        before = jnp.where(lane >= 126, pltpu.roll(columns, 126 - 2 * k, 1), 0.0)
        after = jnp.where(lane < 2, pltpu.roll(columns, 124 - 2 * k, 1), 0.0)
        sources.append(assembled(top_lines[k], own(acc_ref, k), bottom_lines[k], before, after))
    x, y, z = advance(xs[...], ys[...], zs[...], *sources)
    xs[...] = x
    ys[...] = y
    zs[...] = z

    def flush(t):
        fetch(t).wait()
        write(t).start()

    sweep(count, total, flush)

    def prime():
        fld[...] = split_fields(xs[8 : 8 + CX, OWN], ys[8 : 8 + CX, OWN])
        acc[...] = jnp.zeros_like(acc)

    prime()

    def second(t):
        updated = tile_step(t, cells_ref, fld[...], table_ref[...], stored(old_ref, t), acc)
        save_state(state, t, updated)

    sweep(0, count, second)

    x = xs[...]
    y = ys[...]
    xl, yl = x[:, 0:128], y[:, 0:128]
    xr, yr = x[:, 384:512], y[:, 384:512]
    edge = jnp.where(
        lane == 127,
        xl,
        jnp.where(
            lane == 126,
            pltpu.roll(yl, 127, 1),
            jnp.where(lane == 0, xr, jnp.where(lane == 1, pltpu.roll(yr, 1, 1), 0.0)),
        ),
    )
    rows = turned(edge)
    ends_l = quadratic(lc, lx0, ly0, rows[127:128], rows[126:127])
    ends_r = quadratic(rc, rx0, ry0, rows[0:1], rows[1:2])
    columns = turned(
        jnp.concatenate([ends_l[0], ends_l[1], ends_r[0], ends_r[1], jnp.zeros((4, CY), F32)], axis=0)
    )[0:TALL]
    lines = []
    for (x0, y0), lines_ref, near, at in (
        (starts[0], top_ref, 7, 7),
        (starts[1], bottom_ref, 0, 8 + CX),
    ):
        ends = quadratic(
            lines_ref[24:48, :], x0, y0, x[at : at + 1, OWN], y[at : at + 1, OWN]
        )
        lines.append([jnp.where(line == near, ends[k], zero_line) for k in range(2)])
    sources = []
    for k in range(2):
        before = jnp.where(lane == 127, pltpu.roll(columns, 127 - k, 1), 0.0)
        after = jnp.where(lane == 0, pltpu.roll(columns, 126 - k, 1), 0.0)
        sources.append(assembled(lines[0][k], own(acc, k), lines[1][k], before, after))
    x, y, z = advance(x, y, zs[...], *sources)
    xs[...] = x
    ys[...] = y
    zs[...] = z
    prime()

    def third(t):
        updated = tile_step(t, cells_ref, fld[...], table_ref[...], stored(state, t), acc)
        buf[tile_rows(t), :] = updated.T
        write(t).start()

    sweep(0, count, third)
    blank = jnp.zeros((TALL, 128), F32)
    sources = [assembled(zero_line, own(acc, k), zero_line, blank, blank) for k in range(2)]
    x, y, z = advance(xs[...], ys[...], zs[...], *sources)
    out_x[...] = x[8 : 8 + CX, OWN]
    out_y[...] = y[8 : 8 + CX, OWN]
    out_z[...] = z[8 : 8 + CX, OWN]
    sweep(0, total, lambda t: write(t).wait())


VMEM = pl.BlockSpec(memory_space=pltpu.VMEM)
SMEM = pl.BlockSpec(memory_space=pltpu.SMEM)
ANY = pl.BlockSpec(memory_space=pl.ANY)
LIMITS = pltpu.CompilerParams(vmem_limit_bytes=40 << 20)


def shaped(shape, dtype=F32):
    return jax.ShapeDtypeStruct(shape, dtype)


def ring(axis, step):
    count = lax.axis_size(axis)
    return [(i, (i + step) % count) for i in range(count)]


def pinned(value):
    return pltpu.with_memory_space_constraint(value, pltpu.VMEM)


def streamed(value):
    return pltpu.with_memory_space_constraint(value, pltpu.HBM)


def held(shape, dtype=F32):
    return pltpu.VMEM(shape, dtype)


def shards(density, cell_index, live_batches, propagator, dipoles, ex, ey, mz):
    slots = density.shape[0]
    tiles = slots // TILE
    cells = cell_index.reshape(slots // 128, 128)
    buffer = pltpu.VMEM((slots, S2), F32)
    sems = pltpu.SemaphoreType.DMA((tiles,))
    sums = (4 * CX, CY)
    halved = pltpu.VMEM((4 * CX, CY), BF16)
    half = held((slots, S2), BF16)
    readout, low, high, west, east, hi, lo = pl.pallas_call(
        coefficient_kernel,
        out_shape=(
            shaped((8, S2)),
            shaped((LINES, CY)),
            shaped((LINES, CY)),
            shaped((32, CX)),
            shaped((32, CX)),
            half,
            half,
        ),
        in_specs=[SMEM] + [ANY] * 7,
        out_specs=(VMEM,) * 7,
        scratch_shapes=[
            buffer,
            pltpu.VMEM((128, CY), F32),
            pltpu.VMEM((128, CX), F32),
            pltpu.VMEM(propagator.shape, F32),
            pltpu.VMEM(dipoles.shape, F32),
            pltpu.VMEM(cells.shape, jnp.int32),
            sems,
            pltpu.SemaphoreType.DMA((9,)),
        ],
        compiler_params=LIMITS,
        name="coefficients",
    )(
        live_batches,
        *(streamed(value) for value in (cells, ex, ey, mz, propagator, dipoles, density)),
    )
    bottom = lax.ppermute(low, "gx", ring("gx", -1))
    top = lax.ppermute(high, "gx", ring("gx", 1))
    table = pl.pallas_call(
        table_kernel,
        out_shape=held((ROWS, 3 * S2), BF16),
        in_specs=[VMEM] * 2,
        out_specs=VMEM,
        compiler_params=LIMITS,
        name="table",
    )(propagator, readout)
    package = shaped((TALL + 64, 128))
    to_left, to_right = pl.pallas_call(
        corner_kernel,
        out_shape=(package, package),
        in_specs=[VMEM] * 5 + [VMEM] * 2 + [ANY],
        out_specs=(VMEM,) * 2,
        compiler_params=LIMITS,
        name="corners",
    )(ex, ey, mz, west, east, pinned(top), pinned(bottom), pinned(table))
    right = lax.ppermute(to_left, "gy", ring("gy", -1))
    left = lax.ppermute(to_right, "gy", ring("gy", 1))
    state, source = pl.pallas_call(
        first_kernel,
        out_shape=(held((2 * S2, slots), BF16), held(sums)),
        in_specs=[SMEM] + [VMEM] * 6,
        out_specs=(VMEM,) * 2,
        scratch_shapes=[halved],
        compiler_params=LIMITS,
        name="first",
    )(live_batches, cells, ex, ey, pinned(table), pinned(hi), pinned(lo))
    field = shaped((CX, CY))
    tall = pltpu.VMEM((TALL, WIDE), F32)
    return pl.pallas_call(
        main_kernel,
        out_shape=(shaped((slots, S2)), field, field, field),
        in_specs=[SMEM] + [VMEM] * 11 + [ANY],
        out_specs=(ANY,) + (VMEM,) * 3,
        scratch_shapes=[
            pltpu.VMEM((2 * S2, slots), BF16), buffer, pltpu.VMEM(sums, F32), halved,
            tall, tall, tall, sems,
        ],
        compiler_params=LIMITS,
        name="main",
    )(
        live_batches, cells, ex, ey, mz, pinned(source), pinned(table), pinned(state),
        pinned(top), pinned(bottom), pinned(left), pinned(right), streamed(density),
    )


def solution(mesh):
    placed = (
        P(("gx", "gy"), None),
        P(("gx", "gy")),
        P(("gx", "gy")),
        P(),
        P(),
        P("gx", "gy"),
        P("gx", "gy"),
        P("gx", "gy"),
    )
    return jax.shard_map(
        shards,
        mesh=mesh,
        in_specs=placed,
        out_specs=(P(("gx", "gy"), None), P("gx", "gy"), P("gx", "gy"), P("gx", "gy")),
        check_vma=False,
    )
```

```python
import jax
import jax.numpy as jnp
from jax import lax
from jax.experimental import pallas as pl
from jax.experimental.pallas import tpu as pltpu
from jax.sharding import PartitionSpec as P

BATCH = 64
STEPS = 3
TILE = 1024
SMALL = 512
COURANT = 0.5
CX = 128
CY = 256
S2 = 256
ROWS = 3 * S2 + 16
FIRST = 6
ORDERS = 24
LINES = 56
TALL = CX + 16
WIDE = CY + 256
F32 = jnp.float32
BF16 = jnp.bfloat16
NT = (((1,), (1,)), ((), ()))


def halves(x):
    hi = x.astype(BF16)
    return hi, (x - hi.astype(F32)).astype(BF16)


def fast_nt(a, b):
    return lax.dot_general(a, b, NT, preferred_element_type=F32)


def functionals_of(prop_ref, dip_ref):
    blocks = [halves(prop_ref[:, b * S2 : (b + 1) * S2]) for b in range(3)]

    def through(value, block):
        rows = value.shape[0]
        vh, vl = halves(value)
        wide = fast_nt(jnp.concatenate([vh, vl], axis=0), block[0])
        return wide[0:rows] + wide[rows:] + fast_nt(vh, block[1])

    dipoles = dip_ref[...]
    padded = jnp.concatenate([dipoles, jnp.zeros((6, S2), F32)], axis=0)
    reads = [through(padded, block)[0:2] for block in blocks]
    first = jnp.concatenate(
        [reads[0] - dipoles, reads[1], reads[2], jnp.zeros((2, S2), F32)], axis=0
    )
    second = [through(first, block)[0:FIRST] for block in blocks]
    return jnp.concatenate([first[0:FIRST], *second, jnp.zeros((8, S2), F32)], axis=0)


def table_kernel(prop_ref, readout_ref, table_ref):
    def put(rows, value):
        hi, lo = halves(value)
        table_ref[rows, 0:S2] = hi
        table_ref[rows, S2 : 2 * S2] = hi
        table_ref[rows, 2 * S2 :] = lo

    put(pl.ds(0, 16), jnp.concatenate([readout_ref[...], jnp.zeros((8, S2), F32)], axis=0))
    for b in range(3):
        block = prop_ref[:, b * S2 : (b + 1) * S2].T
        for q in range(S2 // 16):
            put(pl.ds(16 + 48 * q + 16 * b, 16), block[16 * q : 16 * q + 16])


def cells_of(cells_ref, t, size=TILE):
    cell = jnp.concatenate(
        [cells_ref[pl.ds(t * (size // 128) + j, 1), :] for j in range(size // 128)], axis=1
    )
    return cell >> 8, cell & (CY - 1)


def matches(index, size):
    return lax.broadcasted_iota(jnp.int32, (size, index.shape[1]), 0) == index


def one_hot(index, size):
    return jnp.where(matches(index, size), 1.0, 0.0).astype(BF16)


def count_of(live_ref, size=TILE):
    return live_ref[0] * BATCH // size


def tile_rows(t, size=TILE):
    return pl.ds(pl.multiple_of(t * size, size), size)


def sweep(lower, upper, body):
    def wrapped(t, carry):
        body(t)
        return carry

    lax.fori_loop(lower, upper, wrapped, 0)


def coefficient_kernel(
    live_ref, cells_hbm, ex_hbm, ey_hbm, mz_hbm, prop_hbm, dip_hbm, dens_hbm,
    readout_ref, low_ref, high_ref, west_ref, east_ref, hi_ref, lo_ref,
    buf, by_row, by_col, prop_ref, dip_ref, cells_ref, sems, loads,
):
    count = count_of(live_ref, SMALL)

    def copy(t):
        return pltpu.make_async_copy(dens_hbm.at[tile_rows(t, SMALL), :], buf.at[tile_rows(t, SMALL), :], sems.at[t])

    pairs = [(dip_hbm, dip_ref), (prop_hbm, prop_ref), (cells_hbm, cells_ref)]
    for ref, start in ((low_ref, 0), (high_ref, CX - 8)):
        for k, field in enumerate((mz_hbm, ex_hbm, ey_hbm)):
            pairs.append((field.at[pl.ds(start, 8), :], ref.at[pl.ds(8 * k, 8), :]))
    moves = [pltpu.make_async_copy(src, dst, loads.at[k]) for k, (src, dst) in enumerate(pairs)]
    for move in moves[:3]:
        move.start()
    sweep(0, count, lambda t: copy(t).start())
    for move in moves[3:]:
        move.start()
    for move in moves[:2]:
        move.wait()
    functionals = functionals_of(prop_ref, dip_ref)
    readout_ref[...] = functionals[0:8]
    fh, fl = halves(functionals)
    stacked = jnp.concatenate([fh, fl], axis=0)
    by_row[...] = jnp.zeros_like(by_row)
    by_col[...] = jnp.zeros_like(by_col)

    def picked(index, near, far, parts):
        out = []
        for place, rows in ((near[0], ORDERS), (near[1], ORDERS), (far[0], 8), (far[1], 8)):
            for part in parts:
                out.append(jnp.where(index == place, part[0:rows], 0.0))
        return jnp.concatenate(out, axis=0).astype(BF16)

    def body(t):
        copy(t).wait()
        dh, dl = halves(buf[tile_rows(t, SMALL), :])
        hi_ref[tile_rows(t, SMALL), :] = dh
        lo_ref[tile_rows(t, SMALL), :] = dl
        wide = fast_nt(stacked, dh)
        values = wide[0:32] + wide[32:64] + fast_nt(fh, dl)
        vh, vl = halves(values)
        parts = (vh.astype(F32), vl.astype(F32))
        row, col = cells_of(cells_ref, t, SMALL)
        by_row[...] += fast_nt(picked(row, (0, CX - 1), (1, CX - 2), parts), one_hot(col, CY))
        by_col[...] += fast_nt(picked(col, (0, CY - 1), (1, CY - 2), parts), one_hot(row, CX))

    for move in moves[2:]:
        move.wait()
    sweep(0, count, body)

    def side(ref, which):
        near = 2 * ORDERS * which
        far = 4 * ORDERS + 16 * which
        return (
            ref[near : near + ORDERS] + ref[near + ORDERS : near + 2 * ORDERS],
            ref[far : far + 8] + ref[far + 8 : far + 16],
        )

    for which, ref in ((0, low_ref), (1, high_ref)):
        near, far = side(by_row, which)
        ref[24:48] = near
        ref[48:56] = far
    for which, ref in ((0, west_ref), (1, east_ref)):
        near, far = side(by_col, which)
        ref[0:ORDERS] = near
        ref[ORDERS:] = far


def tile_step(t, cells_ref, fields, table, state, source_ref):
    row, col = cells_of(cells_ref, t)
    hot_col = one_hot(col, CY)
    mask = matches(row, CX)
    lines = jnp.dot(fields, hot_col, preferred_element_type=F32)
    sample_x = jnp.sum(
        jnp.where(mask, lines[0:CX] + lines[CX : 2 * CX], 0.0), axis=0, keepdims=True
    )
    sample_y = jnp.sum(
        jnp.where(mask, lines[2 * CX : 3 * CX] + lines[3 * CX :], 0.0), axis=0, keepdims=True
    )
    product = state(table)
    reads = product[0:8]
    current_x = reads[0:1] + sample_x * reads[2:3] + sample_y * reads[4:5]
    current_y = reads[1:2] + sample_x * reads[3:4] + sample_y * reads[5:6]
    parts = []
    for current in (current_x, current_y):
        for part in halves(current):
            parts.append(jnp.where(mask, part.astype(F32), 0.0).astype(BF16))
    source_ref[...] += fast_nt(jnp.concatenate(parts, axis=0), hot_col)
    groups = []
    for q in range(S2 // 16):
        base = 16 + 48 * q
        groups.append(
            product[base : base + 16]
            + sample_x * product[base + 16 : base + 32]
            + sample_y * product[base + 32 : base + 48]
        )
    return jnp.concatenate(groups, axis=0)


def split_fields(ex, ey):
    xh, xl = halves(ex)
    yh, yl = halves(ey)
    return jnp.concatenate([xh, xl, yh, yl], axis=0)


def save_state(state_ref, t, updated):
    hi, lo = halves(updated)
    state_ref[0:S2, tile_rows(t)] = hi
    state_ref[S2:, tile_rows(t)] = lo


def stored(state_ref, t):
    def product(table):
        hi, lo = state_ref[0:S2, tile_rows(t)], state_ref[S2:, tile_rows(t)]
        return jnp.dot(table, jnp.concatenate([hi, lo, hi], axis=0), preferred_element_type=F32)

    return product


def first_tile(t, cells_ref, fields, table_ref, hi_ref, lo_ref, state_ref, acc):
    def product(table):
        hi, lo = hi_ref[tile_rows(t), :], lo_ref[tile_rows(t), :]
        return fast_nt(table, jnp.concatenate([hi, lo, hi], axis=1))

    save_state(state_ref, 0, tile_step(t, cells_ref, fields, table_ref[...], product, acc))


def early_kernel(
    live_ref, cells_ref, ex_ref, ey_ref, table_ref, hi_ref, lo_ref, state_ref, acc
):
    acc[...] = jnp.zeros_like(acc)

    @pl.when(count_of(live_ref) > 0)
    def _():
        fields = split_fields(ex_ref[...], ey_ref[...])
        first_tile(0, cells_ref, fields, table_ref, hi_ref, lo_ref, state_ref, acc)


def late_kernel(
    live_ref, cells_ref, ex_ref, ey_ref, table_ref, hi_ref, lo_ref, before_ref, after_ref,
    state_ref, acc,
):
    acc[...] = before_ref[...]

    @pl.when(count_of(live_ref) > 1)
    def _():
        fields = split_fields(ex_ref[...], ey_ref[...])
        first_tile(1, cells_ref, fields, table_ref, hi_ref, lo_ref, state_ref, acc)


def corner_kernel(
    ex_ref, ey_ref, mz_ref, west_ref, east_ref, top_ref, bottom_ref, after_ref, left_ref, right_ref
):
    tops = top_ref[...]
    bottoms = bottom_ref[...]
    lane = lax.broadcasted_iota(jnp.int32, (TALL, 128), 1)
    for side, ref, coefs_ref in ((0, left_ref, west_ref), (1, right_ref, east_ref)):
        half = slice(128 * side, 128 * side + 128)

        def tall(k, field_ref):
            rows = slice(8 * k, 8 * k + 8)
            return jnp.concatenate([tops[rows, half], field_ref[:, half], bottoms[rows, half]], axis=0)

        shift = 8 * side
        m = tall(0, mz_ref)
        if shift:
            m = pltpu.roll(m, shift, 1)
        x = pltpu.roll(tall(1, ex_ref), 8 + shift, 1)
        y = pltpu.roll(tall(2, ey_ref), 16 + shift, 1)
        ref[0:TALL] = jnp.where(lane < 8, m, jnp.where(lane < 16, x, y))
        coefs = coefs_ref[...]
        wide = pltpu.roll(jnp.concatenate([coefs, jnp.zeros_like(coefs)], axis=1), 8, 1)
        lower = wide[:, 0:128]
        upper = wide[:, 128:256]
        place = lax.broadcasted_iota(jnp.int32, (32, 128), 1)
        gap = jnp.zeros((16, 128), F32)

        def both(lines, near_from, far_from, near_to, far_to, base):
            near = lines[24:48, half]
            far = lines[48:56, half]
            at_near = jnp.concatenate(
                [
                    pltpu.roll(near, (near_to - near_from) % 128, 1),
                    pltpu.roll(near[0:8], (near_to - far_from) % 128, 1),
                ],
                axis=0,
            )
            at_far = jnp.concatenate(
                [
                    pltpu.roll(far, (far_to - near_from) % 128, 1),
                    gap,
                    pltpu.roll(far, (far_to - far_from) % 128, 1),
                ],
                axis=0,
            )
            return jnp.where(place == near_to, at_near, jnp.where(place == far_to, at_far, base))

        near_from, far_from = (127, 126) if side else (0, 1)
        ref[TALL : TALL + 32] = both(tops, near_from, far_from, 7, 6, lower)
        ref[TALL + 32 :] = both(bottoms, near_from, far_from, 8, 9, upper)


def linear(coefs, x, y):
    return (
        coefs[0:1] + x * coefs[2:3] + y * coefs[4:5],
        coefs[1:2] + x * coefs[3:4] + y * coefs[5:6],
    )


def quadratic(coefs, x0, y0, x1, y1):
    terms = [linear(coefs[FIRST * (c + 1) : FIRST * (c + 2)], x1, y1) for c in range(3)]
    return tuple(terms[0][k] + x0 * terms[1][k] + y0 * terms[2][k] for k in range(2))


def turned(value):
    rows, lanes = value.shape
    if rows < 128:
        value = jnp.concatenate([value, jnp.zeros((128 - rows, lanes), F32)], axis=0)
    elif rows < 256:
        value = jnp.concatenate([value, jnp.zeros((256 - rows, lanes), F32)], axis=0)
    return value.T


def advance(x, y, z, source_x, source_y):
    y_next = pltpu.roll(y, TALL - 1, 0)
    x_next = pltpu.roll(x, WIDE - 1, 1)
    z = z - COURANT * ((y_next - y) - (x_next - x))
    x = x + COURANT * (z - pltpu.roll(z, 1, 1)) - source_x
    y = y - COURANT * (z - pltpu.roll(z, 1, 0)) - source_y
    return x, y, z


OWN = slice(128, 128 + CY)


def main_kernel(
    live_ref, cells_ref, ex_ref, ey_ref, mz_ref, acc_ref, table_ref, early_ref, late_ref,
    top_ref, bottom_ref, left_ref, right_ref, dens_ref,
    evolved_ref, out_x, out_y, out_z, state, buf, acc, fld, xs, ys, zs, sems,
):
    count = count_of(live_ref)
    total = dens_ref.shape[0] // TILE

    def fetch(t):
        return pltpu.make_async_copy(dens_ref.at[tile_rows(t), :], buf.at[tile_rows(t), :], sems.at[t])

    def write(t):
        return pltpu.make_async_copy(buf.at[tile_rows(t), :], evolved_ref.at[tile_rows(t), :], sems.at[t])

    sweep(count, total, lambda t: fetch(t).start())

    left = left_ref[...]
    right = right_ref[...]

    def extended(k, field_ref):
        rows = slice(8 * k, 8 * k + 8)
        middle = jnp.concatenate([top_ref[rows, :], field_ref[...], bottom_ref[rows, :]], axis=0)
        before = pltpu.roll(left[0:TALL], 120 - 8 * k, 1)
        after = right[0:TALL]
        if k:
            after = pltpu.roll(after, 128 - 8 * k, 1)
        return jnp.concatenate([before, middle, after], axis=1)

    zs[...] = extended(0, mz_ref)
    xs[...] = extended(1, ex_ref)
    ys[...] = extended(2, ey_ref)

    sides = []
    for package, near, far in ((left, 7, 6), (right, 0, 1)):
        lines = turned(package[0:TALL])
        coefs = jnp.concatenate([package[TALL : TALL + 32], package[TALL + 32 :]], axis=1)
        near_x, near_y = lines[8 + near : 9 + near], lines[16 + near : 17 + near]
        far_x, far_y = lines[8 + far : 9 + far], lines[16 + far : 17 + far]
        sides.append(
            (
                coefs,
                near_x,
                near_y,
                linear(coefs[0:FIRST], near_x, near_y),
                linear(coefs[ORDERS : ORDERS + FIRST], far_x, far_y),
            )
        )
    lane = lax.broadcasted_iota(jnp.int32, (TALL, 128), 1)
    line = lax.broadcasted_iota(jnp.int32, (8, CY), 0)

    def assembled(tops, rows, bottoms, before, after):
        middle = jnp.concatenate([tops, rows, bottoms], axis=0)
        return jnp.concatenate([before, middle, after], axis=1)

    (lc, lx0, ly0, lnear, lfar), (rc, rx0, ry0, rnear, rfar) = sides
    columns = turned(
        jnp.concatenate(
            [lfar[0], lnear[0], lfar[1], lnear[1], rnear[0], rfar[0], rnear[1], rfar[1]], axis=0
        )
    )[0:TALL]
    zero_line = jnp.zeros((8, CY), F32)
    starts = []
    top_lines = []
    bottom_lines = []
    for lines_ref, near, far, out in (
        (top_ref, 7, 6, top_lines),
        (bottom_ref, 0, 1, bottom_lines),
    ):
        near_x, near_y = lines_ref[8 + near : 9 + near, :], lines_ref[16 + near : 17 + near, :]
        far_x, far_y = lines_ref[8 + far : 9 + far, :], lines_ref[16 + far : 17 + far, :]
        starts.append((near_x, near_y))
        at_near = linear(lines_ref[24 : 24 + FIRST, :], near_x, near_y)
        at_far = linear(lines_ref[48 : 48 + FIRST, :], far_x, far_y)
        for k in range(2):
            out.append(
                jnp.where(line == near, at_near[k], jnp.where(line == far, at_far[k], zero_line))
            )

    def own(ref, k):
        return ref[2 * k * CX : (2 * k + 1) * CX] + ref[(2 * k + 1) * CX : (2 * k + 2) * CX]

    sources = []
    for k in range(2):
        before = jnp.where(lane >= 126, pltpu.roll(columns, 126 - 2 * k, 1), 0.0)
        after = jnp.where(lane < 2, pltpu.roll(columns, 124 - 2 * k, 1), 0.0)
        sources.append(assembled(top_lines[k], own(acc_ref, k), bottom_lines[k], before, after))
    x, y, z = advance(xs[...], ys[...], zs[...], *sources)
    xs[...] = x
    ys[...] = y
    zs[...] = z

    def flush(t):
        fetch(t).wait()
        write(t).start()

    sweep(count, total, flush)

    def prime():
        fld[...] = split_fields(xs[8 : 8 + CX, OWN], ys[8 : 8 + CX, OWN])
        acc[...] = jnp.zeros_like(acc)

    prime()

    for t, old_ref in enumerate((early_ref, late_ref)):

        @pl.when(count > t)
        def _():
            product = stored(old_ref, 0)
            save_state(state, t, tile_step(t, cells_ref, fld[...], table_ref[...], product, acc))

    x = xs[...]
    y = ys[...]
    xl, yl = x[:, 0:128], y[:, 0:128]
    xr, yr = x[:, 384:512], y[:, 384:512]
    edge = jnp.where(
        lane == 127,
        xl,
        jnp.where(
            lane == 126,
            pltpu.roll(yl, 127, 1),
            jnp.where(lane == 0, xr, jnp.where(lane == 1, pltpu.roll(yr, 1, 1), 0.0)),
        ),
    )
    rows = turned(edge)
    ends_l = quadratic(lc, lx0, ly0, rows[127:128], rows[126:127])
    ends_r = quadratic(rc, rx0, ry0, rows[0:1], rows[1:2])
    columns = turned(
        jnp.concatenate([ends_l[0], ends_l[1], ends_r[0], ends_r[1], jnp.zeros((4, CY), F32)], axis=0)
    )[0:TALL]
    lines = []
    for (x0, y0), lines_ref, near, at in (
        (starts[0], top_ref, 7, 7),
        (starts[1], bottom_ref, 0, 8 + CX),
    ):
        ends = quadratic(
            lines_ref[24:48, :], x0, y0, x[at : at + 1, OWN], y[at : at + 1, OWN]
        )
        lines.append([jnp.where(line == near, ends[k], zero_line) for k in range(2)])
    sources = []
    for k in range(2):
        before = jnp.where(lane == 127, pltpu.roll(columns, 127 - k, 1), 0.0)
        after = jnp.where(lane == 0, pltpu.roll(columns, 126 - k, 1), 0.0)
        sources.append(assembled(lines[0][k], own(acc, k), lines[1][k], before, after))
    x, y, z = advance(x, y, zs[...], *sources)
    xs[...] = x
    ys[...] = y
    zs[...] = z
    prime()

    def third(t):
        updated = tile_step(t, cells_ref, fld[...], table_ref[...], stored(state, t), acc)
        buf[tile_rows(t), :] = updated.T
        write(t).start()

    sweep(0, count, third)
    blank = jnp.zeros((TALL, 128), F32)
    sources = [assembled(zero_line, own(acc, k), zero_line, blank, blank) for k in range(2)]
    x, y, z = advance(xs[...], ys[...], zs[...], *sources)
    out_x[...] = x[8 : 8 + CX, OWN]
    out_y[...] = y[8 : 8 + CX, OWN]
    out_z[...] = z[8 : 8 + CX, OWN]
    sweep(0, total, lambda t: write(t).wait())


VMEM = pl.BlockSpec(memory_space=pltpu.VMEM)
SMEM = pl.BlockSpec(memory_space=pltpu.SMEM)
ANY = pl.BlockSpec(memory_space=pl.ANY)
LIMITS = pltpu.CompilerParams(vmem_limit_bytes=40 << 20)


def shaped(shape, dtype=F32):
    return jax.ShapeDtypeStruct(shape, dtype)


def ring(axis, step):
    count = lax.axis_size(axis)
    return [(i, (i + step) % count) for i in range(count)]


def pinned(value):
    return pltpu.with_memory_space_constraint(value, pltpu.VMEM)


def streamed(value):
    return pltpu.with_memory_space_constraint(value, pltpu.HBM)


def held(shape, dtype=F32):
    return pltpu.VMEM(shape, dtype)


def shards(density, cell_index, live_batches, propagator, dipoles, ex, ey, mz):
    slots = density.shape[0]
    tiles = slots // TILE
    assert tiles == 2
    cells = cell_index.reshape(slots // 128, 128)
    buffer = pltpu.VMEM((slots, S2), F32)
    sems = pltpu.SemaphoreType.DMA((tiles,))
    sums = (4 * CX, CY)
    halved = pltpu.VMEM((4 * CX, CY), BF16)
    half = held((slots, S2), BF16)
    readout, low, high, west, east, hi, lo = pl.pallas_call(
        coefficient_kernel,
        out_shape=(
            shaped((8, S2)),
            shaped((LINES, CY)),
            shaped((LINES, CY)),
            shaped((32, CX)),
            shaped((32, CX)),
            half,
            half,
        ),
        in_specs=[SMEM] + [ANY] * 7,
        out_specs=(VMEM,) * 7,
        scratch_shapes=[
            buffer,
            pltpu.VMEM((128, CY), F32),
            pltpu.VMEM((128, CX), F32),
            pltpu.VMEM(propagator.shape, F32),
            pltpu.VMEM(dipoles.shape, F32),
            pltpu.VMEM(cells.shape, jnp.int32),
            pltpu.SemaphoreType.DMA((slots // SMALL,)),
            pltpu.SemaphoreType.DMA((9,)),
        ],
        compiler_params=LIMITS,
        name="coefficients",
    )(
        live_batches,
        *(streamed(value) for value in (cells, ex, ey, mz, propagator, dipoles, density)),
    )
    bottom = lax.ppermute(low, "gx", ring("gx", -1))
    top = lax.ppermute(high, "gx", ring("gx", 1))
    table = pl.pallas_call(
        table_kernel,
        out_shape=held((ROWS, 3 * S2), BF16),
        in_specs=[VMEM] * 2,
        out_specs=VMEM,
        compiler_params=LIMITS,
        name="table",
    )(propagator, readout)
    piece = held((2 * S2, TILE), BF16)
    common = (live_batches, cells, ex, ey, pinned(table), pinned(hi), pinned(lo))
    early, source = pl.pallas_call(
        early_kernel,
        out_shape=(piece, held(sums)),
        in_specs=[SMEM] + [VMEM] * 6,
        out_specs=(VMEM,) * 2,
        compiler_params=LIMITS,
        name="early",
    )(*common)
    package = shaped((TALL + 64, 128))
    to_left, to_right = pl.pallas_call(
        corner_kernel,
        out_shape=(package, package),
        in_specs=[VMEM] * 5 + [VMEM] * 2 + [ANY],
        out_specs=(VMEM,) * 2,
        compiler_params=LIMITS,
        name="corners",
    )(ex, ey, mz, west, east, pinned(top), pinned(bottom), pinned(source))
    right = lax.ppermute(to_left, "gy", ring("gy", -1))
    left = lax.ppermute(to_right, "gy", ring("gy", 1))
    late, source = pl.pallas_call(
        late_kernel,
        out_shape=(piece, held(sums)),
        in_specs=[SMEM] + [VMEM] * 7 + [ANY],
        out_specs=(VMEM,) * 2,
        compiler_params=LIMITS,
        name="late",
    )(*common, pinned(source), to_left)
    field = shaped((CX, CY))
    tall = pltpu.VMEM((TALL, WIDE), F32)
    return pl.pallas_call(
        main_kernel,
        out_shape=(shaped((slots, S2)), field, field, field),
        in_specs=[SMEM] + [VMEM] * 12 + [ANY],
        out_specs=(ANY,) + (VMEM,) * 3,
        scratch_shapes=[
            pltpu.VMEM((2 * S2, slots), BF16), buffer, pltpu.VMEM(sums, F32), halved,
            tall, tall, tall, sems,
        ],
        compiler_params=LIMITS,
        name="main",
    )(
        live_batches, cells, ex, ey, mz, pinned(source), pinned(table), pinned(early),
        pinned(late),
        pinned(top), pinned(bottom), pinned(left), pinned(right), streamed(density),
    )


def solution(mesh):
    placed = (
        P(("gx", "gy"), None),
        P(("gx", "gy")),
        P(("gx", "gy")),
        P(),
        P(),
        P("gx", "gy"),
        P("gx", "gy"),
        P("gx", "gy"),
    )
    return jax.shard_map(
        shards,
        mesh=mesh,
        in_specs=placed,
        out_specs=(P(("gx", "gy"), None), P("gx", "gy"), P("gx", "gy"), P("gx", "gy")),
        check_vma=False,
    )
```

```python
import jax
import jax.numpy as jnp
from jax import lax
from jax.experimental import pallas as pl
from jax.experimental.pallas import tpu as pltpu
from jax.sharding import PartitionSpec as P

BATCH = 64
STEPS = 3
TILE = 1024
SMALL = 512
COURANT = 0.5
CX = 128
CY = 256
S2 = 256
ROWS = 3 * S2 + 16
FIRST = 6
ORDERS = 24
LINES = 56
TALL = CX + 16
WIDE = CY + 256
F32 = jnp.float32
BF16 = jnp.bfloat16
NT = (((1,), (1,)), ((), ()))


def halves(x):
    hi = x.astype(BF16)
    return hi, (x - hi.astype(F32)).astype(BF16)


def fast_nt(a, b):
    return lax.dot_general(a, b, NT, preferred_element_type=F32)


def functionals_of(prop_ref, dip_ref):
    blocks = [halves(prop_ref[:, b * S2 : (b + 1) * S2]) for b in range(3)]

    def through(value, block):
        rows = value.shape[0]
        vh, vl = halves(value)
        wide = fast_nt(jnp.concatenate([vh, vl], axis=0), block[0])
        return wide[0:rows] + wide[rows:] + fast_nt(vh, block[1])

    dipoles = dip_ref[...]
    padded = jnp.concatenate([dipoles, jnp.zeros((6, S2), F32)], axis=0)
    reads = [through(padded, block)[0:2] for block in blocks]
    first = jnp.concatenate(
        [reads[0] - dipoles, reads[1], reads[2], jnp.zeros((2, S2), F32)], axis=0
    )
    second = [through(first, block)[0:FIRST] for block in blocks]
    return jnp.concatenate([first[0:FIRST], *second, jnp.zeros((8, S2), F32)], axis=0)


def table_kernel(prop_ref, readout_ref, table_ref):
    def put(rows, value):
        hi, lo = halves(value)
        table_ref[rows, 0:S2] = hi
        table_ref[rows, S2 : 2 * S2] = hi
        table_ref[rows, 2 * S2 :] = lo

    put(pl.ds(0, 16), jnp.concatenate([readout_ref[...], jnp.zeros((8, S2), F32)], axis=0))
    for b in range(3):
        block = prop_ref[:, b * S2 : (b + 1) * S2].T
        for q in range(S2 // 16):
            put(pl.ds(16 + 48 * q + 16 * b, 16), block[16 * q : 16 * q + 16])


def cells_of(cells_ref, t, size=TILE):
    cell = jnp.concatenate(
        [cells_ref[pl.ds(t * (size // 128) + j, 1), :] for j in range(size // 128)], axis=1
    )
    return cell >> 8, cell & (CY - 1)


def matches(index, size):
    return lax.broadcasted_iota(jnp.int32, (size, index.shape[1]), 0) == index


def one_hot(index, size):
    return jnp.where(matches(index, size), 1.0, 0.0).astype(BF16)


def count_of(live_ref, size=TILE):
    return live_ref[0] * BATCH // size


def tile_rows(t, size=TILE):
    return pl.ds(pl.multiple_of(t * size, size), size)


def sweep(lower, upper, body):
    def wrapped(t, carry):
        body(t)
        return carry

    lax.fori_loop(lower, upper, wrapped, 0)


def coefficient_kernel(
    live_ref, cells_hbm, ex_hbm, ey_hbm, mz_hbm, prop_hbm, dip_hbm, dens_hbm,
    readout_ref, low_ref, high_ref, west_ref, east_ref, hi_ref, lo_ref,
    buf, by_row, by_col, prop_ref, dip_ref, cells_ref, sems, loads,
):
    count = count_of(live_ref, SMALL)

    def copy(t):
        return pltpu.make_async_copy(dens_hbm.at[tile_rows(t, SMALL), :], buf.at[tile_rows(t, SMALL), :], sems.at[t])

    pairs = [(dip_hbm, dip_ref), (prop_hbm, prop_ref), (cells_hbm, cells_ref)]
    for ref, start in ((low_ref, 0), (high_ref, CX - 8)):
        for k, field in enumerate((mz_hbm, ex_hbm, ey_hbm)):
            pairs.append((field.at[pl.ds(start, 8), :], ref.at[pl.ds(8 * k, 8), :]))
    moves = [pltpu.make_async_copy(src, dst, loads.at[k]) for k, (src, dst) in enumerate(pairs)]
    for move in moves[:3]:
        move.start()
    sweep(0, count, lambda t: copy(t).start())
    for move in moves[3:]:
        move.start()
    for move in moves[:2]:
        move.wait()
    functionals = functionals_of(prop_ref, dip_ref)
    readout_ref[...] = functionals[0:8]
    fh, fl = halves(functionals)
    stacked = jnp.concatenate([fh, fl], axis=0)
    by_row[...] = jnp.zeros_like(by_row)
    by_col[...] = jnp.zeros_like(by_col)

    def picked(index, near, far, parts):
        out = []
        for place, rows in ((near[0], ORDERS), (near[1], ORDERS), (far[0], 8), (far[1], 8)):
            for part in parts:
                out.append(jnp.where(index == place, part[0:rows], 0.0))
        return jnp.concatenate(out, axis=0).astype(BF16)

    def body(t):
        copy(t).wait()
        dh, dl = halves(buf[tile_rows(t, SMALL), :])
        hi_ref[tile_rows(t, SMALL), :] = dh
        lo_ref[tile_rows(t, SMALL), :] = dl
        wide = fast_nt(stacked, dh)
        values = wide[0:32] + wide[32:64] + fast_nt(fh, dl)
        vh, vl = halves(values)
        parts = (vh.astype(F32), vl.astype(F32))
        row, col = cells_of(cells_ref, t, SMALL)
        by_row[...] += fast_nt(picked(row, (0, CX - 1), (1, CX - 2), parts), one_hot(col, CY))
        by_col[...] += fast_nt(picked(col, (0, CY - 1), (1, CY - 2), parts), one_hot(row, CX))

    for move in moves[2:]:
        move.wait()
    sweep(0, count, body)

    def side(ref, which):
        near = 2 * ORDERS * which
        far = 4 * ORDERS + 16 * which
        return (
            ref[near : near + ORDERS] + ref[near + ORDERS : near + 2 * ORDERS],
            ref[far : far + 8] + ref[far + 8 : far + 16],
        )

    for which, ref in ((0, low_ref), (1, high_ref)):
        near, far = side(by_row, which)
        ref[24:48] = near
        ref[48:56] = far
    for which, ref in ((0, west_ref), (1, east_ref)):
        near, far = side(by_col, which)
        ref[0:ORDERS] = near
        ref[ORDERS:] = far


def tile_step(t, cells_ref, fields, make, source_ref):
    row, col = cells_of(cells_ref, t)
    hot_col = one_hot(col, CY)
    mask = matches(row, CX)
    lines = jnp.dot(fields, hot_col, preferred_element_type=F32)
    sample_x = jnp.sum(
        jnp.where(mask, lines[0:CX] + lines[CX : 2 * CX], 0.0), axis=0, keepdims=True
    )
    sample_y = jnp.sum(
        jnp.where(mask, lines[2 * CX : 3 * CX] + lines[3 * CX :], 0.0), axis=0, keepdims=True
    )
    product = make()
    reads = product(0, 8)
    current_x = reads[0:1] + sample_x * reads[2:3] + sample_y * reads[4:5]
    current_y = reads[1:2] + sample_x * reads[3:4] + sample_y * reads[5:6]
    parts = []
    for current in (current_x, current_y):
        for part in halves(current):
            parts.append(jnp.where(mask, part.astype(F32), 0.0).astype(BF16))
    source_ref[...] += fast_nt(jnp.concatenate(parts, axis=0), hot_col)
    groups = []
    for q in range(S2 // 16):
        base = 16 + 48 * q
        groups.append(
            product(base, 16)
            + sample_x * product(base + 16, 16)
            + sample_y * product(base + 32, 16)
        )
    return jnp.concatenate(groups, axis=0)


def split_fields(ex, ey):
    xh, xl = halves(ex)
    yh, yl = halves(ey)
    return jnp.concatenate([xh, xl, yh, yl], axis=0)


def save_state(state_ref, t, updated):
    hi, lo = halves(updated)
    state_ref[0:S2, tile_rows(t)] = hi
    state_ref[S2:, tile_rows(t)] = lo


def rows_of(value):
    return lambda start, size: value[start : start + size]


def stored_product(table_ref, state_ref, t):
    hi, lo = state_ref[0:S2, tile_rows(t)], state_ref[S2:, tile_rows(t)]
    return jnp.dot(
        table_ref[...], jnp.concatenate([hi, lo, hi], axis=0), preferred_element_type=F32
    )


def first_kernel(
    live_ref, cells_ref, ex_ref, ey_ref, table_ref, hi_ref, lo_ref, state_ref, acc, fld
):
    fld[...] = split_fields(ex_ref[...], ey_ref[...])
    acc[...] = jnp.zeros_like(acc)

    def body(t):
        hi, lo = hi_ref[tile_rows(t), :], lo_ref[tile_rows(t), :]

        def make():
            return rows_of(fast_nt(table_ref[...], jnp.concatenate([hi, lo, hi], axis=1)))

        save_state(state_ref, t, tile_step(t, cells_ref, fld[...], make, acc))

    sweep(0, count_of(live_ref), body)


def ahead_kernel(live_ref, table_ref, state_ref, after_ref, product_ref):
    def body(t):
        product_ref[:, tile_rows(t)] = stored_product(table_ref, state_ref, t)

    sweep(0, count_of(live_ref), body)


def turned(value):
    rows, lanes = value.shape
    if rows < 128:
        value = jnp.concatenate([value, jnp.zeros((128 - rows, lanes), F32)], axis=0)
    elif rows < 256:
        value = jnp.concatenate([value, jnp.zeros((256 - rows, lanes), F32)], axis=0)
    return value.T


def corner_kernel(
    ex_ref, ey_ref, mz_ref, west_ref, east_ref, top_ref, bottom_ref, after_ref, left_ref, right_ref
):
    tops = top_ref[...]
    bottoms = bottom_ref[...]
    lane = lax.broadcasted_iota(jnp.int32, (TALL, 128), 1)
    for side, ref, coefs_ref in ((0, left_ref, west_ref), (1, right_ref, east_ref)):
        half = slice(128 * side, 128 * side + 128)

        def tall(k, field_ref):
            rows = slice(8 * k, 8 * k + 8)
            return jnp.concatenate([tops[rows, half], field_ref[:, half], bottoms[rows, half]], axis=0)

        shift = 8 * side
        m = tall(0, mz_ref)
        if shift:
            m = pltpu.roll(m, shift, 1)
        x = pltpu.roll(tall(1, ex_ref), 8 + shift, 1)
        y = pltpu.roll(tall(2, ey_ref), 16 + shift, 1)
        items = jnp.where(lane < 8, m, jnp.where(lane < 16, x, y))
        ref[0:24] = turned(items)[0:24]
        coefs = coefs_ref[...]
        wide = pltpu.roll(jnp.concatenate([coefs, jnp.zeros_like(coefs)], axis=1), 8, 1)
        lower = wide[:, 0:128]
        upper = wide[:, 128:256]
        place = lax.broadcasted_iota(jnp.int32, (32, 128), 1)
        gap = jnp.zeros((16, 128), F32)

        def both(lines, near_from, far_from, near_to, far_to, base):
            near = lines[24:48, half]
            far = lines[48:56, half]
            at_near = jnp.concatenate(
                [
                    pltpu.roll(near, (near_to - near_from) % 128, 1),
                    pltpu.roll(near[0:8], (near_to - far_from) % 128, 1),
                ],
                axis=0,
            )
            at_far = jnp.concatenate(
                [
                    pltpu.roll(far, (far_to - near_from) % 128, 1),
                    gap,
                    pltpu.roll(far, (far_to - far_from) % 128, 1),
                ],
                axis=0,
            )
            return jnp.where(place == near_to, at_near, jnp.where(place == far_to, at_far, base))

        near_from, far_from = (127, 126) if side else (0, 1)
        ref[24:, 0:128] = both(tops, near_from, far_from, 7, 6, lower)
        ref[24:, 128:] = both(bottoms, near_from, far_from, 8, 9, upper)


def linear(coefs, x, y):
    return (
        coefs[0:1] + x * coefs[2:3] + y * coefs[4:5],
        coefs[1:2] + x * coefs[3:4] + y * coefs[5:6],
    )


def quadratic(coefs, x0, y0, x1, y1):
    terms = [linear(coefs[FIRST * (c + 1) : FIRST * (c + 2)], x1, y1) for c in range(3)]
    return tuple(terms[0][k] + x0 * terms[1][k] + y0 * terms[2][k] for k in range(2))


def advance(x, y, z, source_x, source_y):
    y_next = pltpu.roll(y, TALL - 1, 0)
    x_next = pltpu.roll(x, WIDE - 1, 1)
    z = z - COURANT * ((y_next - y) - (x_next - x))
    x = x + COURANT * (z - pltpu.roll(z, 1, 1)) - source_x
    y = y - COURANT * (z - pltpu.roll(z, 1, 0)) - source_y
    return x, y, z


OWN = slice(128, 128 + CY)


def main_kernel(
    live_ref, cells_ref, ex_ref, ey_ref, mz_ref, acc_ref, table_ref, product_ref,
    top_ref, bottom_ref, left_ref, right_ref, dens_ref,
    evolved_ref, out_x, out_y, out_z, state, buf, acc, fld, xs, ys, zs, sems,
):
    count = count_of(live_ref)
    total = dens_ref.shape[0] // TILE

    def fetch(t):
        return pltpu.make_async_copy(dens_ref.at[tile_rows(t), :], buf.at[tile_rows(t), :], sems.at[t])

    def write(t):
        return pltpu.make_async_copy(buf.at[tile_rows(t), :], evolved_ref.at[tile_rows(t), :], sems.at[t])

    sweep(count, total, lambda t: fetch(t).start())

    left = left_ref[...]
    right = right_ref[...]
    left_items = turned(left[0:24])[0:TALL]
    right_items = turned(right[0:24])[0:TALL]

    def extended(k, field_ref):
        rows = slice(8 * k, 8 * k + 8)
        middle = jnp.concatenate([top_ref[rows, :], field_ref[...], bottom_ref[rows, :]], axis=0)
        before = pltpu.roll(left_items, 120 - 8 * k, 1)
        after = right_items
        if k:
            after = pltpu.roll(after, 128 - 8 * k, 1)
        return jnp.concatenate([before, middle, after], axis=1)

    zs[...] = extended(0, mz_ref)
    xs[...] = extended(1, ex_ref)
    ys[...] = extended(2, ey_ref)

    sides = []
    for package, near, far in ((left, 7, 6), (right, 0, 1)):
        lines = package[0:24]
        coefs = package[24:]
        near_x, near_y = lines[8 + near : 9 + near], lines[16 + near : 17 + near]
        far_x, far_y = lines[8 + far : 9 + far], lines[16 + far : 17 + far]
        sides.append(
            (
                coefs,
                near_x,
                near_y,
                linear(coefs[0:FIRST], near_x, near_y),
                linear(coefs[ORDERS : ORDERS + FIRST], far_x, far_y),
            )
        )
    lane = lax.broadcasted_iota(jnp.int32, (TALL, 128), 1)
    line = lax.broadcasted_iota(jnp.int32, (8, CY), 0)

    def assembled(tops, rows, bottoms, before, after):
        middle = jnp.concatenate([tops, rows, bottoms], axis=0)
        return jnp.concatenate([before, middle, after], axis=1)

    (lc, lx0, ly0, lnear, lfar), (rc, rx0, ry0, rnear, rfar) = sides
    columns = turned(
        jnp.concatenate(
            [lfar[0], lnear[0], lfar[1], lnear[1], rnear[0], rfar[0], rnear[1], rfar[1]], axis=0
        )
    )[0:TALL]
    zero_line = jnp.zeros((8, CY), F32)
    starts = []
    top_lines = []
    bottom_lines = []
    for lines_ref, near, far, out in (
        (top_ref, 7, 6, top_lines),
        (bottom_ref, 0, 1, bottom_lines),
    ):
        near_x, near_y = lines_ref[8 + near : 9 + near, :], lines_ref[16 + near : 17 + near, :]
        far_x, far_y = lines_ref[8 + far : 9 + far, :], lines_ref[16 + far : 17 + far, :]
        starts.append((near_x, near_y))
        at_near = linear(lines_ref[24 : 24 + FIRST, :], near_x, near_y)
        at_far = linear(lines_ref[48 : 48 + FIRST, :], far_x, far_y)
        for k in range(2):
            out.append(
                jnp.where(line == near, at_near[k], jnp.where(line == far, at_far[k], zero_line))
            )

    def own(ref, k):
        return ref[2 * k * CX : (2 * k + 1) * CX] + ref[(2 * k + 1) * CX : (2 * k + 2) * CX]

    sources = []
    for k in range(2):
        before = jnp.where(lane >= 126, pltpu.roll(columns, 126 - 2 * k, 1), 0.0)
        after = jnp.where(lane < 2, pltpu.roll(columns, 124 - 2 * k, 1), 0.0)
        sources.append(assembled(top_lines[k], own(acc_ref, k), bottom_lines[k], before, after))
    x, y, z = advance(xs[...], ys[...], zs[...], *sources)
    xs[...] = x
    ys[...] = y
    zs[...] = z

    def flush(t):
        fetch(t).wait()
        write(t).start()

    sweep(count, total, flush)

    def prime():
        fld[...] = split_fields(xs[8 : 8 + CX, OWN], ys[8 : 8 + CX, OWN])
        acc[...] = jnp.zeros_like(acc)

    prime()

    def second(t):
        def make():
            return lambda start, size: product_ref[start : start + size, tile_rows(t)]

        save_state(state, t, tile_step(t, cells_ref, fld[...], make, acc))

    sweep(0, count, second)

    x = xs[...]
    y = ys[...]
    xl, yl = x[:, 0:128], y[:, 0:128]
    xr, yr = x[:, 384:512], y[:, 384:512]
    edge = jnp.where(
        lane == 127,
        xl,
        jnp.where(
            lane == 126,
            pltpu.roll(yl, 127, 1),
            jnp.where(lane == 0, xr, jnp.where(lane == 1, pltpu.roll(yr, 1, 1), 0.0)),
        ),
    )
    rows = turned(edge)
    ends_l = quadratic(lc, lx0, ly0, rows[127:128], rows[126:127])
    ends_r = quadratic(rc, rx0, ry0, rows[0:1], rows[1:2])
    columns = turned(
        jnp.concatenate([ends_l[0], ends_l[1], ends_r[0], ends_r[1], jnp.zeros((4, CY), F32)], axis=0)
    )[0:TALL]
    lines = []
    for (x0, y0), lines_ref, near, at in (
        (starts[0], top_ref, 7, 7),
        (starts[1], bottom_ref, 0, 8 + CX),
    ):
        ends = quadratic(
            lines_ref[24:48, :], x0, y0, x[at : at + 1, OWN], y[at : at + 1, OWN]
        )
        lines.append([jnp.where(line == near, ends[k], zero_line) for k in range(2)])
    sources = []
    for k in range(2):
        before = jnp.where(lane == 127, pltpu.roll(columns, 127 - k, 1), 0.0)
        after = jnp.where(lane == 0, pltpu.roll(columns, 126 - k, 1), 0.0)
        sources.append(assembled(lines[0][k], own(acc, k), lines[1][k], before, after))
    x, y, z = advance(x, y, zs[...], *sources)
    xs[...] = x
    ys[...] = y
    zs[...] = z
    prime()

    def third(t):
        def make():
            return rows_of(stored_product(table_ref, state, t))

        updated = tile_step(t, cells_ref, fld[...], make, acc)
        buf[tile_rows(t), :] = updated.T
        write(t).start()

    sweep(0, count, third)
    blank = jnp.zeros((TALL, 128), F32)
    sources = [assembled(zero_line, own(acc, k), zero_line, blank, blank) for k in range(2)]
    x, y, z = advance(xs[...], ys[...], zs[...], *sources)
    out_x[...] = x[8 : 8 + CX, OWN]
    out_y[...] = y[8 : 8 + CX, OWN]
    out_z[...] = z[8 : 8 + CX, OWN]
    sweep(0, total, lambda t: write(t).wait())


VMEM = pl.BlockSpec(memory_space=pltpu.VMEM)
SMEM = pl.BlockSpec(memory_space=pltpu.SMEM)
ANY = pl.BlockSpec(memory_space=pl.ANY)
LIMITS = pltpu.CompilerParams(vmem_limit_bytes=40 << 20)


def shaped(shape, dtype=F32):
    return jax.ShapeDtypeStruct(shape, dtype)


def ring(axis, step):
    count = lax.axis_size(axis)
    return [(i, (i + step) % count) for i in range(count)]


def pinned(value):
    return pltpu.with_memory_space_constraint(value, pltpu.VMEM)


def streamed(value):
    return pltpu.with_memory_space_constraint(value, pltpu.HBM)


def held(shape, dtype=F32):
    return pltpu.VMEM(shape, dtype)


def shards(density, cell_index, live_batches, propagator, dipoles, ex, ey, mz):
    slots = density.shape[0]
    tiles = slots // TILE
    cells = cell_index.reshape(slots // 128, 128)
    buffer = pltpu.VMEM((slots, S2), F32)
    sems = pltpu.SemaphoreType.DMA((tiles,))
    sums = (4 * CX, CY)
    halved = pltpu.VMEM((4 * CX, CY), BF16)
    half = held((slots, S2), BF16)
    readout, low, high, west, east, hi, lo = pl.pallas_call(
        coefficient_kernel,
        out_shape=(
            shaped((8, S2)),
            shaped((LINES, CY)),
            shaped((LINES, CY)),
            shaped((32, CX)),
            shaped((32, CX)),
            half,
            half,
        ),
        in_specs=[SMEM] + [ANY] * 7,
        out_specs=(VMEM,) * 7,
        scratch_shapes=[
            buffer,
            pltpu.VMEM((128, CY), F32),
            pltpu.VMEM((128, CX), F32),
            pltpu.VMEM(propagator.shape, F32),
            pltpu.VMEM(dipoles.shape, F32),
            pltpu.VMEM(cells.shape, jnp.int32),
            pltpu.SemaphoreType.DMA((slots // SMALL,)),
            pltpu.SemaphoreType.DMA((9,)),
        ],
        compiler_params=LIMITS,
        name="coefficients",
    )(
        live_batches,
        *(streamed(value) for value in (cells, ex, ey, mz, propagator, dipoles, density)),
    )
    bottom = lax.ppermute(low, "gx", ring("gx", -1))
    top = lax.ppermute(high, "gx", ring("gx", 1))
    table = pl.pallas_call(
        table_kernel,
        out_shape=held((ROWS, 3 * S2), BF16),
        in_specs=[VMEM] * 2,
        out_specs=VMEM,
        compiler_params=LIMITS,
        name="table",
    )(propagator, readout)
    state, source = pl.pallas_call(
        first_kernel,
        out_shape=(held((2 * S2, slots), BF16), held(sums)),
        in_specs=[SMEM] + [VMEM] * 6,
        out_specs=(VMEM,) * 2,
        scratch_shapes=[halved],
        compiler_params=LIMITS,
        name="first",
    )(live_batches, cells, ex, ey, pinned(table), pinned(hi), pinned(lo))
    package = held((LINES, CY))
    to_left, to_right = pl.pallas_call(
        corner_kernel,
        out_shape=(package, package),
        in_specs=[VMEM] * 5 + [VMEM] * 2 + [ANY],
        out_specs=(VMEM,) * 2,
        compiler_params=LIMITS,
        name="corners",
    )(ex, ey, mz, west, east, pinned(top), pinned(bottom), pinned(source))
    right = lax.ppermute(to_left, "gy", ring("gy", -1))
    left = lax.ppermute(to_right, "gy", ring("gy", 1))
    product = pl.pallas_call(
        ahead_kernel,
        out_shape=held((ROWS, slots)),
        in_specs=[SMEM] + [VMEM] * 2 + [ANY],
        out_specs=VMEM,
        compiler_params=LIMITS,
        name="ahead",
    )(live_batches, pinned(table), pinned(state), pinned(to_left))
    field = shaped((CX, CY))
    tall = pltpu.VMEM((TALL, WIDE), F32)
    return pl.pallas_call(
        main_kernel,
        out_shape=(shaped((slots, S2)), field, field, field),
        in_specs=[SMEM] + [VMEM] * 11 + [ANY],
        out_specs=(ANY,) + (VMEM,) * 3,
        scratch_shapes=[
            pltpu.VMEM((2 * S2, slots), BF16), buffer, pltpu.VMEM(sums, F32), halved,
            tall, tall, tall, sems,
        ],
        compiler_params=LIMITS,
        name="main",
    )(
        live_batches, cells, ex, ey, mz, pinned(source), pinned(table), pinned(product),
        pinned(top), pinned(bottom), pinned(left), pinned(right), streamed(density),
    )


def solution(mesh):
    placed = (
        P(("gx", "gy"), None),
        P(("gx", "gy")),
        P(("gx", "gy")),
        P(),
        P(),
        P("gx", "gy"),
        P("gx", "gy"),
        P("gx", "gy"),
    )
    return jax.shard_map(
        shards,
        mesh=mesh,
        in_specs=placed,
        out_specs=(P(("gx", "gy"), None), P("gx", "gy"), P("gx", "gy"), P("gx", "gy")),
        check_vma=False,
    )
```

```python
import jax
import jax.numpy as jnp
from jax import lax
from jax.experimental import pallas as pl
from jax.experimental.pallas import tpu as pltpu
from jax.sharding import PartitionSpec as P

BATCH = 64
STEPS = 3
TILE = 1024
SMALL = 512
COURANT = 0.5
CX = 128
CY = 256
S2 = 256
ROWS = 3 * S2 + 16
FIRST = 6
ORDERS = 24
LINES = 56
TALL = CX + 16
WIDE = CY + 256
F32 = jnp.float32
BF16 = jnp.bfloat16
NT = (((1,), (1,)), ((), ()))


def halves(x):
    hi = x.astype(BF16)
    return hi, (x - hi.astype(F32)).astype(BF16)


def fast_nt(a, b):
    return lax.dot_general(a, b, NT, preferred_element_type=F32)


def functionals_of(prop_ref, dip_ref):
    blocks = [halves(prop_ref[:, b * S2 : (b + 1) * S2]) for b in range(3)]

    def through(value, block):
        rows = value.shape[0]
        vh, vl = halves(value)
        wide = fast_nt(jnp.concatenate([vh, vl], axis=0), block[0])
        return wide[0:rows] + wide[rows:] + fast_nt(vh, block[1])

    dipoles = dip_ref[...]
    padded = jnp.concatenate([dipoles, jnp.zeros((6, S2), F32)], axis=0)
    reads = [through(padded, block)[0:2] for block in blocks]
    first = jnp.concatenate(
        [reads[0] - dipoles, reads[1], reads[2], jnp.zeros((2, S2), F32)], axis=0
    )
    second = [through(first, block)[0:FIRST] for block in blocks]
    return jnp.concatenate([first[0:FIRST], *second, jnp.zeros((8, S2), F32)], axis=0)


def table_kernel(prop_ref, readout_ref, table_ref):
    def put(rows, value):
        hi, lo = halves(value)
        table_ref[rows, 0:S2] = hi
        table_ref[rows, S2 : 2 * S2] = hi
        table_ref[rows, 2 * S2 :] = lo

    put(pl.ds(0, 16), jnp.concatenate([readout_ref[...], jnp.zeros((8, S2), F32)], axis=0))
    for b in range(3):
        block = prop_ref[:, b * S2 : (b + 1) * S2].T
        for q in range(S2 // 16):
            put(pl.ds(16 + 48 * q + 16 * b, 16), block[16 * q : 16 * q + 16])


def even(axis):
    return lax.axis_index(axis) % 2 == 0


def cells_of(cells_ref, t, size=TILE):
    cell = jnp.concatenate(
        [cells_ref[pl.ds(t * (size // 128) + j, 1), :] for j in range(size // 128)], axis=1
    )
    return cell >> 8, cell & (CY - 1)


def matches(index, size):
    return lax.broadcasted_iota(jnp.int32, (size, index.shape[1]), 0) == index


def one_hot(index, size):
    return jnp.where(matches(index, size), 1.0, 0.0).astype(BF16)


def count_of(live_ref, size=TILE):
    return live_ref[0] * BATCH // size


def tile_rows(t, size=TILE):
    return pl.ds(pl.multiple_of(t * size, size), size)


def sweep(lower, upper, body):
    def wrapped(t, carry):
        body(t)
        return carry

    lax.fori_loop(lower, upper, wrapped, 0)


def coefficient_kernel(
    live_ref, cells_hbm, ex_hbm, ey_hbm, mz_hbm, prop_hbm, dip_hbm, dens_hbm,
    readout_ref, one_ref, two_ref, west_ref, east_ref, hi_ref, lo_ref,
    buf, by_row, by_col, prop_ref, dip_ref, cells_ref, sems, loads,
):
    count = count_of(live_ref, SMALL)

    def copy(t):
        return pltpu.make_async_copy(dens_hbm.at[tile_rows(t, SMALL), :], buf.at[tile_rows(t, SMALL), :], sems.at[t])

    pairs = [(dip_hbm, dip_ref), (prop_hbm, prop_ref), (cells_hbm, cells_ref)]
    is_even = even("gx")
    starts = (jnp.where(is_even, CX - 8, 0), jnp.where(is_even, 0, CX - 8))
    for ref, start in zip((one_ref, two_ref), starts):
        start = pl.multiple_of(start, 8)
        for k, field in enumerate((mz_hbm, ex_hbm, ey_hbm)):
            pairs.append((field.at[pl.ds(start, 8), :], ref.at[pl.ds(8 * k, 8), :]))
    moves = [pltpu.make_async_copy(src, dst, loads.at[k]) for k, (src, dst) in enumerate(pairs)]
    for move in moves[:3]:
        move.start()
    sweep(0, count, lambda t: copy(t).start())
    for move in moves[3:]:
        move.start()
    for move in moves[:2]:
        move.wait()
    functionals = functionals_of(prop_ref, dip_ref)
    readout_ref[...] = functionals[0:8]
    fh, fl = halves(functionals)
    stacked = jnp.concatenate([fh, fl], axis=0)
    by_row[...] = jnp.zeros_like(by_row)
    by_col[...] = jnp.zeros_like(by_col)

    def picked(index, near, far, parts):
        out = []
        for place, rows in ((near[0], ORDERS), (near[1], ORDERS), (far[0], 8), (far[1], 8)):
            for part in parts:
                out.append(jnp.where(index == place, part[0:rows], 0.0))
        return jnp.concatenate(out, axis=0).astype(BF16)

    def body(t):
        copy(t).wait()
        dh, dl = halves(buf[tile_rows(t, SMALL), :])
        hi_ref[tile_rows(t, SMALL), :] = dh
        lo_ref[tile_rows(t, SMALL), :] = dl
        wide = fast_nt(stacked, dh)
        values = wide[0:32] + wide[32:64] + fast_nt(fh, dl)
        vh, vl = halves(values)
        parts = (vh.astype(F32), vl.astype(F32))
        row, col = cells_of(cells_ref, t, SMALL)
        by_row[...] += fast_nt(picked(row, (0, CX - 1), (1, CX - 2), parts), one_hot(col, CY))
        by_col[...] += fast_nt(picked(col, (0, CY - 1), (1, CY - 2), parts), one_hot(row, CX))

    for move in moves[2:]:
        move.wait()
    sweep(0, count, body)

    def side(ref, which):
        near = 2 * ORDERS * which
        far = 4 * ORDERS + 16 * which
        return (
            ref[near : near + ORDERS] + ref[near + ORDERS : near + 2 * ORDERS],
            ref[far : far + 8] + ref[far + 8 : far + 16],
        )

    low, high = side(by_row, 0), side(by_row, 1)
    for ref, if_even, if_odd in ((one_ref, high, low), (two_ref, low, high)):
        ref[24:48] = jnp.where(is_even, if_even[0], if_odd[0])
        ref[48:56] = jnp.where(is_even, if_even[1], if_odd[1])
    for which, ref in ((0, west_ref), (1, east_ref)):
        near, far = side(by_col, which)
        ref[0:ORDERS] = near
        ref[ORDERS:] = far


def tile_step(t, cells_ref, fields, make, source_ref):
    row, col = cells_of(cells_ref, t)
    hot_col = one_hot(col, CY)
    mask = matches(row, CX)
    lines = jnp.dot(fields, hot_col, preferred_element_type=F32)
    sample_x = jnp.sum(
        jnp.where(mask, lines[0:CX] + lines[CX : 2 * CX], 0.0), axis=0, keepdims=True
    )
    sample_y = jnp.sum(
        jnp.where(mask, lines[2 * CX : 3 * CX] + lines[3 * CX :], 0.0), axis=0, keepdims=True
    )
    product = make()
    reads = product(0, 8)
    current_x = reads[0:1] + sample_x * reads[2:3] + sample_y * reads[4:5]
    current_y = reads[1:2] + sample_x * reads[3:4] + sample_y * reads[5:6]
    parts = []
    for current in (current_x, current_y):
        for part in halves(current):
            parts.append(jnp.where(mask, part.astype(F32), 0.0).astype(BF16))
    source_ref[...] += fast_nt(jnp.concatenate(parts, axis=0), hot_col)
    groups = []
    for q in range(S2 // 16):
        base = 16 + 48 * q
        groups.append(
            product(base, 16)
            + sample_x * product(base + 16, 16)
            + sample_y * product(base + 32, 16)
        )
    return jnp.concatenate(groups, axis=0)


def split_fields(ex, ey):
    xh, xl = halves(ex)
    yh, yl = halves(ey)
    return jnp.concatenate([xh, xl, yh, yl], axis=0)


def save_state(state_ref, t, updated):
    hi, lo = halves(updated)
    state_ref[0:S2, tile_rows(t)] = hi
    state_ref[S2:, tile_rows(t)] = lo


def rows_of(value):
    return lambda start, size: value[start : start + size]


def stored_product(table_ref, state_ref, t):
    hi, lo = state_ref[0:S2, tile_rows(t)], state_ref[S2:, tile_rows(t)]
    return jnp.dot(
        table_ref[...], jnp.concatenate([hi, lo, hi], axis=0), preferred_element_type=F32
    )


def first_kernel(
    live_ref, cells_ref, ex_ref, ey_ref, table_ref, hi_ref, lo_ref, state_ref, acc, fld
):
    fld[...] = split_fields(ex_ref[...], ey_ref[...])
    acc[...] = jnp.zeros_like(acc)

    def body(t):
        hi, lo = hi_ref[tile_rows(t), :], lo_ref[tile_rows(t), :]

        def make():
            return rows_of(fast_nt(table_ref[...], jnp.concatenate([hi, lo, hi], axis=1)))

        save_state(state_ref, t, tile_step(t, cells_ref, fld[...], make, acc))

    sweep(0, count_of(live_ref), body)


def ahead_kernel(live_ref, table_ref, state_ref, after_ref, product_ref):
    def body(t):
        product_ref[:, tile_rows(t)] = stored_product(table_ref, state_ref, t)

    sweep(0, count_of(live_ref), body)


def turned(value):
    rows, lanes = value.shape
    if rows < 128:
        value = jnp.concatenate([value, jnp.zeros((128 - rows, lanes), F32)], axis=0)
    elif rows < 256:
        value = jnp.concatenate([value, jnp.zeros((256 - rows, lanes), F32)], axis=0)
    return value.T


def ordered(axis, one_ref, two_ref):
    is_even = even(axis)
    one, two = one_ref[...], two_ref[...]
    return jnp.where(is_even, two, one), jnp.where(is_even, one, two)


def corner_kernel(
    ex_ref, ey_ref, mz_ref, west_ref, east_ref, one_ref, two_ref, after_ref, to_one_ref, to_two_ref
):
    tops, bottoms = ordered("gx", one_ref, two_ref)
    packages = []
    lane = lax.broadcasted_iota(jnp.int32, (TALL, 128), 1)
    for side, coefs_ref in ((0, west_ref), (1, east_ref)):
        half = slice(128 * side, 128 * side + 128)

        def tall(k, field_ref):
            rows = slice(8 * k, 8 * k + 8)
            return jnp.concatenate([tops[rows, half], field_ref[:, half], bottoms[rows, half]], axis=0)

        shift = 8 * side
        m = tall(0, mz_ref)
        if shift:
            m = pltpu.roll(m, shift, 1)
        x = pltpu.roll(tall(1, ex_ref), 8 + shift, 1)
        y = pltpu.roll(tall(2, ey_ref), 16 + shift, 1)
        items = jnp.where(lane < 8, m, jnp.where(lane < 16, x, y))
        coefs = coefs_ref[...]
        wide = pltpu.roll(jnp.concatenate([coefs, jnp.zeros_like(coefs)], axis=1), 8, 1)
        lower = wide[:, 0:128]
        upper = wide[:, 128:256]
        place = lax.broadcasted_iota(jnp.int32, (32, 128), 1)
        gap = jnp.zeros((16, 128), F32)

        def both(lines, near_from, far_from, near_to, far_to, base):
            near = lines[24:48, half]
            far = lines[48:56, half]
            at_near = jnp.concatenate(
                [
                    pltpu.roll(near, (near_to - near_from) % 128, 1),
                    pltpu.roll(near[0:8], (near_to - far_from) % 128, 1),
                ],
                axis=0,
            )
            at_far = jnp.concatenate(
                [
                    pltpu.roll(far, (far_to - near_from) % 128, 1),
                    gap,
                    pltpu.roll(far, (far_to - far_from) % 128, 1),
                ],
                axis=0,
            )
            return jnp.where(place == near_to, at_near, jnp.where(place == far_to, at_far, base))

        near_from, far_from = (127, 126) if side else (0, 1)
        spread = jnp.concatenate(
            [
                both(tops, near_from, far_from, 7, 6, lower),
                both(bottoms, near_from, far_from, 8, 9, upper),
            ],
            axis=1,
        )
        packages.append(jnp.concatenate([turned(items)[0:24], spread], axis=0))
    left, right = packages
    is_even = even("gy")
    to_one_ref[...] = jnp.where(is_even, right, left)
    to_two_ref[...] = jnp.where(is_even, left, right)


def linear(coefs, x, y):
    return (
        coefs[0:1] + x * coefs[2:3] + y * coefs[4:5],
        coefs[1:2] + x * coefs[3:4] + y * coefs[5:6],
    )


def quadratic(coefs, x0, y0, x1, y1):
    terms = [linear(coefs[FIRST * (c + 1) : FIRST * (c + 2)], x1, y1) for c in range(3)]
    return tuple(terms[0][k] + x0 * terms[1][k] + y0 * terms[2][k] for k in range(2))


def advance(x, y, z, source_x, source_y):
    y_next = pltpu.roll(y, TALL - 1, 0)
    x_next = pltpu.roll(x, WIDE - 1, 1)
    z = z - COURANT * ((y_next - y) - (x_next - x))
    x = x + COURANT * (z - pltpu.roll(z, 1, 1)) - source_x
    y = y - COURANT * (z - pltpu.roll(z, 1, 0)) - source_y
    return x, y, z


OWN = slice(128, 128 + CY)


def main_kernel(
    live_ref, cells_ref, ex_ref, ey_ref, mz_ref, acc_ref, table_ref, product_ref,
    row_one_ref, row_two_ref, col_one_ref, col_two_ref, dens_ref,
    evolved_ref, out_x, out_y, out_z, state, buf, acc, fld, xs, ys, zs, sems,
):
    count = count_of(live_ref)
    total = dens_ref.shape[0] // TILE

    def fetch(t):
        return pltpu.make_async_copy(dens_ref.at[tile_rows(t), :], buf.at[tile_rows(t), :], sems.at[t])

    def write(t):
        return pltpu.make_async_copy(buf.at[tile_rows(t), :], evolved_ref.at[tile_rows(t), :], sems.at[t])

    sweep(count, total, lambda t: fetch(t).start())

    tops, bottoms = ordered("gx", row_one_ref, row_two_ref)
    left, right = ordered("gy", col_one_ref, col_two_ref)
    left_items = turned(left[0:24])[0:TALL]
    right_items = turned(right[0:24])[0:TALL]

    def extended(k, field_ref):
        rows = slice(8 * k, 8 * k + 8)
        middle = jnp.concatenate([tops[rows, :], field_ref[...], bottoms[rows, :]], axis=0)
        before = pltpu.roll(left_items, 120 - 8 * k, 1)
        after = right_items
        if k:
            after = pltpu.roll(after, 128 - 8 * k, 1)
        return jnp.concatenate([before, middle, after], axis=1)

    zs[...] = extended(0, mz_ref)
    xs[...] = extended(1, ex_ref)
    ys[...] = extended(2, ey_ref)

    sides = []
    for package, near, far in ((left, 7, 6), (right, 0, 1)):
        lines = package[0:24]
        coefs = package[24:]
        near_x, near_y = lines[8 + near : 9 + near], lines[16 + near : 17 + near]
        far_x, far_y = lines[8 + far : 9 + far], lines[16 + far : 17 + far]
        sides.append(
            (
                coefs,
                near_x,
                near_y,
                linear(coefs[0:FIRST], near_x, near_y),
                linear(coefs[ORDERS : ORDERS + FIRST], far_x, far_y),
            )
        )
    lane = lax.broadcasted_iota(jnp.int32, (TALL, 128), 1)
    line = lax.broadcasted_iota(jnp.int32, (8, CY), 0)

    def assembled(tops, rows, bottoms, before, after):
        middle = jnp.concatenate([tops, rows, bottoms], axis=0)
        return jnp.concatenate([before, middle, after], axis=1)

    (lc, lx0, ly0, lnear, lfar), (rc, rx0, ry0, rnear, rfar) = sides
    columns = turned(
        jnp.concatenate(
            [lfar[0], lnear[0], lfar[1], lnear[1], rnear[0], rfar[0], rnear[1], rfar[1]], axis=0
        )
    )[0:TALL]
    zero_line = jnp.zeros((8, CY), F32)
    starts = []
    top_lines = []
    bottom_lines = []
    for lines_of, near, far, out in (
        (tops, 7, 6, top_lines),
        (bottoms, 0, 1, bottom_lines),
    ):
        near_x, near_y = lines_of[8 + near : 9 + near, :], lines_of[16 + near : 17 + near, :]
        far_x, far_y = lines_of[8 + far : 9 + far, :], lines_of[16 + far : 17 + far, :]
        starts.append((near_x, near_y))
        at_near = linear(lines_of[24 : 24 + FIRST, :], near_x, near_y)
        at_far = linear(lines_of[48 : 48 + FIRST, :], far_x, far_y)
        for k in range(2):
            out.append(
                jnp.where(line == near, at_near[k], jnp.where(line == far, at_far[k], zero_line))
            )

    def own(ref, k):
        return ref[2 * k * CX : (2 * k + 1) * CX] + ref[(2 * k + 1) * CX : (2 * k + 2) * CX]

    sources = []
    for k in range(2):
        before = jnp.where(lane >= 126, pltpu.roll(columns, 126 - 2 * k, 1), 0.0)
        after = jnp.where(lane < 2, pltpu.roll(columns, 124 - 2 * k, 1), 0.0)
        sources.append(assembled(top_lines[k], own(acc_ref, k), bottom_lines[k], before, after))
    x, y, z = advance(xs[...], ys[...], zs[...], *sources)
    xs[...] = x
    ys[...] = y
    zs[...] = z

    def flush(t):
        fetch(t).wait()
        write(t).start()

    sweep(count, total, flush)

    def prime():
        fld[...] = split_fields(xs[8 : 8 + CX, OWN], ys[8 : 8 + CX, OWN])
        acc[...] = jnp.zeros_like(acc)

    prime()

    def second(t):
        def make():
            return lambda start, size: product_ref[start : start + size, tile_rows(t)]

        save_state(state, t, tile_step(t, cells_ref, fld[...], make, acc))

    sweep(0, count, second)

    x = xs[...]
    y = ys[...]
    xl, yl = x[:, 0:128], y[:, 0:128]
    xr, yr = x[:, 384:512], y[:, 384:512]
    edge = jnp.where(
        lane == 127,
        xl,
        jnp.where(
            lane == 126,
            pltpu.roll(yl, 127, 1),
            jnp.where(lane == 0, xr, jnp.where(lane == 1, pltpu.roll(yr, 1, 1), 0.0)),
        ),
    )
    rows = turned(edge)
    ends_l = quadratic(lc, lx0, ly0, rows[127:128], rows[126:127])
    ends_r = quadratic(rc, rx0, ry0, rows[0:1], rows[1:2])
    columns = turned(
        jnp.concatenate([ends_l[0], ends_l[1], ends_r[0], ends_r[1], jnp.zeros((4, CY), F32)], axis=0)
    )[0:TALL]
    lines = []
    for (x0, y0), lines_of, near, at in (
        (starts[0], tops, 7, 7),
        (starts[1], bottoms, 0, 8 + CX),
    ):
        ends = quadratic(
            lines_of[24:48, :], x0, y0, x[at : at + 1, OWN], y[at : at + 1, OWN]
        )
        lines.append([jnp.where(line == near, ends[k], zero_line) for k in range(2)])
    sources = []
    for k in range(2):
        before = jnp.where(lane == 127, pltpu.roll(columns, 127 - k, 1), 0.0)
        after = jnp.where(lane == 0, pltpu.roll(columns, 126 - k, 1), 0.0)
        sources.append(assembled(lines[0][k], own(acc, k), lines[1][k], before, after))
    x, y, z = advance(x, y, zs[...], *sources)
    xs[...] = x
    ys[...] = y
    zs[...] = z
    prime()

    def third(t):
        def make():
            return rows_of(stored_product(table_ref, state, t))

        updated = tile_step(t, cells_ref, fld[...], make, acc)
        buf[tile_rows(t), :] = updated.T
        write(t).start()

    sweep(0, count, third)
    blank = jnp.zeros((TALL, 128), F32)
    sources = [assembled(zero_line, own(acc, k), zero_line, blank, blank) for k in range(2)]
    x, y, z = advance(xs[...], ys[...], zs[...], *sources)
    out_x[...] = x[8 : 8 + CX, OWN]
    out_y[...] = y[8 : 8 + CX, OWN]
    out_z[...] = z[8 : 8 + CX, OWN]
    sweep(0, total, lambda t: write(t).wait())


VMEM = pl.BlockSpec(memory_space=pltpu.VMEM)
SMEM = pl.BlockSpec(memory_space=pltpu.SMEM)
ANY = pl.BlockSpec(memory_space=pl.ANY)
LIMITS = pltpu.CompilerParams(vmem_limit_bytes=40 << 20)


def shaped(shape, dtype=F32):
    return jax.ShapeDtypeStruct(shape, dtype)


def pairs(axis, first):
    count = lax.axis_size(axis)
    swaps = [(i % count, (i + 1) % count) for i in range(first, first + count, 2)]
    return swaps + [(b, a) for a, b in swaps]


def pinned(value):
    return pltpu.with_memory_space_constraint(value, pltpu.VMEM)


def streamed(value):
    return pltpu.with_memory_space_constraint(value, pltpu.HBM)


def held(shape, dtype=F32):
    return pltpu.VMEM(shape, dtype)


def shards(density, cell_index, live_batches, propagator, dipoles, ex, ey, mz):
    slots = density.shape[0]
    tiles = slots // TILE
    cells = cell_index.reshape(slots // 128, 128)
    buffer = pltpu.VMEM((slots, S2), F32)
    sems = pltpu.SemaphoreType.DMA((tiles,))
    sums = (4 * CX, CY)
    halved = pltpu.VMEM((4 * CX, CY), BF16)
    half = held((slots, S2), BF16)
    readout, one, two, west, east, hi, lo = pl.pallas_call(
        coefficient_kernel,
        out_shape=(
            shaped((8, S2)),
            shaped((LINES, CY)),
            shaped((LINES, CY)),
            shaped((32, CX)),
            shaped((32, CX)),
            half,
            half,
        ),
        in_specs=[SMEM] + [ANY] * 7,
        out_specs=(VMEM,) * 7,
        scratch_shapes=[
            buffer,
            pltpu.VMEM((128, CY), F32),
            pltpu.VMEM((128, CX), F32),
            pltpu.VMEM(propagator.shape, F32),
            pltpu.VMEM(dipoles.shape, F32),
            pltpu.VMEM(cells.shape, jnp.int32),
            pltpu.SemaphoreType.DMA((slots // SMALL,)),
            pltpu.SemaphoreType.DMA((9,)),
        ],
        compiler_params=LIMITS,
        name="coefficients",
    )(
        live_batches,
        *(streamed(value) for value in (cells, ex, ey, mz, propagator, dipoles, density)),
    )
    row_one = lax.ppermute(one, "gx", pairs("gx", 0))
    row_two = lax.ppermute(two, "gx", pairs("gx", 1))
    table = pl.pallas_call(
        table_kernel,
        out_shape=held((ROWS, 3 * S2), BF16),
        in_specs=[VMEM] * 2,
        out_specs=VMEM,
        compiler_params=LIMITS,
        name="table",
    )(propagator, readout)
    state, source = pl.pallas_call(
        first_kernel,
        out_shape=(held((2 * S2, slots), BF16), held(sums)),
        in_specs=[SMEM] + [VMEM] * 6,
        out_specs=(VMEM,) * 2,
        scratch_shapes=[halved],
        compiler_params=LIMITS,
        name="first",
    )(live_batches, cells, ex, ey, pinned(table), pinned(hi), pinned(lo))
    package = held((LINES, CY))
    to_one, to_two = pl.pallas_call(
        corner_kernel,
        out_shape=(package, package),
        in_specs=[VMEM] * 5 + [VMEM] * 2 + [ANY],
        out_specs=(VMEM,) * 2,
        compiler_params=LIMITS,
        name="corners",
    )(ex, ey, mz, west, east, pinned(row_one), pinned(row_two), pinned(source))
    col_one = lax.ppermute(to_one, "gy", pairs("gy", 0))
    col_two = lax.ppermute(to_two, "gy", pairs("gy", 1))
    product = pl.pallas_call(
        ahead_kernel,
        out_shape=held((ROWS, slots)),
        in_specs=[SMEM] + [VMEM] * 2 + [ANY],
        out_specs=VMEM,
        compiler_params=LIMITS,
        name="ahead",
    )(live_batches, pinned(table), pinned(state), pinned(to_one))
    field = shaped((CX, CY))
    tall = pltpu.VMEM((TALL, WIDE), F32)
    return pl.pallas_call(
        main_kernel,
        out_shape=(shaped((slots, S2)), field, field, field),
        in_specs=[SMEM] + [VMEM] * 11 + [ANY],
        out_specs=(ANY,) + (VMEM,) * 3,
        scratch_shapes=[
            pltpu.VMEM((2 * S2, slots), BF16), buffer, pltpu.VMEM(sums, F32), halved,
            tall, tall, tall, sems,
        ],
        compiler_params=LIMITS,
        name="main",
    )(
        live_batches, cells, ex, ey, mz, pinned(source), pinned(table), pinned(product),
        pinned(row_one), pinned(row_two), pinned(col_one), pinned(col_two), streamed(density),
    )


def solution(mesh):
    placed = (
        P(("gx", "gy"), None),
        P(("gx", "gy")),
        P(("gx", "gy")),
        P(),
        P(),
        P("gx", "gy"),
        P("gx", "gy"),
        P("gx", "gy"),
    )
    return jax.shard_map(
        shards,
        mesh=mesh,
        in_specs=placed,
        out_specs=(P(("gx", "gy"), None), P("gx", "gy"), P("gx", "gy"), P("gx", "gy")),
        check_vma=False,
    )
```

```python
import jax
import jax.numpy as jnp
from jax import lax
from jax.experimental import pallas as pl
from jax.experimental.pallas import tpu as pltpu
from jax.sharding import PartitionSpec as P

BATCH = 64
STEPS = 3
TILE = 1024
SMALL = 512
COURANT = 0.5
CX = 128
CY = 256
S2 = 256
ROWS = 3 * S2 + 16
FIRST = 6
ORDERS = 24
LINES = 56
TALL = CX + 16
WIDE = CY + 256
F32 = jnp.float32
BF16 = jnp.bfloat16
NT = (((1,), (1,)), ((), ()))


def halves(x):
    hi = x.astype(BF16)
    return hi, (x - hi.astype(F32)).astype(BF16)


def fast_nt(a, b):
    return lax.dot_general(a, b, NT, preferred_element_type=F32)


def functionals_of(prop_ref, dip_ref):
    blocks = [halves(prop_ref[:, b * S2 : (b + 1) * S2]) for b in range(3)]

    def through(value, block):
        rows = value.shape[0]
        vh, vl = halves(value)
        wide = fast_nt(jnp.concatenate([vh, vl], axis=0), block[0])
        return wide[0:rows] + wide[rows:] + fast_nt(vh, block[1])

    dipoles = dip_ref[...]
    padded = jnp.concatenate([dipoles, jnp.zeros((6, S2), F32)], axis=0)
    reads = [through(padded, block)[0:2] for block in blocks]
    first = jnp.concatenate(
        [reads[0] - dipoles, reads[1], reads[2], jnp.zeros((2, S2), F32)], axis=0
    )
    second = [through(first, block)[0:FIRST] for block in blocks]
    return jnp.concatenate([first[0:FIRST], *second, jnp.zeros((8, S2), F32)], axis=0)


def table_kernel(prop_ref, readout_ref, table_ref):
    def put(rows, value):
        hi, lo = halves(value)
        table_ref[rows, 0:S2] = hi
        table_ref[rows, S2 : 2 * S2] = hi
        table_ref[rows, 2 * S2 :] = lo

    put(pl.ds(0, 16), jnp.concatenate([readout_ref[...], jnp.zeros((8, S2), F32)], axis=0))
    for b in range(3):
        block = prop_ref[:, b * S2 : (b + 1) * S2].T
        for q in range(S2 // 16):
            put(pl.ds(16 + 48 * q + 16 * b, 16), block[16 * q : 16 * q + 16])


def even(axis):
    return lax.axis_index(axis) % 2 == 0


def cells_of(cells_ref, t, size=TILE):
    cell = jnp.concatenate(
        [cells_ref[pl.ds(t * (size // 128) + j, 1), :] for j in range(size // 128)], axis=1
    )
    return cell >> 8, cell & (CY - 1)


def matches(index, size):
    return lax.broadcasted_iota(jnp.int32, (size, index.shape[1]), 0) == index


def one_hot(index, size):
    return jnp.where(matches(index, size), 1.0, 0.0).astype(BF16)


def count_of(live_ref, size=TILE):
    return live_ref[0] * BATCH // size


def tile_rows(t, size=TILE):
    return pl.ds(pl.multiple_of(t * size, size), size)


def sweep(lower, upper, body):
    def wrapped(t, carry):
        body(t)
        return carry

    lax.fori_loop(lower, upper, wrapped, 0)


def coefficient_kernel(
    live_ref, cells_hbm, ex_hbm, ey_hbm, mz_hbm, prop_hbm, dip_hbm, dens_hbm,
    readout_ref, one_ref, two_ref, west_ref, east_ref, hi_ref, lo_ref,
    buf, by_row, by_col, prop_ref, dip_ref, cells_ref, sems, loads,
):
    count = count_of(live_ref, SMALL)

    def copy(t):
        return pltpu.make_async_copy(dens_hbm.at[tile_rows(t, SMALL), :], buf.at[tile_rows(t, SMALL), :], sems.at[t])

    pairs = [(dip_hbm, dip_ref), (prop_hbm, prop_ref), (cells_hbm, cells_ref)]
    is_even = even("gx")
    starts = (jnp.where(is_even, CX - 8, 0), jnp.where(is_even, 0, CX - 8))
    for ref, start in zip((one_ref, two_ref), starts):
        start = pl.multiple_of(start, 8)
        for k, field in enumerate((mz_hbm, ex_hbm, ey_hbm)):
            pairs.append((field.at[pl.ds(start, 8), :], ref.at[pl.ds(8 * k, 8), :]))
    moves = [pltpu.make_async_copy(src, dst, loads.at[k]) for k, (src, dst) in enumerate(pairs)]
    for move in moves[:3]:
        move.start()
    sweep(0, count, lambda t: copy(t).start())
    for move in moves[3:]:
        move.start()
    for move in moves[:2]:
        move.wait()
    functionals = functionals_of(prop_ref, dip_ref)
    readout_ref[...] = functionals[0:8]
    fh, fl = halves(functionals)
    stacked = jnp.concatenate([fh, fl], axis=0)
    by_row[...] = jnp.zeros_like(by_row)
    by_col[...] = jnp.zeros_like(by_col)

    def picked(index, near, far, parts):
        out = []
        for place, rows in ((near[0], ORDERS), (near[1], ORDERS), (far[0], 8), (far[1], 8)):
            for part in parts:
                out.append(jnp.where(index == place, part[0:rows], 0.0))
        return jnp.concatenate(out, axis=0).astype(BF16)

    def body(t):
        copy(t).wait()
        dh, dl = halves(buf[tile_rows(t, SMALL), :])
        hi_ref[tile_rows(t, SMALL), :] = dh
        lo_ref[tile_rows(t, SMALL), :] = dl
        wide = fast_nt(stacked, dh)
        values = wide[0:32] + wide[32:64] + fast_nt(fh, dl)
        vh, vl = halves(values)
        parts = (vh.astype(F32), vl.astype(F32))
        row, col = cells_of(cells_ref, t, SMALL)
        by_row[...] += fast_nt(picked(row, (0, CX - 1), (1, CX - 2), parts), one_hot(col, CY))
        by_col[...] += fast_nt(picked(col, (0, CY - 1), (1, CY - 2), parts), one_hot(row, CX))

    for move in moves[2:]:
        move.wait()
    sweep(0, count, body)

    def side(ref, which):
        near = 2 * ORDERS * which
        far = 4 * ORDERS + 16 * which
        return (
            ref[near : near + ORDERS] + ref[near + ORDERS : near + 2 * ORDERS],
            ref[far : far + 8] + ref[far + 8 : far + 16],
        )

    low, high = side(by_row, 0), side(by_row, 1)
    for ref, if_even, if_odd in ((one_ref, high, low), (two_ref, low, high)):
        ref[24:48] = jnp.where(is_even, if_even[0], if_odd[0])
        ref[48:56] = jnp.where(is_even, if_even[1], if_odd[1])
    for which, ref in ((0, west_ref), (1, east_ref)):
        near, far = side(by_col, which)
        ref[0:ORDERS] = near
        ref[ORDERS:] = far


def tile_step(t, cells_ref, fields, make, source_ref):
    row, col = cells_of(cells_ref, t)
    hot_col = one_hot(col, CY)
    mask = matches(row, CX)
    lines = jnp.dot(fields, hot_col, preferred_element_type=F32)
    sample_x = jnp.sum(
        jnp.where(mask, lines[0:CX] + lines[CX : 2 * CX], 0.0), axis=0, keepdims=True
    )
    sample_y = jnp.sum(
        jnp.where(mask, lines[2 * CX : 3 * CX] + lines[3 * CX :], 0.0), axis=0, keepdims=True
    )
    product = make()
    reads = product(0, 8)
    current_x = reads[0:1] + sample_x * reads[2:3] + sample_y * reads[4:5]
    current_y = reads[1:2] + sample_x * reads[3:4] + sample_y * reads[5:6]
    parts = [part for current in (current_x, current_y) for part in halves(current)]
    groups = []
    for k, part in enumerate(parts):
        marked = jnp.where(mask, part.astype(F32), 0.0).astype(BF16)
        source_ref[k * CX : (k + 1) * CX] += fast_nt(marked, hot_col)
        for q in range(4 * k, 4 * k + 4):
            base = 16 + 48 * q
            groups.append(
                product(base, 16)
                + sample_x * product(base + 16, 16)
                + sample_y * product(base + 32, 16)
            )
    return jnp.concatenate(groups, axis=0)


def split_fields(ex, ey):
    xh, xl = halves(ex)
    yh, yl = halves(ey)
    return jnp.concatenate([xh, xl, yh, yl], axis=0)


def save_state(state_ref, t, updated):
    hi, lo = halves(updated.T)
    state_ref[tile_rows(t), 0:S2] = hi
    state_ref[tile_rows(t), S2:] = lo


def rows_of(value):
    return lambda start, size: value[start : start + size]


def stored_product(table_ref, state_ref, t):
    hi, lo = state_ref[tile_rows(t), 0:S2], state_ref[tile_rows(t), S2:]
    return fast_nt(table_ref[...], jnp.concatenate([hi, lo, hi], axis=1))


def first_kernel(
    live_ref, cells_ref, ex_ref, ey_ref, table_ref, hi_ref, lo_ref, state_ref, acc, fld
):
    fld[...] = split_fields(ex_ref[...], ey_ref[...])
    acc[...] = jnp.zeros_like(acc)

    def body(t):
        hi, lo = hi_ref[tile_rows(t), :], lo_ref[tile_rows(t), :]

        def make():
            return rows_of(fast_nt(table_ref[...], jnp.concatenate([hi, lo, hi], axis=1)))

        save_state(state_ref, t, tile_step(t, cells_ref, fld[...], make, acc))

    sweep(0, count_of(live_ref), body)


def ahead_kernel(live_ref, table_ref, state_ref, after_ref, product_ref):
    def body(t):
        product_ref[:, tile_rows(t)] = stored_product(table_ref, state_ref, t)

    sweep(0, count_of(live_ref), body)


def turned(value):
    rows, lanes = value.shape
    if rows < 128:
        value = jnp.concatenate([value, jnp.zeros((128 - rows, lanes), F32)], axis=0)
    elif rows < 256:
        value = jnp.concatenate([value, jnp.zeros((256 - rows, lanes), F32)], axis=0)
    return value.T


def ordered(axis, one_ref, two_ref):
    is_even = even(axis)
    one, two = one_ref[...], two_ref[...]
    return jnp.where(is_even, two, one), jnp.where(is_even, one, two)


def corner_kernel(
    ex_ref, ey_ref, mz_ref, west_ref, east_ref, one_ref, two_ref, after_ref, to_one_ref, to_two_ref
):
    tops, bottoms = ordered("gx", one_ref, two_ref)
    packages = []
    lane = lax.broadcasted_iota(jnp.int32, (TALL, 128), 1)
    for side, coefs_ref in ((0, west_ref), (1, east_ref)):
        half = slice(128 * side, 128 * side + 128)

        def tall(k, field_ref):
            rows = slice(8 * k, 8 * k + 8)
            return jnp.concatenate([tops[rows, half], field_ref[:, half], bottoms[rows, half]], axis=0)

        shift = 8 * side
        m = tall(0, mz_ref)
        if shift:
            m = pltpu.roll(m, shift, 1)
        x = pltpu.roll(tall(1, ex_ref), 8 + shift, 1)
        y = pltpu.roll(tall(2, ey_ref), 16 + shift, 1)
        items = jnp.where(lane < 8, m, jnp.where(lane < 16, x, y))
        coefs = coefs_ref[...]
        wide = pltpu.roll(jnp.concatenate([coefs, jnp.zeros_like(coefs)], axis=1), 8, 1)
        lower = wide[:, 0:128]
        upper = wide[:, 128:256]
        place = lax.broadcasted_iota(jnp.int32, (32, 128), 1)
        gap = jnp.zeros((16, 128), F32)

        def both(lines, near_from, far_from, near_to, far_to, base):
            near = lines[24:48, half]
            far = lines[48:56, half]
            at_near = jnp.concatenate(
                [
                    pltpu.roll(near, (near_to - near_from) % 128, 1),
                    pltpu.roll(near[0:8], (near_to - far_from) % 128, 1),
                ],
                axis=0,
            )
            at_far = jnp.concatenate(
                [
                    pltpu.roll(far, (far_to - near_from) % 128, 1),
                    gap,
                    pltpu.roll(far, (far_to - far_from) % 128, 1),
                ],
                axis=0,
            )
            return jnp.where(place == near_to, at_near, jnp.where(place == far_to, at_far, base))

        near_from, far_from = (127, 126) if side else (0, 1)
        spread = jnp.concatenate(
            [
                both(tops, near_from, far_from, 7, 6, lower),
                both(bottoms, near_from, far_from, 8, 9, upper),
            ],
            axis=1,
        )
        packages.append(jnp.concatenate([turned(items)[0:24], spread], axis=0))
    left, right = packages
    is_even = even("gy")
    to_one_ref[...] = jnp.where(is_even, right, left)
    to_two_ref[...] = jnp.where(is_even, left, right)


def linear(coefs, x, y):
    return (
        coefs[0:1] + x * coefs[2:3] + y * coefs[4:5],
        coefs[1:2] + x * coefs[3:4] + y * coefs[5:6],
    )


def quadratic(coefs, x0, y0, x1, y1):
    terms = [linear(coefs[FIRST * (c + 1) : FIRST * (c + 2)], x1, y1) for c in range(3)]
    return tuple(terms[0][k] + x0 * terms[1][k] + y0 * terms[2][k] for k in range(2))


def advance(x, y, z, source_x, source_y):
    y_next = pltpu.roll(y, TALL - 1, 0)
    x_next = pltpu.roll(x, WIDE - 1, 1)
    z = z - COURANT * ((y_next - y) - (x_next - x))
    x = x + COURANT * (z - pltpu.roll(z, 1, 1)) - source_x
    y = y - COURANT * (z - pltpu.roll(z, 1, 0)) - source_y
    return x, y, z


OWN = slice(128, 128 + CY)


def main_kernel(
    live_ref, cells_ref, ex_ref, ey_ref, mz_ref, acc_ref, table_ref, product_ref,
    row_one_ref, row_two_ref, col_one_ref, col_two_ref, dens_ref,
    evolved_ref, out_x, out_y, out_z, state, buf, acc, fld, xs, ys, zs, sems,
):
    count = count_of(live_ref)
    total = dens_ref.shape[0] // TILE

    def fetch(t):
        return pltpu.make_async_copy(dens_ref.at[tile_rows(t), :], buf.at[tile_rows(t), :], sems.at[t])

    def write(t):
        return pltpu.make_async_copy(buf.at[tile_rows(t), :], evolved_ref.at[tile_rows(t), :], sems.at[t])

    sweep(count, total, lambda t: fetch(t).start())

    tops, bottoms = ordered("gx", row_one_ref, row_two_ref)
    left, right = ordered("gy", col_one_ref, col_two_ref)
    left_items = turned(left[0:24])[0:TALL]
    right_items = turned(right[0:24])[0:TALL]

    def extended(k, field_ref):
        rows = slice(8 * k, 8 * k + 8)
        middle = jnp.concatenate([tops[rows, :], field_ref[...], bottoms[rows, :]], axis=0)
        before = pltpu.roll(left_items, 120 - 8 * k, 1)
        after = right_items
        if k:
            after = pltpu.roll(after, 128 - 8 * k, 1)
        return jnp.concatenate([before, middle, after], axis=1)

    zs[...] = extended(0, mz_ref)
    xs[...] = extended(1, ex_ref)
    ys[...] = extended(2, ey_ref)

    sides = []
    for package, near, far in ((left, 7, 6), (right, 0, 1)):
        lines = package[0:24]
        coefs = package[24:]
        near_x, near_y = lines[8 + near : 9 + near], lines[16 + near : 17 + near]
        far_x, far_y = lines[8 + far : 9 + far], lines[16 + far : 17 + far]
        sides.append(
            (
                coefs,
                near_x,
                near_y,
                linear(coefs[0:FIRST], near_x, near_y),
                linear(coefs[ORDERS : ORDERS + FIRST], far_x, far_y),
            )
        )
    lane = lax.broadcasted_iota(jnp.int32, (TALL, 128), 1)
    line = lax.broadcasted_iota(jnp.int32, (8, CY), 0)

    def assembled(tops, rows, bottoms, before, after):
        middle = jnp.concatenate([tops, rows, bottoms], axis=0)
        return jnp.concatenate([before, middle, after], axis=1)

    (lc, lx0, ly0, lnear, lfar), (rc, rx0, ry0, rnear, rfar) = sides
    columns = turned(
        jnp.concatenate(
            [lfar[0], lnear[0], lfar[1], lnear[1], rnear[0], rfar[0], rnear[1], rfar[1]], axis=0
        )
    )[0:TALL]
    zero_line = jnp.zeros((8, CY), F32)
    starts = []
    top_lines = []
    bottom_lines = []
    for lines_of, near, far, out in (
        (tops, 7, 6, top_lines),
        (bottoms, 0, 1, bottom_lines),
    ):
        near_x, near_y = lines_of[8 + near : 9 + near, :], lines_of[16 + near : 17 + near, :]
        far_x, far_y = lines_of[8 + far : 9 + far, :], lines_of[16 + far : 17 + far, :]
        starts.append((near_x, near_y))
        at_near = linear(lines_of[24 : 24 + FIRST, :], near_x, near_y)
        at_far = linear(lines_of[48 : 48 + FIRST, :], far_x, far_y)
        for k in range(2):
            out.append(
                jnp.where(line == near, at_near[k], jnp.where(line == far, at_far[k], zero_line))
            )

    def own(ref, k):
        return ref[2 * k * CX : (2 * k + 1) * CX] + ref[(2 * k + 1) * CX : (2 * k + 2) * CX]

    sources = []
    for k in range(2):
        before = jnp.where(lane >= 126, pltpu.roll(columns, 126 - 2 * k, 1), 0.0)
        after = jnp.where(lane < 2, pltpu.roll(columns, 124 - 2 * k, 1), 0.0)
        sources.append(assembled(top_lines[k], own(acc_ref, k), bottom_lines[k], before, after))
    x, y, z = advance(xs[...], ys[...], zs[...], *sources)
    xs[...] = x
    ys[...] = y
    zs[...] = z

    def flush(t):
        fetch(t).wait()
        write(t).start()

    sweep(count, total, flush)

    def prime():
        fld[...] = split_fields(xs[8 : 8 + CX, OWN], ys[8 : 8 + CX, OWN])
        acc[...] = jnp.zeros_like(acc)

    prime()

    def second(t):
        def make():
            return lambda start, size: product_ref[start : start + size, tile_rows(t)]

        save_state(state, t, tile_step(t, cells_ref, fld[...], make, acc))

    sweep(0, count, second)

    x = xs[...]
    y = ys[...]
    xl, yl = x[:, 0:128], y[:, 0:128]
    xr, yr = x[:, 384:512], y[:, 384:512]
    edge = jnp.where(
        lane == 127,
        xl,
        jnp.where(
            lane == 126,
            pltpu.roll(yl, 127, 1),
            jnp.where(lane == 0, xr, jnp.where(lane == 1, pltpu.roll(yr, 1, 1), 0.0)),
        ),
    )
    rows = turned(edge)
    ends_l = quadratic(lc, lx0, ly0, rows[127:128], rows[126:127])
    ends_r = quadratic(rc, rx0, ry0, rows[0:1], rows[1:2])
    columns = turned(
        jnp.concatenate([ends_l[0], ends_l[1], ends_r[0], ends_r[1], jnp.zeros((4, CY), F32)], axis=0)
    )[0:TALL]
    lines = []
    for (x0, y0), lines_of, near, at in (
        (starts[0], tops, 7, 7),
        (starts[1], bottoms, 0, 8 + CX),
    ):
        ends = quadratic(
            lines_of[24:48, :], x0, y0, x[at : at + 1, OWN], y[at : at + 1, OWN]
        )
        lines.append([jnp.where(line == near, ends[k], zero_line) for k in range(2)])
    sources = []
    for k in range(2):
        before = jnp.where(lane == 127, pltpu.roll(columns, 127 - k, 1), 0.0)
        after = jnp.where(lane == 0, pltpu.roll(columns, 126 - k, 1), 0.0)
        sources.append(assembled(lines[0][k], own(acc, k), lines[1][k], before, after))
    x, y, z = advance(x, y, zs[...], *sources)
    xs[...] = x
    ys[...] = y
    zs[...] = z
    prime()

    def third(t):
        def make():
            return rows_of(stored_product(table_ref, state, t))

        updated = tile_step(t, cells_ref, fld[...], make, acc)
        buf[tile_rows(t), :] = updated.T
        write(t).start()

    sweep(0, count, third)
    blank = jnp.zeros((TALL, 128), F32)
    sources = [assembled(zero_line, own(acc, k), zero_line, blank, blank) for k in range(2)]
    x, y, z = advance(xs[...], ys[...], zs[...], *sources)
    xs[8 : 8 + CX, OWN] = x[8 : 8 + CX, OWN]
    ys[8 : 8 + CX, OWN] = y[8 : 8 + CX, OWN]
    zs[8 : 8 + CX, OWN] = z[8 : 8 + CX, OWN]
    saves = [
        pltpu.make_async_copy(src.at[pl.ds(8, CX), pl.ds(128, CY)], dst, sems.at[total + k])
        for k, (src, dst) in enumerate(((xs, out_x), (ys, out_y), (zs, out_z)))
    ]
    for save in saves:
        save.start()
    sweep(0, total, lambda t: write(t).wait())
    for save in saves:
        save.wait()


VMEM = pl.BlockSpec(memory_space=pltpu.VMEM)
SMEM = pl.BlockSpec(memory_space=pltpu.SMEM)
ANY = pl.BlockSpec(memory_space=pl.ANY)
LIMITS = pltpu.CompilerParams(vmem_limit_bytes=40 << 20)


def shaped(shape, dtype=F32):
    return jax.ShapeDtypeStruct(shape, dtype)


def pairs(axis, first):
    count = lax.axis_size(axis)
    swaps = [(i % count, (i + 1) % count) for i in range(first, first + count, 2)]
    return swaps + [(b, a) for a, b in swaps]


def pinned(value):
    return pltpu.with_memory_space_constraint(value, pltpu.VMEM)


def streamed(value):
    return pltpu.with_memory_space_constraint(value, pltpu.HBM)


def held(shape, dtype=F32):
    return pltpu.VMEM(shape, dtype)


def shards(density, cell_index, live_batches, propagator, dipoles, ex, ey, mz):
    slots = density.shape[0]
    tiles = slots // TILE
    cells = cell_index.reshape(slots // 128, 128)
    buffer = pltpu.VMEM((slots, S2), F32)
    sems = pltpu.SemaphoreType.DMA((tiles + 3,))
    sums = (4 * CX, CY)
    halved = pltpu.VMEM((4 * CX, CY), BF16)
    half = held((slots, S2), BF16)
    readout, one, two, west, east, hi, lo = pl.pallas_call(
        coefficient_kernel,
        out_shape=(
            shaped((8, S2)),
            shaped((LINES, CY)),
            shaped((LINES, CY)),
            shaped((32, CX)),
            shaped((32, CX)),
            half,
            half,
        ),
        in_specs=[SMEM] + [ANY] * 7,
        out_specs=(VMEM,) * 7,
        scratch_shapes=[
            buffer,
            pltpu.VMEM((128, CY), F32),
            pltpu.VMEM((128, CX), F32),
            pltpu.VMEM(propagator.shape, F32),
            pltpu.VMEM(dipoles.shape, F32),
            pltpu.VMEM(cells.shape, jnp.int32),
            pltpu.SemaphoreType.DMA((slots // SMALL,)),
            pltpu.SemaphoreType.DMA((9,)),
        ],
        compiler_params=LIMITS,
        name="coefficients",
    )(
        live_batches,
        *(streamed(value) for value in (cells, ex, ey, mz, propagator, dipoles, density)),
    )
    row_one = lax.ppermute(one, "gx", pairs("gx", 0))
    row_two = lax.ppermute(two, "gx", pairs("gx", 1))
    table = pl.pallas_call(
        table_kernel,
        out_shape=held((ROWS, 3 * S2), BF16),
        in_specs=[VMEM] * 2,
        out_specs=VMEM,
        compiler_params=LIMITS,
        name="table",
    )(propagator, readout)
    state, source = pl.pallas_call(
        first_kernel,
        out_shape=(held((slots, 2 * S2), BF16), held(sums)),
        in_specs=[SMEM] + [VMEM] * 6,
        out_specs=(VMEM,) * 2,
        scratch_shapes=[halved],
        compiler_params=LIMITS,
        name="first",
    )(live_batches, cells, ex, ey, pinned(table), pinned(hi), pinned(lo))
    package = held((LINES, CY))
    to_one, to_two = pl.pallas_call(
        corner_kernel,
        out_shape=(package, package),
        in_specs=[VMEM] * 5 + [VMEM] * 2 + [ANY],
        out_specs=(VMEM,) * 2,
        compiler_params=LIMITS,
        name="corners",
    )(ex, ey, mz, west, east, pinned(row_one), pinned(row_two), pinned(source))
    col_one = lax.ppermute(to_one, "gy", pairs("gy", 0))
    col_two = lax.ppermute(to_two, "gy", pairs("gy", 1))
    product = pl.pallas_call(
        ahead_kernel,
        out_shape=held((ROWS, slots)),
        in_specs=[SMEM] + [VMEM] * 2 + [ANY],
        out_specs=VMEM,
        compiler_params=LIMITS,
        name="ahead",
    )(live_batches, pinned(table), pinned(state), pinned(to_one))
    field = shaped((CX, CY))
    tall = pltpu.VMEM((TALL, WIDE), F32)
    return pl.pallas_call(
        main_kernel,
        out_shape=(shaped((slots, S2)), field, field, field),
        in_specs=[SMEM] + [VMEM] * 11 + [ANY],
        out_specs=(ANY,) * 4,
        scratch_shapes=[
            pltpu.VMEM((slots, 2 * S2), BF16), buffer, pltpu.VMEM(sums, F32), halved,
            tall, tall, tall, sems,
        ],
        compiler_params=LIMITS,
        name="main",
    )(
        live_batches, cells, ex, ey, mz, pinned(source), pinned(table), pinned(product),
        pinned(row_one), pinned(row_two), pinned(col_one), pinned(col_two), streamed(density),
    )


def solution(mesh):
    placed = (
        P(("gx", "gy"), None),
        P(("gx", "gy")),
        P(("gx", "gy")),
        P(),
        P(),
        P("gx", "gy"),
        P("gx", "gy"),
        P("gx", "gy"),
    )
    return jax.shard_map(
        shards,
        mesh=mesh,
        in_specs=placed,
        out_specs=(P(("gx", "gy"), None), P("gx", "gy"), P("gx", "gy"), P("gx", "gy")),
        check_vma=False,
    )
```

```python
import jax
import jax.numpy as jnp
from jax import lax
from jax.experimental import pallas as pl
from jax.experimental.pallas import tpu as pltpu
from jax.sharding import PartitionSpec as P

BATCH = 64
STEPS = 3
TILE = 1024
SMALL = 512
COURANT = 0.5
CX = 128
CY = 256
S2 = 256
ROWS = 3 * S2 + 16
FIRST = 6
ORDERS = 24
LINES = 56
TALL = CX + 16
WIDE = CY + 256
F32 = jnp.float32
BF16 = jnp.bfloat16
NT = (((1,), (1,)), ((), ()))


def halves(x):
    hi = x.astype(BF16)
    return hi, (x - hi.astype(F32)).astype(BF16)


def fast_nt(a, b):
    return lax.dot_general(a, b, NT, preferred_element_type=F32)


def functionals_of(prop_ref, dip_ref):
    blocks = [halves(prop_ref[:, b * S2 : (b + 1) * S2]) for b in range(3)]

    def through(value, block):
        rows = value.shape[0]
        vh, vl = halves(value)
        wide = fast_nt(jnp.concatenate([vh, vl], axis=0), block[0])
        return wide[0:rows] + wide[rows:] + fast_nt(vh, block[1])

    dipoles = dip_ref[...]
    padded = jnp.concatenate([dipoles, jnp.zeros((6, S2), F32)], axis=0)
    reads = [through(padded, block)[0:2] for block in blocks]
    first = jnp.concatenate(
        [reads[0] - dipoles, reads[1], reads[2], jnp.zeros((2, S2), F32)], axis=0
    )
    second = [through(first, block)[0:FIRST] for block in blocks]
    return jnp.concatenate([first[0:FIRST], *second, jnp.zeros((8, S2), F32)], axis=0)


def table_kernel(prop_ref, readout_ref, table_ref):
    def put(rows, value):
        hi, lo = halves(value)
        table_ref[rows, 0:S2] = hi
        table_ref[rows, S2 : 2 * S2] = hi
        table_ref[rows, 2 * S2 :] = lo

    put(pl.ds(0, 16), jnp.concatenate([readout_ref[...], jnp.zeros((8, S2), F32)], axis=0))
    for b in range(3):
        block = prop_ref[:, b * S2 : (b + 1) * S2].T
        for q in range(S2 // 16):
            put(pl.ds(16 + 48 * q + 16 * b, 16), block[16 * q : 16 * q + 16])


def even(axis):
    return lax.axis_index(axis) % 2 == 0


def cells_of(cells_ref, t, size=TILE):
    cell = jnp.concatenate(
        [cells_ref[pl.ds(t * (size // 128) + j, 1), :] for j in range(size // 128)], axis=1
    )
    return cell >> 8, cell & (CY - 1)


def matches(index, size):
    return lax.broadcasted_iota(jnp.int32, (size, index.shape[1]), 0) == index


def one_hot(index, size):
    return jnp.where(matches(index, size), 1.0, 0.0).astype(BF16)


def count_of(live_ref, size=TILE):
    return live_ref[0] * BATCH // size


def tile_rows(t, size=TILE):
    return pl.ds(pl.multiple_of(t * size, size), size)


def sweep(lower, upper, body):
    def wrapped(t, carry):
        body(t)
        return carry

    lax.fori_loop(lower, upper, wrapped, 0)


def coefficient_kernel(
    live_ref, cells_hbm, ex_hbm, ey_hbm, mz_hbm, prop_hbm, dip_hbm, dens_hbm,
    readout_ref, one_ref, two_ref, west_ref, east_ref, hi_ref, lo_ref,
    buf, by_row, by_col, prop_ref, dip_ref, cells_ref, sems, loads,
):
    count = count_of(live_ref, SMALL)

    def copy(t):
        return pltpu.make_async_copy(dens_hbm.at[tile_rows(t, SMALL), :], buf.at[tile_rows(t, SMALL), :], sems.at[t])

    pairs = [(dip_hbm, dip_ref), (prop_hbm, prop_ref), (cells_hbm, cells_ref)]
    is_even = even("gx")
    starts = (jnp.where(is_even, CX - 8, 0), jnp.where(is_even, 0, CX - 8))
    for ref, start in zip((one_ref, two_ref), starts):
        start = pl.multiple_of(start, 8)
        for k, field in enumerate((mz_hbm, ex_hbm, ey_hbm)):
            pairs.append((field.at[pl.ds(start, 8), :], ref.at[pl.ds(8 * k, 8), :]))
    moves = [pltpu.make_async_copy(src, dst, loads.at[k]) for k, (src, dst) in enumerate(pairs)]
    for move in moves[:3]:
        move.start()
    sweep(0, count, lambda t: copy(t).start())
    for move in moves[3:]:
        move.start()
    for move in moves[:2]:
        move.wait()
    functionals = functionals_of(prop_ref, dip_ref)
    readout_ref[...] = functionals[0:8]
    fh, fl = halves(functionals)
    stacked = jnp.concatenate([fh, fl], axis=0)
    by_row[...] = jnp.zeros_like(by_row)
    by_col[...] = jnp.zeros_like(by_col)

    def picked(index, near, far, parts):
        out = []
        for place, rows in ((near[0], ORDERS), (near[1], ORDERS), (far[0], 8), (far[1], 8)):
            for part in parts:
                out.append(jnp.where(index == place, part[0:rows], 0.0))
        return jnp.concatenate(out, axis=0).astype(BF16)

    def body(t):
        copy(t).wait()
        dh, dl = halves(buf[tile_rows(t, SMALL), :])
        hi_ref[tile_rows(t, SMALL), :] = dh
        lo_ref[tile_rows(t, SMALL), :] = dl
        wide = fast_nt(stacked, dh)
        values = wide[0:32] + wide[32:64] + fast_nt(fh, dl)
        vh, vl = halves(values)
        parts = (vh.astype(F32), vl.astype(F32))
        row, col = cells_of(cells_ref, t, SMALL)
        by_row[...] += fast_nt(picked(row, (0, CX - 1), (1, CX - 2), parts), one_hot(col, CY))
        by_col[...] += fast_nt(picked(col, (0, CY - 1), (1, CY - 2), parts), one_hot(row, CX))

    for move in moves[2:]:
        move.wait()
    sweep(0, count, body)

    def side(ref, which):
        near = 2 * ORDERS * which
        far = 4 * ORDERS + 16 * which
        return (
            ref[near : near + ORDERS] + ref[near + ORDERS : near + 2 * ORDERS],
            ref[far : far + 8] + ref[far + 8 : far + 16],
        )

    low, high = side(by_row, 0), side(by_row, 1)
    for ref, if_even, if_odd in ((one_ref, high, low), (two_ref, low, high)):
        ref[24:48] = jnp.where(is_even, if_even[0], if_odd[0])
        ref[48:56] = jnp.where(is_even, if_even[1], if_odd[1])
    for which, ref in ((0, west_ref), (1, east_ref)):
        near, far = side(by_col, which)
        ref[0:ORDERS] = near
        ref[ORDERS:] = far


def sampled(t, cells_ref, fields):
    cell = cells_ref[pl.ds(pl.multiple_of(t * (TILE // 128), 8), TILE // 128), :]
    lane = cell & 127
    strip = cell >> 7
    values = [jnp.zeros(cell.shape, F32) for _ in fields]
    for r in range(CX):
        for half in range(CY // 128):
            here = strip == r * (CY // 128) + half
            for k, field in enumerate(fields):
                line = jnp.broadcast_to(field[r : r + 1, 128 * half : 128 * half + 128], cell.shape)
                found = jnp.take_along_axis(line, lane, axis=1)
                values[k] = jnp.where(here, found, values[k])
    return [
        jnp.concatenate([value[j : j + 1] for j in range(TILE // 128)], axis=1) for value in values
    ]


def tile_step(t, cells_ref, fields, make, source_ref, split=False):
    row, col = cells_of(cells_ref, t)
    hot_col = one_hot(col, CY)
    mask = matches(row, CX)
    if split:
        lines = jnp.dot(fields, hot_col, preferred_element_type=F32)
        sample_x, sample_y = (
            jnp.sum(
                jnp.where(mask, lines[k : k + CX] + lines[k + CX : k + 2 * CX], 0.0),
                axis=0,
                keepdims=True,
            )
            for k in (0, 2 * CX)
        )
    else:
        sample_x, sample_y = sampled(t, cells_ref, fields)
    product = make()
    reads = product(0, 8)
    current_x = reads[0:1] + sample_x * reads[2:3] + sample_y * reads[4:5]
    current_y = reads[1:2] + sample_x * reads[3:4] + sample_y * reads[5:6]
    marked = [
        jnp.where(mask, part.astype(F32), 0.0).astype(BF16)
        for current in (current_x, current_y)
        for part in halves(current)
    ]
    if not split:
        source_ref[...] += fast_nt(jnp.concatenate(marked, axis=0), hot_col)
    groups = []
    for k in range(4):
        if split:
            source_ref[k * CX : (k + 1) * CX] += fast_nt(marked[k], hot_col)
        for q in range(4 * k, 4 * k + 4):
            base = 16 + 48 * q
            groups.append(
                product(base, 16)
                + sample_x * product(base + 16, 16)
                + sample_y * product(base + 32, 16)
            )
    return jnp.concatenate(groups, axis=0)


def split_fields(ex, ey):
    xh, xl = halves(ex)
    yh, yl = halves(ey)
    return jnp.concatenate([xh, xl, yh, yl], axis=0)


def save_state(state_ref, t, updated):
    hi, lo = halves(updated.T)
    state_ref[tile_rows(t), 0:S2] = hi
    state_ref[tile_rows(t), S2:] = lo


def rows_of(value):
    return lambda start, size: value[start : start + size]


def stored_product(table_ref, state_ref, t):
    hi, lo = state_ref[tile_rows(t), 0:S2], state_ref[tile_rows(t), S2:]
    return fast_nt(table_ref[...], jnp.concatenate([hi, lo, hi], axis=1))


def first_kernel(
    live_ref, cells_ref, ex_ref, ey_ref, table_ref, hi_ref, lo_ref, state_ref, acc
):
    acc[...] = jnp.zeros_like(acc)

    def body(t):
        hi, lo = hi_ref[tile_rows(t), :], lo_ref[tile_rows(t), :]

        def make():
            return rows_of(fast_nt(table_ref[...], jnp.concatenate([hi, lo, hi], axis=1)))

        save_state(state_ref, t, tile_step(t, cells_ref, (ex_ref, ey_ref), make, acc))

    sweep(0, count_of(live_ref), body)


def ahead_kernel(live_ref, table_ref, state_ref, after_ref, product_ref):
    def body(t):
        product_ref[:, tile_rows(t)] = stored_product(table_ref, state_ref, t)

    sweep(0, count_of(live_ref), body)


def turned(value):
    rows, lanes = value.shape
    if rows < 128:
        value = jnp.concatenate([value, jnp.zeros((128 - rows, lanes), F32)], axis=0)
    elif rows < 256:
        value = jnp.concatenate([value, jnp.zeros((256 - rows, lanes), F32)], axis=0)
    return value.T


def ordered(axis, one_ref, two_ref):
    is_even = even(axis)
    one, two = one_ref[...], two_ref[...]
    return jnp.where(is_even, two, one), jnp.where(is_even, one, two)


def corner_kernel(
    ex_ref, ey_ref, mz_ref, west_ref, east_ref, one_ref, two_ref, after_ref, to_one_ref, to_two_ref
):
    tops, bottoms = ordered("gx", one_ref, two_ref)
    packages = []
    lane = lax.broadcasted_iota(jnp.int32, (TALL, 128), 1)
    for side, coefs_ref in ((0, west_ref), (1, east_ref)):
        half = slice(128 * side, 128 * side + 128)

        def tall(k, field_ref):
            rows = slice(8 * k, 8 * k + 8)
            return jnp.concatenate([tops[rows, half], field_ref[:, half], bottoms[rows, half]], axis=0)

        shift = 8 * side
        m = tall(0, mz_ref)
        if shift:
            m = pltpu.roll(m, shift, 1)
        x = pltpu.roll(tall(1, ex_ref), 8 + shift, 1)
        y = pltpu.roll(tall(2, ey_ref), 16 + shift, 1)
        items = jnp.where(lane < 8, m, jnp.where(lane < 16, x, y))
        coefs = coefs_ref[...]
        wide = pltpu.roll(jnp.concatenate([coefs, jnp.zeros_like(coefs)], axis=1), 8, 1)
        lower = wide[:, 0:128]
        upper = wide[:, 128:256]
        place = lax.broadcasted_iota(jnp.int32, (32, 128), 1)
        gap = jnp.zeros((16, 128), F32)

        def both(lines, near_from, far_from, near_to, far_to, base):
            near = lines[24:48, half]
            far = lines[48:56, half]
            at_near = jnp.concatenate(
                [
                    pltpu.roll(near, (near_to - near_from) % 128, 1),
                    pltpu.roll(near[0:8], (near_to - far_from) % 128, 1),
                ],
                axis=0,
            )
            at_far = jnp.concatenate(
                [
                    pltpu.roll(far, (far_to - near_from) % 128, 1),
                    gap,
                    pltpu.roll(far, (far_to - far_from) % 128, 1),
                ],
                axis=0,
            )
            return jnp.where(place == near_to, at_near, jnp.where(place == far_to, at_far, base))

        near_from, far_from = (127, 126) if side else (0, 1)
        spread = jnp.concatenate(
            [
                both(tops, near_from, far_from, 7, 6, lower),
                both(bottoms, near_from, far_from, 8, 9, upper),
            ],
            axis=1,
        )
        packages.append(jnp.concatenate([turned(items)[0:24], spread], axis=0))
    left, right = packages
    is_even = even("gy")
    to_one_ref[...] = jnp.where(is_even, right, left)
    to_two_ref[...] = jnp.where(is_even, left, right)


def linear(coefs, x, y):
    return (
        coefs[0:1] + x * coefs[2:3] + y * coefs[4:5],
        coefs[1:2] + x * coefs[3:4] + y * coefs[5:6],
    )


def quadratic(coefs, x0, y0, x1, y1):
    terms = [linear(coefs[FIRST * (c + 1) : FIRST * (c + 2)], x1, y1) for c in range(3)]
    return tuple(terms[0][k] + x0 * terms[1][k] + y0 * terms[2][k] for k in range(2))


def advance(x, y, z, source_x, source_y):
    y_next = pltpu.roll(y, TALL - 1, 0)
    x_next = pltpu.roll(x, WIDE - 1, 1)
    z = z - COURANT * ((y_next - y) - (x_next - x))
    x = x + COURANT * (z - pltpu.roll(z, 1, 1)) - source_x
    y = y - COURANT * (z - pltpu.roll(z, 1, 0)) - source_y
    return x, y, z


OWN = slice(128, 128 + CY)


def main_kernel(
    live_ref, cells_ref, ex_ref, ey_ref, mz_ref, acc_ref, table_ref, product_ref,
    row_one_ref, row_two_ref, col_one_ref, col_two_ref, dens_ref,
    evolved_ref, out_x, out_y, out_z, state, buf, acc, fld, xs, ys, zs, sems,
):
    count = count_of(live_ref)
    total = dens_ref.shape[0] // TILE

    def fetch(t):
        return pltpu.make_async_copy(dens_ref.at[tile_rows(t), :], buf.at[tile_rows(t), :], sems.at[t])

    def write(t):
        return pltpu.make_async_copy(buf.at[tile_rows(t), :], evolved_ref.at[tile_rows(t), :], sems.at[t])

    sweep(count, total, lambda t: fetch(t).start())

    tops, bottoms = ordered("gx", row_one_ref, row_two_ref)
    left, right = ordered("gy", col_one_ref, col_two_ref)
    left_items = turned(left[0:24])[0:TALL]
    right_items = turned(right[0:24])[0:TALL]

    def extended(k, field_ref):
        rows = slice(8 * k, 8 * k + 8)
        middle = jnp.concatenate([tops[rows, :], field_ref[...], bottoms[rows, :]], axis=0)
        before = pltpu.roll(left_items, 120 - 8 * k, 1)
        after = right_items
        if k:
            after = pltpu.roll(after, 128 - 8 * k, 1)
        return jnp.concatenate([before, middle, after], axis=1)

    zs[...] = extended(0, mz_ref)
    xs[...] = extended(1, ex_ref)
    ys[...] = extended(2, ey_ref)

    sides = []
    for package, near, far in ((left, 7, 6), (right, 0, 1)):
        lines = package[0:24]
        coefs = package[24:]
        near_x, near_y = lines[8 + near : 9 + near], lines[16 + near : 17 + near]
        far_x, far_y = lines[8 + far : 9 + far], lines[16 + far : 17 + far]
        sides.append(
            (
                coefs,
                near_x,
                near_y,
                linear(coefs[0:FIRST], near_x, near_y),
                linear(coefs[ORDERS : ORDERS + FIRST], far_x, far_y),
            )
        )
    lane = lax.broadcasted_iota(jnp.int32, (TALL, 128), 1)
    line = lax.broadcasted_iota(jnp.int32, (8, CY), 0)

    def assembled(tops, rows, bottoms, before, after):
        middle = jnp.concatenate([tops, rows, bottoms], axis=0)
        return jnp.concatenate([before, middle, after], axis=1)

    (lc, lx0, ly0, lnear, lfar), (rc, rx0, ry0, rnear, rfar) = sides
    columns = turned(
        jnp.concatenate(
            [lfar[0], lnear[0], lfar[1], lnear[1], rnear[0], rfar[0], rnear[1], rfar[1]], axis=0
        )
    )[0:TALL]
    zero_line = jnp.zeros((8, CY), F32)
    starts = []
    top_lines = []
    bottom_lines = []
    for lines_of, near, far, out in (
        (tops, 7, 6, top_lines),
        (bottoms, 0, 1, bottom_lines),
    ):
        near_x, near_y = lines_of[8 + near : 9 + near, :], lines_of[16 + near : 17 + near, :]
        far_x, far_y = lines_of[8 + far : 9 + far, :], lines_of[16 + far : 17 + far, :]
        starts.append((near_x, near_y))
        at_near = linear(lines_of[24 : 24 + FIRST, :], near_x, near_y)
        at_far = linear(lines_of[48 : 48 + FIRST, :], far_x, far_y)
        for k in range(2):
            out.append(
                jnp.where(line == near, at_near[k], jnp.where(line == far, at_far[k], zero_line))
            )

    def own(ref, k):
        return ref[2 * k * CX : (2 * k + 1) * CX] + ref[(2 * k + 1) * CX : (2 * k + 2) * CX]

    sources = []
    for k in range(2):
        before = jnp.where(lane >= 126, pltpu.roll(columns, 126 - 2 * k, 1), 0.0)
        after = jnp.where(lane < 2, pltpu.roll(columns, 124 - 2 * k, 1), 0.0)
        sources.append(assembled(top_lines[k], own(acc_ref, k), bottom_lines[k], before, after))
    x, y, z = advance(xs[...], ys[...], zs[...], *sources)
    xs[...] = x
    ys[...] = y
    zs[...] = z

    def flush(t):
        fetch(t).wait()
        write(t).start()

    sweep(count, total, flush)

    fields = [ref.at[pl.ds(8, CX), pl.ds(128, CY)] for ref in (xs, ys)]
    fld[...] = split_fields(*(field[...] for field in fields))
    acc[...] = jnp.zeros_like(acc)

    def second(t):
        def make():
            return lambda start, size: product_ref[start : start + size, tile_rows(t)]

        save_state(state, t, tile_step(t, cells_ref, fld[...], make, acc, True))

    sweep(0, count, second)

    x = xs[...]
    y = ys[...]
    xl, yl = x[:, 0:128], y[:, 0:128]
    xr, yr = x[:, 384:512], y[:, 384:512]
    edge = jnp.where(
        lane == 127,
        xl,
        jnp.where(
            lane == 126,
            pltpu.roll(yl, 127, 1),
            jnp.where(lane == 0, xr, jnp.where(lane == 1, pltpu.roll(yr, 1, 1), 0.0)),
        ),
    )
    rows = turned(edge)
    ends_l = quadratic(lc, lx0, ly0, rows[127:128], rows[126:127])
    ends_r = quadratic(rc, rx0, ry0, rows[0:1], rows[1:2])
    columns = turned(
        jnp.concatenate([ends_l[0], ends_l[1], ends_r[0], ends_r[1], jnp.zeros((4, CY), F32)], axis=0)
    )[0:TALL]
    lines = []
    for (x0, y0), lines_of, near, at in (
        (starts[0], tops, 7, 7),
        (starts[1], bottoms, 0, 8 + CX),
    ):
        ends = quadratic(
            lines_of[24:48, :], x0, y0, x[at : at + 1, OWN], y[at : at + 1, OWN]
        )
        lines.append([jnp.where(line == near, ends[k], zero_line) for k in range(2)])
    sources = []
    for k in range(2):
        before = jnp.where(lane == 127, pltpu.roll(columns, 127 - k, 1), 0.0)
        after = jnp.where(lane == 0, pltpu.roll(columns, 126 - k, 1), 0.0)
        sources.append(assembled(lines[0][k], own(acc, k), lines[1][k], before, after))
    x, y, z = advance(x, y, zs[...], *sources)
    xs[...] = x
    ys[...] = y
    zs[...] = z
    acc[...] = jnp.zeros_like(acc)

    def third(t):
        def make():
            return rows_of(stored_product(table_ref, state, t))

        updated = tile_step(t, cells_ref, fields, make, acc)
        buf[tile_rows(t), :] = updated.T
        write(t).start()

    sweep(0, count, third)
    blank = jnp.zeros((TALL, 128), F32)
    sources = [assembled(zero_line, own(acc, k), zero_line, blank, blank) for k in range(2)]
    x, y, z = advance(xs[...], ys[...], zs[...], *sources)
    xs[8 : 8 + CX, OWN] = x[8 : 8 + CX, OWN]
    ys[8 : 8 + CX, OWN] = y[8 : 8 + CX, OWN]
    zs[8 : 8 + CX, OWN] = z[8 : 8 + CX, OWN]
    saves = [
        pltpu.make_async_copy(src.at[pl.ds(8, CX), pl.ds(128, CY)], dst, sems.at[total + k])
        for k, (src, dst) in enumerate(((xs, out_x), (ys, out_y), (zs, out_z)))
    ]
    for save in saves:
        save.start()
    sweep(0, total, lambda t: write(t).wait())
    for save in saves:
        save.wait()


VMEM = pl.BlockSpec(memory_space=pltpu.VMEM)
SMEM = pl.BlockSpec(memory_space=pltpu.SMEM)
ANY = pl.BlockSpec(memory_space=pl.ANY)
LIMITS = pltpu.CompilerParams(vmem_limit_bytes=40 << 20)


def shaped(shape, dtype=F32):
    return jax.ShapeDtypeStruct(shape, dtype)


def pairs(axis, first):
    count = lax.axis_size(axis)
    swaps = [(i % count, (i + 1) % count) for i in range(first, first + count, 2)]
    return swaps + [(b, a) for a, b in swaps]


def pinned(value):
    return pltpu.with_memory_space_constraint(value, pltpu.VMEM)


def streamed(value):
    return pltpu.with_memory_space_constraint(value, pltpu.HBM)


def held(shape, dtype=F32):
    return pltpu.VMEM(shape, dtype)


def shards(density, cell_index, live_batches, propagator, dipoles, ex, ey, mz):
    slots = density.shape[0]
    tiles = slots // TILE
    cells = cell_index.reshape(slots // 128, 128)
    buffer = pltpu.VMEM((slots, S2), F32)
    sems = pltpu.SemaphoreType.DMA((tiles + 3,))
    sums = (4 * CX, CY)
    half = held((slots, S2), BF16)
    readout, one, two, west, east, hi, lo = pl.pallas_call(
        coefficient_kernel,
        out_shape=(
            shaped((8, S2)),
            shaped((LINES, CY)),
            shaped((LINES, CY)),
            shaped((32, CX)),
            shaped((32, CX)),
            half,
            half,
        ),
        in_specs=[SMEM] + [ANY] * 7,
        out_specs=(VMEM,) * 7,
        scratch_shapes=[
            buffer,
            pltpu.VMEM((128, CY), F32),
            pltpu.VMEM((128, CX), F32),
            pltpu.VMEM(propagator.shape, F32),
            pltpu.VMEM(dipoles.shape, F32),
            pltpu.VMEM(cells.shape, jnp.int32),
            pltpu.SemaphoreType.DMA((slots // SMALL,)),
            pltpu.SemaphoreType.DMA((9,)),
        ],
        compiler_params=LIMITS,
        name="coefficients",
    )(
        live_batches,
        *(streamed(value) for value in (cells, ex, ey, mz, propagator, dipoles, density)),
    )
    row_one = lax.ppermute(one, "gx", pairs("gx", 0))
    row_two = lax.ppermute(two, "gx", pairs("gx", 1))
    table = pl.pallas_call(
        table_kernel,
        out_shape=held((ROWS, 3 * S2), BF16),
        in_specs=[VMEM] * 2,
        out_specs=VMEM,
        compiler_params=LIMITS,
        name="table",
    )(propagator, readout)
    state, source = pl.pallas_call(
        first_kernel,
        out_shape=(held((slots, 2 * S2), BF16), held(sums)),
        in_specs=[SMEM] + [VMEM] * 6,
        out_specs=(VMEM,) * 2,
        compiler_params=LIMITS,
        name="first",
    )(live_batches, cells, ex, ey, pinned(table), pinned(hi), pinned(lo))
    package = held((LINES, CY))
    to_one, to_two = pl.pallas_call(
        corner_kernel,
        out_shape=(package, package),
        in_specs=[VMEM] * 5 + [VMEM] * 2 + [ANY],
        out_specs=(VMEM,) * 2,
        compiler_params=LIMITS,
        name="corners",
    )(ex, ey, mz, west, east, pinned(row_one), pinned(row_two), pinned(source))
    col_one = lax.ppermute(to_one, "gy", pairs("gy", 0))
    col_two = lax.ppermute(to_two, "gy", pairs("gy", 1))
    product = pl.pallas_call(
        ahead_kernel,
        out_shape=held((ROWS, slots)),
        in_specs=[SMEM] + [VMEM] * 2 + [ANY],
        out_specs=VMEM,
        compiler_params=LIMITS,
        name="ahead",
    )(live_batches, pinned(table), pinned(state), pinned(to_one))
    field = shaped((CX, CY))
    tall = pltpu.VMEM((TALL, WIDE), F32)
    return pl.pallas_call(
        main_kernel,
        out_shape=(shaped((slots, S2)), field, field, field),
        in_specs=[SMEM] + [VMEM] * 11 + [ANY],
        out_specs=(ANY,) * 4,
        scratch_shapes=[
            pltpu.VMEM((slots, 2 * S2), BF16), buffer, pltpu.VMEM(sums, F32), pltpu.VMEM(sums, BF16),
            tall, tall, tall, sems,
        ],
        compiler_params=LIMITS,
        name="main",
    )(
        live_batches, cells, ex, ey, mz, pinned(source), pinned(table), pinned(product),
        pinned(row_one), pinned(row_two), pinned(col_one), pinned(col_two), streamed(density),
    )


def solution(mesh):
    placed = (
        P(("gx", "gy"), None),
        P(("gx", "gy")),
        P(("gx", "gy")),
        P(),
        P(),
        P("gx", "gy"),
        P("gx", "gy"),
        P("gx", "gy"),
    )
    return jax.shard_map(
        shards,
        mesh=mesh,
        in_specs=placed,
        out_specs=(P(("gx", "gy"), None), P("gx", "gy"), P("gx", "gy"), P("gx", "gy")),
        check_vma=False,
    )
```

```python
import jax
import jax.numpy as jnp
from jax import lax
from jax.experimental import pallas as pl
from jax.experimental.pallas import tpu as pltpu
from jax.sharding import PartitionSpec as P

BATCH = 64
STEPS = 3
TILE = 1024
SMALL = 1024
PART = 256
COURANT = 0.5
CX = 128
CY = 256
S2 = 256
ROWS = 3 * S2 + 16
FIRST = 6
ORDERS = 24
LINES = 56
TALL = CX + 16
WIDE = CY + 256
F32 = jnp.float32
BF16 = jnp.bfloat16
NT = (((1,), (1,)), ((), ()))


def halves(x):
    hi = x.astype(BF16)
    return hi, (x - hi.astype(F32)).astype(BF16)


def fast_nt(a, b):
    return lax.dot_general(a, b, NT, preferred_element_type=F32)


def functionals_of(prop_ref, dip_ref):
    blocks = [halves(prop_ref[:, b * S2 : (b + 1) * S2]) for b in range(3)]

    def through(value, block):
        rows = value.shape[0]
        vh, vl = halves(value)
        wide = fast_nt(jnp.concatenate([vh, vl], axis=0), block[0])
        return wide[0:rows] + wide[rows:] + fast_nt(vh, block[1])

    dipoles = dip_ref[...]
    padded = jnp.concatenate([dipoles, jnp.zeros((6, S2), F32)], axis=0)
    reads = [through(padded, block)[0:2] for block in blocks]
    first = jnp.concatenate(
        [reads[0] - dipoles, reads[1], reads[2], jnp.zeros((2, S2), F32)], axis=0
    )
    second = [through(first, block)[0:FIRST] for block in blocks]
    return jnp.concatenate([first[0:FIRST], *second, jnp.zeros((8, S2), F32)], axis=0)


def table_kernel(prop_ref, readout_ref, table_ref):
    def put(rows, value):
        hi, lo = halves(value)
        table_ref[rows, 0:S2] = hi
        table_ref[rows, S2 : 2 * S2] = hi
        table_ref[rows, 2 * S2 :] = lo

    put(pl.ds(0, 16), jnp.concatenate([readout_ref[...], jnp.zeros((8, S2), F32)], axis=0))
    for b in range(3):
        block = prop_ref[:, b * S2 : (b + 1) * S2].T
        for q in range(S2 // 16):
            put(pl.ds(16 + 48 * q + 16 * b, 16), block[16 * q : 16 * q + 16])


def even(axis):
    return lax.axis_index(axis) % 2 == 0


def cells_of(cells_ref, t, size=TILE):
    cell = jnp.concatenate(
        [cells_ref[pl.ds(t * (size // 128) + j, 1), :] for j in range(size // 128)], axis=1
    )
    return cell >> 8, cell & (CY - 1)


def matches(index, size):
    return lax.broadcasted_iota(jnp.int32, (size, index.shape[1]), 0) == index


def one_hot(index, size):
    return jnp.where(matches(index, size), 1.0, 0.0).astype(BF16)


def count_of(live_ref, size=TILE):
    return live_ref[0] * BATCH // size


def tile_rows(t, size=TILE):
    return pl.ds(pl.multiple_of(t * size, size), size)


def sweep(lower, upper, body):
    def wrapped(t, carry):
        body(t)
        return carry

    lax.fori_loop(lower, upper, wrapped, 0)


def coefficient_kernel(
    live_ref, cells_hbm, ex_hbm, ey_hbm, mz_hbm, prop_hbm, dip_hbm, dens_hbm,
    readout_ref, one_ref, two_ref, west_ref, east_ref, hi_ref, lo_ref,
    buf, by_row, by_col, prop_ref, dip_ref, cells_ref, sems, loads,
):
    count = count_of(live_ref, SMALL)

    def copy(t):
        return pltpu.make_async_copy(dens_hbm.at[tile_rows(t, SMALL), :], buf.at[tile_rows(t, SMALL), :], sems.at[t])

    pairs = [(dip_hbm, dip_ref), (prop_hbm, prop_ref), (cells_hbm, cells_ref)]
    is_even = even("gx")
    starts = (jnp.where(is_even, CX - 8, 0), jnp.where(is_even, 0, CX - 8))
    for ref, start in zip((one_ref, two_ref), starts):
        start = pl.multiple_of(start, 8)
        for k, field in enumerate((mz_hbm, ex_hbm, ey_hbm)):
            pairs.append((field.at[pl.ds(start, 8), :], ref.at[pl.ds(8 * k, 8), :]))
    moves = [pltpu.make_async_copy(src, dst, loads.at[k]) for k, (src, dst) in enumerate(pairs)]
    for move in moves[:3]:
        move.start()
    sweep(0, count, lambda t: copy(t).start())
    for move in moves[3:]:
        move.start()
    for move in moves[:2]:
        move.wait()
    functionals = functionals_of(prop_ref, dip_ref)
    readout_ref[...] = functionals[0:8]
    fh, fl = halves(functionals)
    stacked = jnp.concatenate([fh, fl], axis=0)
    by_row[...] = jnp.zeros_like(by_row)
    by_col[...] = jnp.zeros_like(by_col)

    def picked(index, near, far, parts):
        out = []
        for place, rows in ((near[0], ORDERS), (near[1], ORDERS), (far[0], 8), (far[1], 8)):
            for part in parts:
                out.append(jnp.where(index == place, part[0:rows], 0.0))
        return jnp.concatenate(out, axis=0).astype(BF16)

    def body(t):
        copy(t).wait()
        dh, dl = halves(buf[tile_rows(t, SMALL), :])
        hi_ref[tile_rows(t, SMALL), :] = dh
        lo_ref[tile_rows(t, SMALL), :] = dl
        wide = fast_nt(stacked, dh)
        values = wide[0:32] + wide[32:64] + fast_nt(fh, dl)
        vh, vl = halves(values)
        parts = (vh.astype(F32), vl.astype(F32))
        row, col = cells_of(cells_ref, t, SMALL)
        by_row[...] += fast_nt(picked(row, (0, CX - 1), (1, CX - 2), parts), one_hot(col, CY))
        by_col[...] += fast_nt(picked(col, (0, CY - 1), (1, CY - 2), parts), one_hot(row, CX))

    for move in moves[2:]:
        move.wait()
    sweep(0, count, body)

    def side(ref, which):
        near = 2 * ORDERS * which
        far = 4 * ORDERS + 16 * which
        return (
            ref[near : near + ORDERS] + ref[near + ORDERS : near + 2 * ORDERS],
            ref[far : far + 8] + ref[far + 8 : far + 16],
        )

    low, high = side(by_row, 0), side(by_row, 1)
    for ref, if_even, if_odd in ((one_ref, high, low), (two_ref, low, high)):
        ref[24:48] = jnp.where(is_even, if_even[0], if_odd[0])
        ref[48:56] = jnp.where(is_even, if_even[1], if_odd[1])
    for which, ref in ((0, west_ref), (1, east_ref)):
        near, far = side(by_col, which)
        ref[0:ORDERS] = near
        ref[ORDERS:] = far


def sampled(t, cells_ref, fields):
    cell = cells_ref[pl.ds(pl.multiple_of(t * (TILE // 128), 8), TILE // 128), :]
    lane = cell & 127
    strip = cell >> 7
    values = [jnp.zeros(cell.shape, F32) for _ in fields]
    for r in range(CX):
        for half in range(CY // 128):
            here = strip == r * (CY // 128) + half
            for k, field in enumerate(fields):
                line = jnp.broadcast_to(field[r : r + 1, 128 * half : 128 * half + 128], cell.shape)
                found = jnp.take_along_axis(line, lane, axis=1)
                values[k] = jnp.where(here, found, values[k])
    return [
        jnp.concatenate([value[j : j + 1] for j in range(TILE // 128)], axis=1) for value in values
    ]


def tile_step(t, cells_ref, fields, make, source_ref, split=False):
    row, col = cells_of(cells_ref, t)
    hot_col = one_hot(col, CY)
    mask = matches(row, CX)
    if split:
        lines = jnp.dot(fields, hot_col, preferred_element_type=F32)
        sample_x, sample_y = (
            jnp.sum(
                jnp.where(mask, lines[k : k + CX] + lines[k + CX : k + 2 * CX], 0.0),
                axis=0,
                keepdims=True,
            )
            for k in (0, 2 * CX)
        )
    else:
        sample_x, sample_y = sampled(t, cells_ref, fields)
    product = make()
    reads = product(0, 8)
    current_x = reads[0:1] + sample_x * reads[2:3] + sample_y * reads[4:5]
    current_y = reads[1:2] + sample_x * reads[3:4] + sample_y * reads[5:6]
    marked = [
        jnp.where(mask, part.astype(F32), 0.0).astype(BF16)
        for current in (current_x, current_y)
        for part in halves(current)
    ]
    if not split:
        source_ref[...] += fast_nt(jnp.concatenate(marked, axis=0), hot_col)
    groups = []
    for k in range(4):
        if split:
            source_ref[k * CX : (k + 1) * CX] += fast_nt(marked[k], hot_col)
        for q in range(4 * k, 4 * k + 4):
            base = 16 + 48 * q
            groups.append(
                product(base, 16)
                + sample_x * product(base + 16, 16)
                + sample_y * product(base + 32, 16)
            )
    return jnp.concatenate(groups, axis=0)


def split_fields(ex, ey):
    xh, xl = halves(ex)
    yh, yl = halves(ey)
    return jnp.concatenate([xh, xl, yh, yl], axis=0)


def save_state(state_ref, t, updated):
    hi, lo = halves(updated.T)
    state_ref[tile_rows(t), 0:S2] = hi
    state_ref[tile_rows(t), S2:] = lo


def rows_of(value):
    return lambda start, size: value[start : start + size]


def stored_product(table_ref, state_ref, t):
    hi, lo = state_ref[tile_rows(t), 0:S2], state_ref[tile_rows(t), S2:]
    return fast_nt(table_ref[...], jnp.concatenate([hi, lo, hi], axis=1))


def first_kernel(
    live_ref, cells_ref, ex_ref, ey_ref, table_ref, hi_ref, lo_ref, state_ref, acc
):
    acc[...] = jnp.zeros_like(acc)

    def body(t):
        hi, lo = hi_ref[tile_rows(t), :], lo_ref[tile_rows(t), :]

        def make():
            return rows_of(fast_nt(table_ref[...], jnp.concatenate([hi, lo, hi], axis=1)))

        save_state(state_ref, t, tile_step(t, cells_ref, (ex_ref, ey_ref), make, acc))

    sweep(0, count_of(live_ref), body)


def ahead_kernel(live_ref, table_ref, state_ref, after_ref, product_ref):
    def body(t):
        product_ref[:, tile_rows(t)] = stored_product(table_ref, state_ref, t)

    sweep(0, count_of(live_ref), body)


def turned(value):
    rows, lanes = value.shape
    if rows < 128:
        value = jnp.concatenate([value, jnp.zeros((128 - rows, lanes), F32)], axis=0)
    elif rows < 256:
        value = jnp.concatenate([value, jnp.zeros((256 - rows, lanes), F32)], axis=0)
    return value.T


def ordered(axis, one_ref, two_ref):
    is_even = even(axis)
    one, two = one_ref[...], two_ref[...]
    return jnp.where(is_even, two, one), jnp.where(is_even, one, two)


def corner_kernel(
    ex_ref, ey_ref, mz_ref, west_ref, east_ref, one_ref, two_ref, after_ref, to_one_ref, to_two_ref
):
    tops, bottoms = ordered("gx", one_ref, two_ref)
    packages = []
    lane = lax.broadcasted_iota(jnp.int32, (TALL, 128), 1)
    for side, coefs_ref in ((0, west_ref), (1, east_ref)):
        half = slice(128 * side, 128 * side + 128)

        def tall(k, field_ref):
            rows = slice(8 * k, 8 * k + 8)
            return jnp.concatenate([tops[rows, half], field_ref[:, half], bottoms[rows, half]], axis=0)

        shift = 8 * side
        m = tall(0, mz_ref)
        if shift:
            m = pltpu.roll(m, shift, 1)
        x = pltpu.roll(tall(1, ex_ref), 8 + shift, 1)
        y = pltpu.roll(tall(2, ey_ref), 16 + shift, 1)
        items = jnp.where(lane < 8, m, jnp.where(lane < 16, x, y))
        coefs = coefs_ref[...]
        wide = pltpu.roll(jnp.concatenate([coefs, jnp.zeros_like(coefs)], axis=1), 8, 1)
        lower = wide[:, 0:128]
        upper = wide[:, 128:256]
        place = lax.broadcasted_iota(jnp.int32, (32, 128), 1)
        gap = jnp.zeros((16, 128), F32)

        def both(lines, near_from, far_from, near_to, far_to, base):
            near = lines[24:48, half]
            far = lines[48:56, half]
            at_near = jnp.concatenate(
                [
                    pltpu.roll(near, (near_to - near_from) % 128, 1),
                    pltpu.roll(near[0:8], (near_to - far_from) % 128, 1),
                ],
                axis=0,
            )
            at_far = jnp.concatenate(
                [
                    pltpu.roll(far, (far_to - near_from) % 128, 1),
                    gap,
                    pltpu.roll(far, (far_to - far_from) % 128, 1),
                ],
                axis=0,
            )
            return jnp.where(place == near_to, at_near, jnp.where(place == far_to, at_far, base))

        near_from, far_from = (127, 126) if side else (0, 1)
        spread = jnp.concatenate(
            [
                both(tops, near_from, far_from, 7, 6, lower),
                both(bottoms, near_from, far_from, 8, 9, upper),
            ],
            axis=1,
        )
        packages.append(jnp.concatenate([turned(items)[0:24], spread], axis=0))
    left, right = packages
    is_even = even("gy")
    to_one_ref[...] = jnp.where(is_even, right, left)
    to_two_ref[...] = jnp.where(is_even, left, right)


def linear(coefs, x, y):
    return (
        coefs[0:1] + x * coefs[2:3] + y * coefs[4:5],
        coefs[1:2] + x * coefs[3:4] + y * coefs[5:6],
    )


def quadratic(coefs, x0, y0, x1, y1):
    terms = [linear(coefs[FIRST * (c + 1) : FIRST * (c + 2)], x1, y1) for c in range(3)]
    return tuple(terms[0][k] + x0 * terms[1][k] + y0 * terms[2][k] for k in range(2))


def advance(x, y, z, source_x, source_y):
    y_next = pltpu.roll(y, TALL - 1, 0)
    x_next = pltpu.roll(x, WIDE - 1, 1)
    z = z - COURANT * ((y_next - y) - (x_next - x))
    x = x + COURANT * (z - pltpu.roll(z, 1, 1)) - source_x
    y = y - COURANT * (z - pltpu.roll(z, 1, 0)) - source_y
    return x, y, z


OWN = slice(128, 128 + CY)


def main_kernel(
    live_ref, cells_ref, ex_ref, ey_ref, mz_ref, acc_ref, table_ref, product_ref,
    row_one_ref, row_two_ref, col_one_ref, col_two_ref, dens_ref,
    evolved_ref, out_x, out_y, out_z, state, buf, acc, fld, xs, ys, zs, sems, parts,
):
    count = count_of(live_ref)
    total = dens_ref.shape[0] // TILE

    def fetch(t):
        return pltpu.make_async_copy(dens_ref.at[tile_rows(t), :], buf.at[tile_rows(t), :], sems.at[t])

    def write(t, c):
        rows = pl.ds(pl.multiple_of(t * TILE + c * PART, PART), PART)
        return pltpu.make_async_copy(buf.at[rows, :], evolved_ref.at[rows, :], parts.at[t, c])

    def write_all(t):
        for c in range(TILE // PART):
            write(t, c).start()

    def finish_all(t):
        for c in range(TILE // PART):
            write(t, c).wait()

    sweep(count, total, lambda t: fetch(t).start())

    tops, bottoms = ordered("gx", row_one_ref, row_two_ref)
    left, right = ordered("gy", col_one_ref, col_two_ref)
    left_items = turned(left[0:24])[0:TALL]
    right_items = turned(right[0:24])[0:TALL]

    def extended(k, field_ref):
        rows = slice(8 * k, 8 * k + 8)
        middle = jnp.concatenate([tops[rows, :], field_ref[...], bottoms[rows, :]], axis=0)
        before = pltpu.roll(left_items, 120 - 8 * k, 1)
        after = right_items
        if k:
            after = pltpu.roll(after, 128 - 8 * k, 1)
        return jnp.concatenate([before, middle, after], axis=1)

    zs[...] = extended(0, mz_ref)
    xs[...] = extended(1, ex_ref)
    ys[...] = extended(2, ey_ref)

    sides = []
    for package, near, far in ((left, 7, 6), (right, 0, 1)):
        lines = package[0:24]
        coefs = package[24:]
        near_x, near_y = lines[8 + near : 9 + near], lines[16 + near : 17 + near]
        far_x, far_y = lines[8 + far : 9 + far], lines[16 + far : 17 + far]
        sides.append(
            (
                coefs,
                near_x,
                near_y,
                linear(coefs[0:FIRST], near_x, near_y),
                linear(coefs[ORDERS : ORDERS + FIRST], far_x, far_y),
            )
        )
    lane = lax.broadcasted_iota(jnp.int32, (TALL, 128), 1)
    line = lax.broadcasted_iota(jnp.int32, (8, CY), 0)

    def assembled(tops, rows, bottoms, before, after):
        middle = jnp.concatenate([tops, rows, bottoms], axis=0)
        return jnp.concatenate([before, middle, after], axis=1)

    (lc, lx0, ly0, lnear, lfar), (rc, rx0, ry0, rnear, rfar) = sides
    columns = turned(
        jnp.concatenate(
            [lfar[0], lnear[0], lfar[1], lnear[1], rnear[0], rfar[0], rnear[1], rfar[1]], axis=0
        )
    )[0:TALL]
    zero_line = jnp.zeros((8, CY), F32)
    starts = []
    top_lines = []
    bottom_lines = []
    for lines_of, near, far, out in (
        (tops, 7, 6, top_lines),
        (bottoms, 0, 1, bottom_lines),
    ):
        near_x, near_y = lines_of[8 + near : 9 + near, :], lines_of[16 + near : 17 + near, :]
        far_x, far_y = lines_of[8 + far : 9 + far, :], lines_of[16 + far : 17 + far, :]
        starts.append((near_x, near_y))
        at_near = linear(lines_of[24 : 24 + FIRST, :], near_x, near_y)
        at_far = linear(lines_of[48 : 48 + FIRST, :], far_x, far_y)
        for k in range(2):
            out.append(
                jnp.where(line == near, at_near[k], jnp.where(line == far, at_far[k], zero_line))
            )

    def own(ref, k):
        return ref[2 * k * CX : (2 * k + 1) * CX] + ref[(2 * k + 1) * CX : (2 * k + 2) * CX]

    sources = []
    for k in range(2):
        before = jnp.where(lane >= 126, pltpu.roll(columns, 126 - 2 * k, 1), 0.0)
        after = jnp.where(lane < 2, pltpu.roll(columns, 124 - 2 * k, 1), 0.0)
        sources.append(assembled(top_lines[k], own(acc_ref, k), bottom_lines[k], before, after))
    x, y, z = advance(xs[...], ys[...], zs[...], *sources)
    xs[...] = x
    ys[...] = y
    zs[...] = z

    def flush(t):
        fetch(t).wait()
        write_all(t)

    sweep(count, total, flush)

    fields = [ref.at[pl.ds(8, CX), pl.ds(128, CY)] for ref in (xs, ys)]
    fld[...] = split_fields(*(field[...] for field in fields))
    acc[...] = jnp.zeros_like(acc)

    def second(t):
        def make():
            return lambda start, size: product_ref[start : start + size, tile_rows(t)]

        save_state(state, t, tile_step(t, cells_ref, fld[...], make, acc, True))

    sweep(0, count, second)

    x = xs[...]
    y = ys[...]
    xl, yl = x[:, 0:128], y[:, 0:128]
    xr, yr = x[:, 384:512], y[:, 384:512]
    edge = jnp.where(
        lane == 127,
        xl,
        jnp.where(
            lane == 126,
            pltpu.roll(yl, 127, 1),
            jnp.where(lane == 0, xr, jnp.where(lane == 1, pltpu.roll(yr, 1, 1), 0.0)),
        ),
    )
    rows = turned(edge)
    ends_l = quadratic(lc, lx0, ly0, rows[127:128], rows[126:127])
    ends_r = quadratic(rc, rx0, ry0, rows[0:1], rows[1:2])
    columns = turned(
        jnp.concatenate([ends_l[0], ends_l[1], ends_r[0], ends_r[1], jnp.zeros((4, CY), F32)], axis=0)
    )[0:TALL]
    lines = []
    for (x0, y0), lines_of, near, at in (
        (starts[0], tops, 7, 7),
        (starts[1], bottoms, 0, 8 + CX),
    ):
        ends = quadratic(
            lines_of[24:48, :], x0, y0, x[at : at + 1, OWN], y[at : at + 1, OWN]
        )
        lines.append([jnp.where(line == near, ends[k], zero_line) for k in range(2)])
    sources = []
    for k in range(2):
        before = jnp.where(lane == 127, pltpu.roll(columns, 127 - k, 1), 0.0)
        after = jnp.where(lane == 0, pltpu.roll(columns, 126 - k, 1), 0.0)
        sources.append(assembled(lines[0][k], own(acc, k), lines[1][k], before, after))
    x, y, z = advance(x, y, zs[...], *sources)
    xs[...] = x
    ys[...] = y
    zs[...] = z
    acc[...] = jnp.zeros_like(acc)

    def third(t):
        def make():
            return rows_of(stored_product(table_ref, state, t))

        updated = tile_step(t, cells_ref, fields, make, acc)
        for c in range(TILE // PART):
            rows = pl.ds(pl.multiple_of(t * TILE + c * PART, PART), PART)
            buf[rows, :] = updated[:, c * PART : (c + 1) * PART].T
            write(t, c).start()

    sweep(0, count, third)
    blank = jnp.zeros((TALL, 128), F32)
    sources = [assembled(zero_line, own(acc, k), zero_line, blank, blank) for k in range(2)]
    x, y, z = advance(xs[...], ys[...], zs[...], *sources)
    xs[8 : 8 + CX, OWN] = x[8 : 8 + CX, OWN]
    ys[8 : 8 + CX, OWN] = y[8 : 8 + CX, OWN]
    zs[8 : 8 + CX, OWN] = z[8 : 8 + CX, OWN]
    saves = [
        pltpu.make_async_copy(src.at[pl.ds(8, CX), pl.ds(128, CY)], dst, sems.at[total + k])
        for k, (src, dst) in enumerate(((xs, out_x), (ys, out_y), (zs, out_z)))
    ]
    for save in saves:
        save.start()
    sweep(0, total, finish_all)
    for save in saves:
        save.wait()


VMEM = pl.BlockSpec(memory_space=pltpu.VMEM)
SMEM = pl.BlockSpec(memory_space=pltpu.SMEM)
ANY = pl.BlockSpec(memory_space=pl.ANY)
LIMITS = pltpu.CompilerParams(vmem_limit_bytes=40 << 20)


def shaped(shape, dtype=F32):
    return jax.ShapeDtypeStruct(shape, dtype)


def pairs(axis, first):
    count = lax.axis_size(axis)
    swaps = [(i % count, (i + 1) % count) for i in range(first, first + count, 2)]
    return swaps + [(b, a) for a, b in swaps]


def pinned(value):
    return pltpu.with_memory_space_constraint(value, pltpu.VMEM)


def streamed(value):
    return pltpu.with_memory_space_constraint(value, pltpu.HBM)


def held(shape, dtype=F32):
    return pltpu.VMEM(shape, dtype)


def shards(density, cell_index, live_batches, propagator, dipoles, ex, ey, mz):
    slots = density.shape[0]
    tiles = slots // TILE
    cells = cell_index.reshape(slots // 128, 128)
    buffer = pltpu.VMEM((slots, S2), F32)
    sems = pltpu.SemaphoreType.DMA((tiles + 3,))
    sums = (4 * CX, CY)
    half = held((slots, S2), BF16)
    readout, one, two, west, east, hi, lo = pl.pallas_call(
        coefficient_kernel,
        out_shape=(
            shaped((8, S2)),
            shaped((LINES, CY)),
            shaped((LINES, CY)),
            shaped((32, CX)),
            shaped((32, CX)),
            half,
            half,
        ),
        in_specs=[SMEM] + [ANY] * 7,
        out_specs=(VMEM,) * 7,
        scratch_shapes=[
            buffer,
            pltpu.VMEM((128, CY), F32),
            pltpu.VMEM((128, CX), F32),
            pltpu.VMEM(propagator.shape, F32),
            pltpu.VMEM(dipoles.shape, F32),
            pltpu.VMEM(cells.shape, jnp.int32),
            pltpu.SemaphoreType.DMA((slots // SMALL,)),
            pltpu.SemaphoreType.DMA((9,)),
        ],
        compiler_params=LIMITS,
        name="coefficients",
    )(
        live_batches,
        *(streamed(value) for value in (cells, ex, ey, mz, propagator, dipoles, density)),
    )
    row_one = lax.ppermute(one, "gx", pairs("gx", 0))
    row_two = lax.ppermute(two, "gx", pairs("gx", 1))
    table = pl.pallas_call(
        table_kernel,
        out_shape=held((ROWS, 3 * S2), BF16),
        in_specs=[VMEM] * 2,
        out_specs=VMEM,
        compiler_params=LIMITS,
        name="table",
    )(propagator, readout)
    state, source = pl.pallas_call(
        first_kernel,
        out_shape=(held((slots, 2 * S2), BF16), held(sums)),
        in_specs=[SMEM] + [VMEM] * 6,
        out_specs=(VMEM,) * 2,
        compiler_params=LIMITS,
        name="first",
    )(live_batches, cells, ex, ey, pinned(table), pinned(hi), pinned(lo))
    package = held((LINES, CY))
    to_one, to_two = pl.pallas_call(
        corner_kernel,
        out_shape=(package, package),
        in_specs=[VMEM] * 5 + [VMEM] * 2 + [ANY],
        out_specs=(VMEM,) * 2,
        compiler_params=LIMITS,
        name="corners",
    )(ex, ey, mz, west, east, pinned(row_one), pinned(row_two), pinned(source))
    col_one = lax.ppermute(to_one, "gy", pairs("gy", 0))
    col_two = lax.ppermute(to_two, "gy", pairs("gy", 1))
    product = pl.pallas_call(
        ahead_kernel,
        out_shape=held((ROWS, slots)),
        in_specs=[SMEM] + [VMEM] * 2 + [ANY],
        out_specs=VMEM,
        compiler_params=LIMITS,
        name="ahead",
    )(live_batches, pinned(table), pinned(state), pinned(to_one))
    field = shaped((CX, CY))
    tall = pltpu.VMEM((TALL, WIDE), F32)
    return pl.pallas_call(
        main_kernel,
        out_shape=(shaped((slots, S2)), field, field, field),
        in_specs=[SMEM] + [VMEM] * 11 + [ANY],
        out_specs=(ANY,) * 4,
        scratch_shapes=[
            pltpu.VMEM((slots, 2 * S2), BF16), buffer, pltpu.VMEM(sums, F32), pltpu.VMEM(sums, BF16),
            tall, tall, tall, sems, pltpu.SemaphoreType.DMA((tiles, TILE // PART)),
        ],
        compiler_params=LIMITS,
        name="main",
    )(
        live_batches, cells, ex, ey, mz, pinned(source), pinned(table), pinned(product),
        pinned(row_one), pinned(row_two), pinned(col_one), pinned(col_two), streamed(density),
    )


def solution(mesh):
    placed = (
        P(("gx", "gy"), None),
        P(("gx", "gy")),
        P(("gx", "gy")),
        P(),
        P(),
        P("gx", "gy"),
        P("gx", "gy"),
        P("gx", "gy"),
    )
    return jax.shard_map(
        shards,
        mesh=mesh,
        in_specs=placed,
        out_specs=(P(("gx", "gy"), None), P("gx", "gy"), P("gx", "gy"), P("gx", "gy")),
        check_vma=False,
    )
```

```python
import jax
import jax.numpy as jnp
from jax import lax
from jax.experimental import pallas as pl
from jax.experimental.pallas import tpu as pltpu
from jax.sharding import PartitionSpec as P

BATCH = 64
STEPS = 3
TILE = 1024
SMALL = 1024
PART = 256
COURANT = 0.5
CX = 128
CY = 256
S2 = 256
ROWS = 3 * S2 + 16
FIRST = 6
ORDERS = 24
LINES = 56
TALL = CX + 16
WIDE = CY + 256
F32 = jnp.float32
BF16 = jnp.bfloat16
NT = (((1,), (1,)), ((), ()))


def halves(x):
    hi = x.astype(BF16)
    return hi, (x - hi.astype(F32)).astype(BF16)


def fast_nt(a, b):
    return lax.dot_general(a, b, NT, preferred_element_type=F32)


def functionals_of(prop_ref, dip_ref):
    blocks = [halves(prop_ref[:, b * S2 : (b + 1) * S2]) for b in range(3)]

    def through(value, block):
        rows = value.shape[0]
        vh, vl = halves(value)
        wide = fast_nt(jnp.concatenate([vh, vl], axis=0), block[0])
        return wide[0:rows] + wide[rows:] + fast_nt(vh, block[1])

    dipoles = dip_ref[...]
    padded = jnp.concatenate([dipoles, jnp.zeros((6, S2), F32)], axis=0)
    reads = [through(padded, block)[0:2] for block in blocks]
    first = jnp.concatenate(
        [reads[0] - dipoles, reads[1], reads[2], jnp.zeros((2, S2), F32)], axis=0
    )
    second = [through(first, block)[0:FIRST] for block in blocks]
    return jnp.concatenate([first[0:FIRST], *second, jnp.zeros((8, S2), F32)], axis=0)


def table_kernel(prop_ref, readout_ref, table_ref):
    def put(rows, value):
        hi, lo = halves(value)
        table_ref[rows, 0:S2] = hi
        table_ref[rows, S2 : 2 * S2] = hi
        table_ref[rows, 2 * S2 :] = lo

    put(pl.ds(0, 16), jnp.concatenate([readout_ref[...], jnp.zeros((8, S2), F32)], axis=0))
    for b in range(3):
        block = prop_ref[:, b * S2 : (b + 1) * S2].T
        for q in range(S2 // 16):
            put(pl.ds(16 + 48 * q + 16 * b, 16), block[16 * q : 16 * q + 16])


def even(axis):
    return lax.axis_index(axis) % 2 == 0


def cells_of(cells_ref, t, size=TILE):
    cell = jnp.concatenate(
        [cells_ref[pl.ds(t * (size // 128) + j, 1), :] for j in range(size // 128)], axis=1
    )
    return cell >> 8, cell & (CY - 1)


def matches(index, size):
    return lax.broadcasted_iota(jnp.int32, (size, index.shape[1]), 0) == index


def one_hot(index, size):
    return jnp.where(matches(index, size), 1.0, 0.0).astype(BF16)


def count_of(live_ref, size=TILE):
    return live_ref[0] * BATCH // size


def tile_rows(t, size=TILE):
    return pl.ds(pl.multiple_of(t * size, size), size)


def sweep(lower, upper, body):
    def wrapped(t, carry):
        body(t)
        return carry

    lax.fori_loop(lower, upper, wrapped, 0)


def coefficient_kernel(
    live_ref, cells_hbm, ex_hbm, ey_hbm, mz_hbm, prop_hbm, dip_hbm, dens_hbm,
    readout_ref, one_ref, two_ref, west_ref, east_ref, hi_ref, lo_ref,
    prop_ref, cells_ref, buf, by_row, by_col, dip_ref, sems, loads,
):
    count = count_of(live_ref, SMALL)

    def copy(t):
        return pltpu.make_async_copy(dens_hbm.at[tile_rows(t, SMALL), :], buf.at[tile_rows(t, SMALL), :], sems.at[t])

    pairs = [(dip_hbm, dip_ref), (prop_hbm, prop_ref), (cells_hbm, cells_ref)]
    is_even = even("gx")
    starts = (jnp.where(is_even, CX - 8, 0), jnp.where(is_even, 0, CX - 8))
    for ref, start in zip((one_ref, two_ref), starts):
        start = pl.multiple_of(start, 8)
        for k, field in enumerate((mz_hbm, ex_hbm, ey_hbm)):
            pairs.append((field.at[pl.ds(start, 8), :], ref.at[pl.ds(8 * k, 8), :]))
    moves = [pltpu.make_async_copy(src, dst, loads.at[k]) for k, (src, dst) in enumerate(pairs)]
    for move in moves[:3]:
        move.start()
    sweep(0, count, lambda t: copy(t).start())
    for move in moves[3:]:
        move.start()
    for move in moves[:2]:
        move.wait()
    functionals = functionals_of(prop_ref, dip_ref)
    readout_ref[...] = functionals[0:8]
    fh, fl = halves(functionals)
    stacked = jnp.concatenate([fh, fl], axis=0)
    by_row[...] = jnp.zeros_like(by_row)
    by_col[...] = jnp.zeros_like(by_col)

    def picked(index, near, far, parts):
        out = []
        for place, rows in ((near[0], ORDERS), (near[1], ORDERS), (far[0], 8), (far[1], 8)):
            for part in parts:
                out.append(jnp.where(index == place, part[0:rows], 0.0))
        return jnp.concatenate(out, axis=0).astype(BF16)

    def body(t):
        copy(t).wait()
        dh, dl = halves(buf[tile_rows(t, SMALL), :])
        hi_ref[tile_rows(t, SMALL), :] = dh
        lo_ref[tile_rows(t, SMALL), :] = dl
        wide = fast_nt(stacked, dh)
        values = wide[0:32] + wide[32:64] + fast_nt(fh, dl)
        vh, vl = halves(values)
        parts = (vh.astype(F32), vl.astype(F32))
        row, col = cells_of(cells_ref, t, SMALL)
        by_row[...] += fast_nt(picked(row, (0, CX - 1), (1, CX - 2), parts), one_hot(col, CY))
        by_col[...] += fast_nt(picked(col, (0, CY - 1), (1, CY - 2), parts), one_hot(row, CX))

    for move in moves[2:]:
        move.wait()
    sweep(0, count, body)

    def side(ref, which):
        near = 2 * ORDERS * which
        far = 4 * ORDERS + 16 * which
        return (
            ref[near : near + ORDERS] + ref[near + ORDERS : near + 2 * ORDERS],
            ref[far : far + 8] + ref[far + 8 : far + 16],
        )

    low, high = side(by_row, 0), side(by_row, 1)
    for ref, if_even, if_odd in ((one_ref, high, low), (two_ref, low, high)):
        ref[24:48] = jnp.where(is_even, if_even[0], if_odd[0])
        ref[48:56] = jnp.where(is_even, if_even[1], if_odd[1])
    for which, ref in ((0, west_ref), (1, east_ref)):
        near, far = side(by_col, which)
        ref[0:ORDERS] = near
        ref[ORDERS:] = far


def sampled(t, cells_ref, fields):
    cell = cells_ref[pl.ds(pl.multiple_of(t * (TILE // 128), 8), TILE // 128), :]
    lane = cell & 127
    strip = cell >> 7
    values = [jnp.zeros(cell.shape, F32) for _ in fields]
    for r in range(CX):
        for half in range(CY // 128):
            here = strip == r * (CY // 128) + half
            for k, field in enumerate(fields):
                line = jnp.broadcast_to(field[r : r + 1, 128 * half : 128 * half + 128], cell.shape)
                found = jnp.take_along_axis(line, lane, axis=1)
                values[k] = jnp.where(here, found, values[k])
    return [
        jnp.concatenate([value[j : j + 1] for j in range(TILE // 128)], axis=1) for value in values
    ]


def tile_step(t, cells_ref, fields, make, source_ref, split=False):
    row, col = cells_of(cells_ref, t)
    hot_col = one_hot(col, CY)
    mask = matches(row, CX)
    if split:
        lines = jnp.dot(fields, hot_col, preferred_element_type=F32)
        sample_x, sample_y = (
            jnp.sum(
                jnp.where(mask, lines[k : k + CX] + lines[k + CX : k + 2 * CX], 0.0),
                axis=0,
                keepdims=True,
            )
            for k in (0, 2 * CX)
        )
    else:
        sample_x, sample_y = sampled(t, cells_ref, fields)
    product = make()
    reads = product(0, 8)
    current_x = reads[0:1] + sample_x * reads[2:3] + sample_y * reads[4:5]
    current_y = reads[1:2] + sample_x * reads[3:4] + sample_y * reads[5:6]
    marked = [
        jnp.where(mask, part.astype(F32), 0.0).astype(BF16)
        for current in (current_x, current_y)
        for part in halves(current)
    ]
    if not split:
        source_ref[...] += fast_nt(jnp.concatenate(marked, axis=0), hot_col)
    groups = []
    for k in range(4):
        if split:
            source_ref[k * CX : (k + 1) * CX] += fast_nt(marked[k], hot_col)
        for q in range(4 * k, 4 * k + 4):
            base = 16 + 48 * q
            groups.append(
                product(base, 16)
                + sample_x * product(base + 16, 16)
                + sample_y * product(base + 32, 16)
            )
    return jnp.concatenate(groups, axis=0)


def split_fields(ex, ey):
    xh, xl = halves(ex)
    yh, yl = halves(ey)
    return jnp.concatenate([xh, xl, yh, yl], axis=0)


def save_state(state_ref, t, updated):
    hi, lo = halves(updated.T)
    state_ref[tile_rows(t), 0:S2] = hi
    state_ref[tile_rows(t), S2:] = lo


def rows_of(value):
    return lambda start, size: value[start : start + size]


def stored_product(table_ref, state_ref, t):
    hi, lo = state_ref[tile_rows(t), 0:S2], state_ref[tile_rows(t), S2:]
    return fast_nt(table_ref[...], jnp.concatenate([hi, lo, hi], axis=1))


def first_kernel(
    live_ref, cells_ref, ex_ref, ey_ref, table_ref, hi_ref, lo_ref, state_ref, acc
):
    acc[...] = jnp.zeros_like(acc)

    def body(t):
        hi, lo = hi_ref[tile_rows(t), :], lo_ref[tile_rows(t), :]

        def make():
            return rows_of(fast_nt(table_ref[...], jnp.concatenate([hi, lo, hi], axis=1)))

        save_state(state_ref, t, tile_step(t, cells_ref, (ex_ref, ey_ref), make, acc))

    sweep(0, count_of(live_ref), body)


def ahead_kernel(live_ref, table_ref, state_ref, after_ref, product_ref):
    def body(t):
        product_ref[:, tile_rows(t)] = stored_product(table_ref, state_ref, t)

    sweep(0, count_of(live_ref), body)


def turned(value):
    rows, lanes = value.shape
    if rows < 128:
        value = jnp.concatenate([value, jnp.zeros((128 - rows, lanes), F32)], axis=0)
    elif rows < 256:
        value = jnp.concatenate([value, jnp.zeros((256 - rows, lanes), F32)], axis=0)
    return value.T


def ordered(axis, one_ref, two_ref):
    is_even = even(axis)
    one, two = one_ref[...], two_ref[...]
    return jnp.where(is_even, two, one), jnp.where(is_even, one, two)


def corner_kernel(
    ex_ref, ey_ref, mz_ref, west_ref, east_ref, one_ref, two_ref, after_ref, to_one_ref, to_two_ref
):
    tops, bottoms = ordered("gx", one_ref, two_ref)
    packages = []
    lane = lax.broadcasted_iota(jnp.int32, (TALL, 128), 1)
    for side, coefs_ref in ((0, west_ref), (1, east_ref)):
        half = slice(128 * side, 128 * side + 128)

        def tall(k, field_ref):
            rows = slice(8 * k, 8 * k + 8)
            return jnp.concatenate([tops[rows, half], field_ref[:, half], bottoms[rows, half]], axis=0)

        shift = 8 * side
        m = tall(0, mz_ref)
        if shift:
            m = pltpu.roll(m, shift, 1)
        x = pltpu.roll(tall(1, ex_ref), 8 + shift, 1)
        y = pltpu.roll(tall(2, ey_ref), 16 + shift, 1)
        items = jnp.where(lane < 8, m, jnp.where(lane < 16, x, y))
        coefs = coefs_ref[...]
        wide = pltpu.roll(jnp.concatenate([coefs, jnp.zeros_like(coefs)], axis=1), 8, 1)
        lower = wide[:, 0:128]
        upper = wide[:, 128:256]
        place = lax.broadcasted_iota(jnp.int32, (32, 128), 1)
        gap = jnp.zeros((16, 128), F32)

        def both(lines, near_from, far_from, near_to, far_to, base):
            near = lines[24:48, half]
            far = lines[48:56, half]
            at_near = jnp.concatenate(
                [
                    pltpu.roll(near, (near_to - near_from) % 128, 1),
                    pltpu.roll(near[0:8], (near_to - far_from) % 128, 1),
                ],
                axis=0,
            )
            at_far = jnp.concatenate(
                [
                    pltpu.roll(far, (far_to - near_from) % 128, 1),
                    gap,
                    pltpu.roll(far, (far_to - far_from) % 128, 1),
                ],
                axis=0,
            )
            return jnp.where(place == near_to, at_near, jnp.where(place == far_to, at_far, base))

        near_from, far_from = (127, 126) if side else (0, 1)
        spread = jnp.concatenate(
            [
                both(tops, near_from, far_from, 7, 6, lower),
                both(bottoms, near_from, far_from, 8, 9, upper),
            ],
            axis=1,
        )
        packages.append(jnp.concatenate([turned(items)[0:24], spread], axis=0))
    left, right = packages
    is_even = even("gy")
    to_one_ref[...] = jnp.where(is_even, right, left)
    to_two_ref[...] = jnp.where(is_even, left, right)


def linear(coefs, x, y):
    return (
        coefs[0:1] + x * coefs[2:3] + y * coefs[4:5],
        coefs[1:2] + x * coefs[3:4] + y * coefs[5:6],
    )


def quadratic(coefs, x0, y0, x1, y1):
    terms = [linear(coefs[FIRST * (c + 1) : FIRST * (c + 2)], x1, y1) for c in range(3)]
    return tuple(terms[0][k] + x0 * terms[1][k] + y0 * terms[2][k] for k in range(2))


def advance(x, y, z, source_x, source_y):
    y_next = pltpu.roll(y, TALL - 1, 0)
    x_next = pltpu.roll(x, WIDE - 1, 1)
    z = z - COURANT * ((y_next - y) - (x_next - x))
    x = x + COURANT * (z - pltpu.roll(z, 1, 1)) - source_x
    y = y - COURANT * (z - pltpu.roll(z, 1, 0)) - source_y
    return x, y, z


OWN = slice(128, 128 + CY)


def main_kernel(
    live_ref, cells_ref, ex_ref, ey_ref, mz_ref, acc_ref, table_ref, product_ref,
    row_one_ref, row_two_ref, col_one_ref, col_two_ref, dens_ref,
    evolved_ref, out_x, out_y, out_z, state, buf, acc, fld, xs, ys, zs, sems, parts,
):
    count = count_of(live_ref)
    total = dens_ref.shape[0] // TILE

    def fetch(t):
        return pltpu.make_async_copy(dens_ref.at[tile_rows(t), :], buf.at[tile_rows(t), :], sems.at[t])

    def write(t, c):
        rows = pl.ds(pl.multiple_of(t * TILE + c * PART, PART), PART)
        return pltpu.make_async_copy(buf.at[rows, :], evolved_ref.at[rows, :], parts.at[t, c])

    def write_all(t):
        for c in range(TILE // PART):
            write(t, c).start()

    def finish_all(t):
        for c in range(TILE // PART):
            write(t, c).wait()

    sweep(count, total, lambda t: fetch(t).start())

    tops, bottoms = ordered("gx", row_one_ref, row_two_ref)
    left, right = ordered("gy", col_one_ref, col_two_ref)
    left_items = turned(left[0:24])[0:TALL]
    right_items = turned(right[0:24])[0:TALL]

    def extended(k, field_ref):
        rows = slice(8 * k, 8 * k + 8)
        middle = jnp.concatenate([tops[rows, :], field_ref[...], bottoms[rows, :]], axis=0)
        before = pltpu.roll(left_items, 120 - 8 * k, 1)
        after = right_items
        if k:
            after = pltpu.roll(after, 128 - 8 * k, 1)
        return jnp.concatenate([before, middle, after], axis=1)

    zs[...] = extended(0, mz_ref)
    xs[...] = extended(1, ex_ref)
    ys[...] = extended(2, ey_ref)

    sides = []
    for package, near, far in ((left, 7, 6), (right, 0, 1)):
        lines = package[0:24]
        coefs = package[24:]
        near_x, near_y = lines[8 + near : 9 + near], lines[16 + near : 17 + near]
        far_x, far_y = lines[8 + far : 9 + far], lines[16 + far : 17 + far]
        sides.append(
            (
                coefs,
                near_x,
                near_y,
                linear(coefs[0:FIRST], near_x, near_y),
                linear(coefs[ORDERS : ORDERS + FIRST], far_x, far_y),
            )
        )
    lane = lax.broadcasted_iota(jnp.int32, (TALL, 128), 1)
    line = lax.broadcasted_iota(jnp.int32, (8, CY), 0)

    def assembled(tops, rows, bottoms, before, after):
        middle = jnp.concatenate([tops, rows, bottoms], axis=0)
        return jnp.concatenate([before, middle, after], axis=1)

    (lc, lx0, ly0, lnear, lfar), (rc, rx0, ry0, rnear, rfar) = sides
    columns = turned(
        jnp.concatenate(
            [lfar[0], lnear[0], lfar[1], lnear[1], rnear[0], rfar[0], rnear[1], rfar[1]], axis=0
        )
    )[0:TALL]
    zero_line = jnp.zeros((8, CY), F32)
    starts = []
    top_lines = []
    bottom_lines = []
    for lines_of, near, far, out in (
        (tops, 7, 6, top_lines),
        (bottoms, 0, 1, bottom_lines),
    ):
        near_x, near_y = lines_of[8 + near : 9 + near, :], lines_of[16 + near : 17 + near, :]
        far_x, far_y = lines_of[8 + far : 9 + far, :], lines_of[16 + far : 17 + far, :]
        starts.append((near_x, near_y))
        at_near = linear(lines_of[24 : 24 + FIRST, :], near_x, near_y)
        at_far = linear(lines_of[48 : 48 + FIRST, :], far_x, far_y)
        for k in range(2):
            out.append(
                jnp.where(line == near, at_near[k], jnp.where(line == far, at_far[k], zero_line))
            )

    def own(ref, k):
        return ref[2 * k * CX : (2 * k + 1) * CX] + ref[(2 * k + 1) * CX : (2 * k + 2) * CX]

    sources = []
    for k in range(2):
        before = jnp.where(lane >= 126, pltpu.roll(columns, 126 - 2 * k, 1), 0.0)
        after = jnp.where(lane < 2, pltpu.roll(columns, 124 - 2 * k, 1), 0.0)
        sources.append(assembled(top_lines[k], own(acc_ref, k), bottom_lines[k], before, after))
    x, y, z = advance(xs[...], ys[...], zs[...], *sources)
    xs[...] = x
    ys[...] = y
    zs[...] = z

    def flush(t):
        fetch(t).wait()
        write_all(t)

    sweep(count, total, flush)

    fields = [ref.at[pl.ds(8, CX), pl.ds(128, CY)] for ref in (xs, ys)]
    fld[...] = split_fields(*(field[...] for field in fields))
    acc[...] = jnp.zeros_like(acc)

    def second(t):
        def make():
            return lambda start, size: product_ref[start : start + size, tile_rows(t)]

        save_state(state, t, tile_step(t, cells_ref, fld[...], make, acc, True))

    sweep(0, count, second)

    x = xs[...]
    y = ys[...]
    xl, yl = x[:, 0:128], y[:, 0:128]
    xr, yr = x[:, 384:512], y[:, 384:512]
    edge = jnp.where(
        lane == 127,
        xl,
        jnp.where(
            lane == 126,
            pltpu.roll(yl, 127, 1),
            jnp.where(lane == 0, xr, jnp.where(lane == 1, pltpu.roll(yr, 1, 1), 0.0)),
        ),
    )
    rows = turned(edge)
    ends_l = quadratic(lc, lx0, ly0, rows[127:128], rows[126:127])
    ends_r = quadratic(rc, rx0, ry0, rows[0:1], rows[1:2])
    columns = turned(
        jnp.concatenate([ends_l[0], ends_l[1], ends_r[0], ends_r[1], jnp.zeros((4, CY), F32)], axis=0)
    )[0:TALL]
    lines = []
    for (x0, y0), lines_of, near, at in (
        (starts[0], tops, 7, 7),
        (starts[1], bottoms, 0, 8 + CX),
    ):
        ends = quadratic(
            lines_of[24:48, :], x0, y0, x[at : at + 1, OWN], y[at : at + 1, OWN]
        )
        lines.append([jnp.where(line == near, ends[k], zero_line) for k in range(2)])
    sources = []
    for k in range(2):
        before = jnp.where(lane == 127, pltpu.roll(columns, 127 - k, 1), 0.0)
        after = jnp.where(lane == 0, pltpu.roll(columns, 126 - k, 1), 0.0)
        sources.append(assembled(lines[0][k], own(acc, k), lines[1][k], before, after))
    x, y, z = advance(x, y, zs[...], *sources)
    xs[...] = x
    ys[...] = y
    zs[...] = z
    acc[...] = jnp.zeros_like(acc)

    def third(t):
        def make():
            return rows_of(stored_product(table_ref, state, t))

        updated = tile_step(t, cells_ref, fields, make, acc)
        for c in range(TILE // PART):
            rows = pl.ds(pl.multiple_of(t * TILE + c * PART, PART), PART)
            buf[rows, :] = updated[:, c * PART : (c + 1) * PART].T
            write(t, c).start()

    sweep(0, count, third)
    blank = jnp.zeros((TALL, 128), F32)
    sources = [assembled(zero_line, own(acc, k), zero_line, blank, blank) for k in range(2)]
    x, y, z = advance(xs[...], ys[...], zs[...], *sources)
    xs[8 : 8 + CX, OWN] = x[8 : 8 + CX, OWN]
    ys[8 : 8 + CX, OWN] = y[8 : 8 + CX, OWN]
    zs[8 : 8 + CX, OWN] = z[8 : 8 + CX, OWN]
    saves = [
        pltpu.make_async_copy(src.at[pl.ds(8, CX), pl.ds(128, CY)], dst, sems.at[total + k])
        for k, (src, dst) in enumerate(((xs, out_x), (ys, out_y), (zs, out_z)))
    ]
    for save in saves:
        save.start()
    sweep(0, total, finish_all)
    for save in saves:
        save.wait()


VMEM = pl.BlockSpec(memory_space=pltpu.VMEM)
SMEM = pl.BlockSpec(memory_space=pltpu.SMEM)
ANY = pl.BlockSpec(memory_space=pl.ANY)
LIMITS = pltpu.CompilerParams(vmem_limit_bytes=40 << 20)


def shaped(shape, dtype=F32):
    return jax.ShapeDtypeStruct(shape, dtype)


def pairs(axis, first):
    count = lax.axis_size(axis)
    swaps = [(i % count, (i + 1) % count) for i in range(first, first + count, 2)]
    return swaps + [(b, a) for a, b in swaps]


def pinned(value):
    return pltpu.with_memory_space_constraint(value, pltpu.VMEM)


def streamed(value):
    return pltpu.with_memory_space_constraint(value, pltpu.HBM)


def held(shape, dtype=F32):
    return pltpu.VMEM(shape, dtype)


def shards(density, cell_index, live_batches, propagator, dipoles, ex, ey, mz):
    slots = density.shape[0]
    tiles = slots // TILE
    cells = cell_index.reshape(slots // 128, 128)
    buffer = pltpu.VMEM((slots, S2), F32)
    sems = pltpu.SemaphoreType.DMA((tiles + 3,))
    sums = (4 * CX, CY)
    half = held((slots, S2), BF16)
    readout, one, two, west, east, hi, lo, fetched, places = pl.pallas_call(
        coefficient_kernel,
        out_shape=(
            shaped((8, S2)),
            shaped((LINES, CY)),
            shaped((LINES, CY)),
            shaped((32, CX)),
            shaped((32, CX)),
            half,
            half,
            held(propagator.shape),
            held(cells.shape, jnp.int32),
        ),
        in_specs=[SMEM] + [ANY] * 7,
        out_specs=(VMEM,) * 9,
        scratch_shapes=[
            buffer,
            pltpu.VMEM((128, CY), F32),
            pltpu.VMEM((128, CX), F32),
            pltpu.VMEM(dipoles.shape, F32),
            pltpu.SemaphoreType.DMA((slots // SMALL,)),
            pltpu.SemaphoreType.DMA((9,)),
        ],
        compiler_params=LIMITS,
        name="coefficients",
    )(
        live_batches,
        *(streamed(value) for value in (cells, ex, ey, mz, propagator, dipoles, density)),
    )
    row_one = lax.ppermute(one, "gx", pairs("gx", 0))
    row_two = lax.ppermute(two, "gx", pairs("gx", 1))
    table = pl.pallas_call(
        table_kernel,
        out_shape=held((ROWS, 3 * S2), BF16),
        in_specs=[VMEM] * 2,
        out_specs=VMEM,
        compiler_params=LIMITS,
        name="table",
    )(pinned(fetched), readout)
    state, source = pl.pallas_call(
        first_kernel,
        out_shape=(held((slots, 2 * S2), BF16), held(sums)),
        in_specs=[SMEM] + [VMEM] * 6,
        out_specs=(VMEM,) * 2,
        compiler_params=LIMITS,
        name="first",
    )(live_batches, pinned(places), ex, ey, pinned(table), pinned(hi), pinned(lo))
    package = held((LINES, CY))
    to_one, to_two = pl.pallas_call(
        corner_kernel,
        out_shape=(package, package),
        in_specs=[VMEM] * 5 + [VMEM] * 2 + [ANY],
        out_specs=(VMEM,) * 2,
        compiler_params=LIMITS,
        name="corners",
    )(ex, ey, mz, west, east, pinned(row_one), pinned(row_two), pinned(source))
    col_one = lax.ppermute(to_one, "gy", pairs("gy", 0))
    col_two = lax.ppermute(to_two, "gy", pairs("gy", 1))
    product = pl.pallas_call(
        ahead_kernel,
        out_shape=held((ROWS, slots)),
        in_specs=[SMEM] + [VMEM] * 2 + [ANY],
        out_specs=VMEM,
        compiler_params=LIMITS,
        name="ahead",
    )(live_batches, pinned(table), pinned(state), pinned(to_one))
    field = shaped((CX, CY))
    tall = pltpu.VMEM((TALL, WIDE), F32)
    return pl.pallas_call(
        main_kernel,
        out_shape=(shaped((slots, S2)), field, field, field),
        in_specs=[SMEM] + [VMEM] * 11 + [ANY],
        out_specs=(ANY,) * 4,
        scratch_shapes=[
            pltpu.VMEM((slots, 2 * S2), BF16), buffer, pltpu.VMEM(sums, F32), pltpu.VMEM(sums, BF16),
            tall, tall, tall, sems, pltpu.SemaphoreType.DMA((tiles, TILE // PART)),
        ],
        compiler_params=LIMITS,
        name="main",
    )(
        live_batches, pinned(places), ex, ey, mz, pinned(source), pinned(table), pinned(product),
        pinned(row_one), pinned(row_two), pinned(col_one), pinned(col_two), streamed(density),
    )


def solution(mesh):
    placed = (
        P(("gx", "gy"), None),
        P(("gx", "gy")),
        P(("gx", "gy")),
        P(),
        P(),
        P("gx", "gy"),
        P("gx", "gy"),
        P("gx", "gy"),
    )
    return jax.shard_map(
        shards,
        mesh=mesh,
        in_specs=placed,
        out_specs=(P(("gx", "gy"), None), P("gx", "gy"), P("gx", "gy"), P("gx", "gy")),
        check_vma=False,
    )
```

```python
import jax
import jax.numpy as jnp
from jax import lax
from jax.experimental import pallas as pl
from jax.experimental.pallas import tpu as pltpu
from jax.sharding import PartitionSpec as P

BATCH = 64
STEPS = 3
TILE = 1024
SMALL = 1024
PART = 256
COURANT = 0.5
CX = 128
CY = 256
S2 = 256
ROWS = 3 * S2 + 16
FIRST = 6
ORDERS = 24
LINES = 56
TALL = CX + 16
WIDE = CY + 256
F32 = jnp.float32
BF16 = jnp.bfloat16
NT = (((1,), (1,)), ((), ()))


def halves(x):
    hi = x.astype(BF16)
    return hi, (x - hi.astype(F32)).astype(BF16)


def fast_nt(a, b):
    return lax.dot_general(a, b, NT, preferred_element_type=F32)


def functionals_of(prop_ref, dip_ref):
    blocks = [halves(prop_ref[:, b * S2 : (b + 1) * S2]) for b in range(3)]

    def through(value, block):
        rows = value.shape[0]
        vh, vl = halves(value)
        wide = fast_nt(jnp.concatenate([vh, vl], axis=0), block[0])
        return wide[0:rows] + wide[rows:] + fast_nt(vh, block[1])

    dipoles = dip_ref[...]
    padded = jnp.concatenate([dipoles, jnp.zeros((6, S2), F32)], axis=0)
    reads = [through(padded, block)[0:2] for block in blocks]
    first = jnp.concatenate(
        [reads[0] - dipoles, reads[1], reads[2], jnp.zeros((2, S2), F32)], axis=0
    )
    second = [through(first, block)[0:FIRST] for block in blocks]
    return jnp.concatenate([first[0:FIRST], *second, jnp.zeros((8, S2), F32)], axis=0)


def table_kernel(prop_ref, readout_ref, table_ref):
    def put(rows, value):
        hi, lo = halves(value)
        table_ref[rows, 0:S2] = hi
        table_ref[rows, S2 : 2 * S2] = hi
        table_ref[rows, 2 * S2 :] = lo

    put(pl.ds(0, 16), jnp.concatenate([readout_ref[...], jnp.zeros((8, S2), F32)], axis=0))
    for b in range(3):
        block = prop_ref[:, b * S2 : (b + 1) * S2].T
        for q in range(S2 // 16):
            put(pl.ds(16 + 48 * q + 16 * b, 16), block[16 * q : 16 * q + 16])


def even(axis):
    return lax.axis_index(axis) % 2 == 0


def cells_of(cells_ref, t, size=TILE):
    cell = jnp.concatenate(
        [cells_ref[pl.ds(t * (size // 128) + j, 1), :] for j in range(size // 128)], axis=1
    )
    return cell >> 8, cell & (CY - 1)


def matches(index, size):
    return lax.broadcasted_iota(jnp.int32, (size, index.shape[1]), 0) == index


def one_hot(index, size):
    return jnp.where(matches(index, size), 1.0, 0.0).astype(BF16)


def count_of(live_ref, size=TILE):
    return live_ref[0] * BATCH // size


def tile_rows(t, size=TILE):
    return pl.ds(pl.multiple_of(t * size, size), size)


def sweep(lower, upper, body):
    def wrapped(t, carry):
        body(t)
        return carry

    lax.fori_loop(lower, upper, wrapped, 0)


def coefficient_kernel(
    live_ref, cells_hbm, ex_hbm, ey_hbm, mz_hbm, prop_hbm, dip_hbm, dens_hbm,
    readout_ref, one_ref, two_ref, west_ref, east_ref, hi_ref, lo_ref,
    prop_ref, cells_ref, buf, by_row, by_col, dip_ref, sems, loads,
):
    count = count_of(live_ref, SMALL)

    def copy(t):
        return pltpu.make_async_copy(dens_hbm.at[tile_rows(t, SMALL), :], buf.at[tile_rows(t, SMALL), :], sems.at[t])

    pairs = [(dip_hbm, dip_ref), (prop_hbm, prop_ref), (cells_hbm, cells_ref)]
    is_even = even("gx")
    starts = (jnp.where(is_even, CX - 8, 0), jnp.where(is_even, 0, CX - 8))
    for ref, start in zip((one_ref, two_ref), starts):
        start = pl.multiple_of(start, 8)
        for k, field in enumerate((mz_hbm, ex_hbm, ey_hbm)):
            pairs.append((field.at[pl.ds(start, 8), :], ref.at[pl.ds(8 * k, 8), :]))
    moves = [pltpu.make_async_copy(src, dst, loads.at[k]) for k, (src, dst) in enumerate(pairs)]
    for move in moves[:3]:
        move.start()
    sweep(0, count, lambda t: copy(t).start())
    for move in moves[3:]:
        move.start()
    for move in moves[:2]:
        move.wait()
    functionals = functionals_of(prop_ref, dip_ref)
    readout_ref[...] = functionals[0:8]
    fh, fl = halves(functionals)
    stacked = jnp.concatenate([fh, fl], axis=0)
    by_row[...] = jnp.zeros_like(by_row)
    by_col[...] = jnp.zeros_like(by_col)

    def picked(index, near, far, parts):
        out = []
        for place, rows in ((near[0], ORDERS), (near[1], ORDERS), (far[0], 8), (far[1], 8)):
            for part in parts:
                out.append(jnp.where(index == place, part[0:rows], 0.0))
        return jnp.concatenate(out, axis=0).astype(BF16)

    def body(t):
        copy(t).wait()
        dh, dl = halves(buf[tile_rows(t, SMALL), :])
        hi_ref[tile_rows(t, SMALL), :] = dh
        lo_ref[tile_rows(t, SMALL), :] = dl
        wide = fast_nt(stacked, dh)
        values = wide[0:32] + wide[32:64] + fast_nt(fh, dl)
        vh, vl = halves(values)
        parts = (vh.astype(F32), vl.astype(F32))
        row, col = cells_of(cells_ref, t, SMALL)
        by_row[...] += fast_nt(picked(row, (0, CX - 1), (1, CX - 2), parts), one_hot(col, CY))
        by_col[...] += fast_nt(picked(col, (0, CY - 1), (1, CY - 2), parts), one_hot(row, CX))

    for move in moves[2:]:
        move.wait()
    sweep(0, count, body)

    def side(ref, which):
        near = 2 * ORDERS * which
        far = 4 * ORDERS + 16 * which
        return (
            ref[near : near + ORDERS] + ref[near + ORDERS : near + 2 * ORDERS],
            ref[far : far + 8] + ref[far + 8 : far + 16],
        )

    low, high = side(by_row, 0), side(by_row, 1)
    for ref, if_even, if_odd in ((one_ref, high, low), (two_ref, low, high)):
        ref[24:48] = jnp.where(is_even, if_even[0], if_odd[0])
        ref[48:56] = jnp.where(is_even, if_even[1], if_odd[1])
    for which, ref in ((0, west_ref), (1, east_ref)):
        near, far = side(by_col, which)
        ref[0:ORDERS] = near
        ref[ORDERS:] = far


def sampled(t, cells_ref, fields):
    cell = cells_ref[pl.ds(pl.multiple_of(t * (TILE // 128), 8), TILE // 128), :]
    lane = cell & 127
    strip = cell >> 7
    values = [jnp.zeros(cell.shape, F32) for _ in fields]
    for r in range(CX):
        for half in range(CY // 128):
            here = strip == r * (CY // 128) + half
            for k, field in enumerate(fields):
                line = jnp.broadcast_to(field[r : r + 1, 128 * half : 128 * half + 128], cell.shape)
                found = jnp.take_along_axis(line, lane, axis=1)
                values[k] = jnp.where(here, found, values[k])
    return [
        jnp.concatenate([value[j : j + 1] for j in range(TILE // 128)], axis=1) for value in values
    ]


def tile_step(t, cells_ref, fields, make, source_ref, split=False):
    row, col = cells_of(cells_ref, t)
    hot_col = one_hot(col, CY)
    mask = matches(row, CX)
    if split:
        lines = jnp.dot(fields, hot_col, preferred_element_type=F32)
        sample_x, sample_y = (
            jnp.sum(
                jnp.where(mask, lines[k : k + CX] + lines[k + CX : k + 2 * CX], 0.0),
                axis=0,
                keepdims=True,
            )
            for k in (0, 2 * CX)
        )
    else:
        sample_x, sample_y = sampled(t, cells_ref, fields)
    product = make()
    reads = product(0, 8)
    current_x = reads[0:1] + sample_x * reads[2:3] + sample_y * reads[4:5]
    current_y = reads[1:2] + sample_x * reads[3:4] + sample_y * reads[5:6]
    marked = [
        jnp.where(mask, part.astype(F32), 0.0).astype(BF16)
        for current in (current_x, current_y)
        for part in halves(current)
    ]
    if not split:
        source_ref[...] += fast_nt(jnp.concatenate(marked, axis=0), hot_col)
    groups = []
    for k in range(4):
        if split:
            source_ref[k * CX : (k + 1) * CX] += fast_nt(marked[k], hot_col)
        for q in range(4 * k, 4 * k + 4):
            base = 16 + 48 * q
            groups.append(
                product(base, 16)
                + sample_x * product(base + 16, 16)
                + sample_y * product(base + 32, 16)
            )
    return jnp.concatenate(groups, axis=0)


def split_fields(ex, ey):
    xh, xl = halves(ex)
    yh, yl = halves(ey)
    return jnp.concatenate([xh, xl, yh, yl], axis=0)


def save_state(state_ref, t, updated):
    hi, lo = halves(updated.T)
    state_ref[tile_rows(t), 0:S2] = hi
    state_ref[tile_rows(t), S2:] = lo


def rows_of(value):
    return lambda start, size: value[start : start + size]


def stored_product(table_ref, state_ref, t):
    hi, lo = state_ref[tile_rows(t), 0:S2], state_ref[tile_rows(t), S2:]
    return fast_nt(table_ref[...], jnp.concatenate([hi, lo, hi], axis=1))


def first_kernel(
    live_ref, cells_ref, ex_ref, ey_ref, table_ref, hi_ref, lo_ref, state_ref, acc
):
    acc[...] = jnp.zeros_like(acc)

    def body(t):
        hi, lo = hi_ref[tile_rows(t), :], lo_ref[tile_rows(t), :]

        def make():
            return rows_of(fast_nt(table_ref[...], jnp.concatenate([hi, lo, hi], axis=1)))

        save_state(state_ref, t, tile_step(t, cells_ref, (ex_ref, ey_ref), make, acc))

    sweep(0, count_of(live_ref), body)


def ahead_kernel(live_ref, table_ref, state_ref, after_ref, product_ref):
    def body(t):
        product_ref[:, tile_rows(t)] = stored_product(table_ref, state_ref, t)

    sweep(0, count_of(live_ref), body)


def turned(value):
    rows, lanes = value.shape
    if rows < 128:
        value = jnp.concatenate([value, jnp.zeros((128 - rows, lanes), F32)], axis=0)
    elif rows < 256:
        value = jnp.concatenate([value, jnp.zeros((256 - rows, lanes), F32)], axis=0)
    return value.T


def ordered(axis, one_ref, two_ref):
    is_even = even(axis)
    one, two = one_ref[...], two_ref[...]
    return jnp.where(is_even, two, one), jnp.where(is_even, one, two)


def corner_kernel(
    ex_ref, ey_ref, mz_ref, west_ref, east_ref, one_ref, two_ref, after_ref, to_one_ref, to_two_ref
):
    tops, bottoms = ordered("gx", one_ref, two_ref)
    packages = []
    lane = lax.broadcasted_iota(jnp.int32, (TALL, 128), 1)
    for side, coefs_ref in ((0, west_ref), (1, east_ref)):
        half = slice(128 * side, 128 * side + 128)

        def tall(k, field_ref):
            rows = slice(8 * k, 8 * k + 8)
            return jnp.concatenate([tops[rows, half], field_ref[:, half], bottoms[rows, half]], axis=0)

        shift = 8 * side
        m = tall(0, mz_ref)
        if shift:
            m = pltpu.roll(m, shift, 1)
        x = pltpu.roll(tall(1, ex_ref), 8 + shift, 1)
        y = pltpu.roll(tall(2, ey_ref), 16 + shift, 1)
        items = jnp.where(lane < 8, m, jnp.where(lane < 16, x, y))
        coefs = coefs_ref[...]
        wide = pltpu.roll(jnp.concatenate([coefs, jnp.zeros_like(coefs)], axis=1), 8, 1)
        lower = wide[:, 0:128]
        upper = wide[:, 128:256]
        place = lax.broadcasted_iota(jnp.int32, (32, 128), 1)
        gap = jnp.zeros((16, 128), F32)

        def both(lines, near_from, far_from, near_to, far_to, base):
            near = lines[24:48, half]
            far = lines[48:56, half]
            at_near = jnp.concatenate(
                [
                    pltpu.roll(near, (near_to - near_from) % 128, 1),
                    pltpu.roll(near[0:8], (near_to - far_from) % 128, 1),
                ],
                axis=0,
            )
            at_far = jnp.concatenate(
                [
                    pltpu.roll(far, (far_to - near_from) % 128, 1),
                    gap,
                    pltpu.roll(far, (far_to - far_from) % 128, 1),
                ],
                axis=0,
            )
            return jnp.where(place == near_to, at_near, jnp.where(place == far_to, at_far, base))

        near_from, far_from = (127, 126) if side else (0, 1)
        spread = jnp.concatenate(
            [
                both(tops, near_from, far_from, 7, 6, lower),
                both(bottoms, near_from, far_from, 8, 9, upper),
            ],
            axis=1,
        )
        packages.append(jnp.concatenate([turned(items)[0:24], spread], axis=0))
    left, right = packages
    is_even = even("gy")
    to_one_ref[...] = jnp.where(is_even, right, left)
    to_two_ref[...] = jnp.where(is_even, left, right)


def linear(coefs, x, y):
    return (
        coefs[0:1] + x * coefs[2:3] + y * coefs[4:5],
        coefs[1:2] + x * coefs[3:4] + y * coefs[5:6],
    )


def quadratic(coefs, x0, y0, x1, y1):
    terms = [linear(coefs[FIRST * (c + 1) : FIRST * (c + 2)], x1, y1) for c in range(3)]
    return tuple(terms[0][k] + x0 * terms[1][k] + y0 * terms[2][k] for k in range(2))


def advance(x, y, z, source_x, source_y):
    y_next = pltpu.roll(y, TALL - 1, 0)
    x_next = pltpu.roll(x, WIDE - 1, 1)
    z = z - COURANT * ((y_next - y) - (x_next - x))
    x = x + COURANT * (z - pltpu.roll(z, 1, 1)) - source_x
    y = y - COURANT * (z - pltpu.roll(z, 1, 0)) - source_y
    return x, y, z


OWN = slice(128, 128 + CY)


def main_kernel(
    live_ref, cells_ref, ex_ref, ey_ref, mz_ref, acc_ref, table_ref, product_ref,
    row_one_ref, row_two_ref, col_one_ref, col_two_ref, dens_ref,
    evolved_ref, out_x, out_y, out_z, state, buf, acc, fld, xs, ys, zs, sems, parts,
):
    count = count_of(live_ref)
    total = dens_ref.shape[0] // TILE

    def fetch(t):
        return pltpu.make_async_copy(dens_ref.at[tile_rows(t), :], buf.at[tile_rows(t), :], sems.at[t])

    def write(t, c):
        rows = pl.ds(pl.multiple_of(t * TILE + c * PART, PART), PART)
        return pltpu.make_async_copy(buf.at[rows, :], evolved_ref.at[rows, :], parts.at[t, c])

    def write_all(t):
        for c in range(TILE // PART):
            write(t, c).start()

    def finish_all(t):
        for c in range(TILE // PART):
            write(t, c).wait()

    sweep(count, total, lambda t: fetch(t).start())

    tops, bottoms = ordered("gx", row_one_ref, row_two_ref)
    left, right = ordered("gy", col_one_ref, col_two_ref)
    left_items = turned(left[0:24])[0:TALL]
    right_items = turned(right[0:24])[0:TALL]

    def extended(k, field_ref):
        rows = slice(8 * k, 8 * k + 8)
        middle = jnp.concatenate([tops[rows, :], field_ref[...], bottoms[rows, :]], axis=0)
        before = pltpu.roll(left_items, 120 - 8 * k, 1)
        after = right_items
        if k:
            after = pltpu.roll(after, 128 - 8 * k, 1)
        return jnp.concatenate([before, middle, after], axis=1)

    zs[...] = extended(0, mz_ref)
    xs[...] = extended(1, ex_ref)
    ys[...] = extended(2, ey_ref)

    sides = []
    for package, near, far in ((left, 7, 6), (right, 0, 1)):
        lines = package[0:24]
        coefs = package[24:]
        near_x, near_y = lines[8 + near : 9 + near], lines[16 + near : 17 + near]
        far_x, far_y = lines[8 + far : 9 + far], lines[16 + far : 17 + far]
        sides.append(
            (
                coefs,
                near_x,
                near_y,
                linear(coefs[0:FIRST], near_x, near_y),
                linear(coefs[ORDERS : ORDERS + FIRST], far_x, far_y),
            )
        )
    lane = lax.broadcasted_iota(jnp.int32, (TALL, 128), 1)
    line = lax.broadcasted_iota(jnp.int32, (8, CY), 0)

    def assembled(tops, rows, bottoms, before, after):
        middle = jnp.concatenate([tops, rows, bottoms], axis=0)
        return jnp.concatenate([before, middle, after], axis=1)

    (lc, lx0, ly0, lnear, lfar), (rc, rx0, ry0, rnear, rfar) = sides
    columns = turned(
        jnp.concatenate(
            [lfar[0], lnear[0], lfar[1], lnear[1], rnear[0], rfar[0], rnear[1], rfar[1]], axis=0
        )
    )[0:TALL]
    zero_line = jnp.zeros((8, CY), F32)
    starts = []
    top_lines = []
    bottom_lines = []
    for lines_of, near, far, out in (
        (tops, 7, 6, top_lines),
        (bottoms, 0, 1, bottom_lines),
    ):
        near_x, near_y = lines_of[8 + near : 9 + near, :], lines_of[16 + near : 17 + near, :]
        far_x, far_y = lines_of[8 + far : 9 + far, :], lines_of[16 + far : 17 + far, :]
        starts.append((near_x, near_y))
        at_near = linear(lines_of[24 : 24 + FIRST, :], near_x, near_y)
        at_far = linear(lines_of[48 : 48 + FIRST, :], far_x, far_y)
        for k in range(2):
            out.append(
                jnp.where(line == near, at_near[k], jnp.where(line == far, at_far[k], zero_line))
            )

    def own(ref, k):
        return ref[2 * k * CX : (2 * k + 1) * CX] + ref[(2 * k + 1) * CX : (2 * k + 2) * CX]

    sources = []
    for k in range(2):
        before = jnp.where(lane >= 126, pltpu.roll(columns, 126 - 2 * k, 1), 0.0)
        after = jnp.where(lane < 2, pltpu.roll(columns, 124 - 2 * k, 1), 0.0)
        sources.append(assembled(top_lines[k], own(acc_ref, k), bottom_lines[k], before, after))
    x, y, z = advance(xs[...], ys[...], zs[...], *sources)
    xs[...] = x
    ys[...] = y
    zs[...] = z

    def flush(t):
        fetch(t).wait()
        write_all(t)

    sweep(count, total, flush)

    fields = [ref.at[pl.ds(8, CX), pl.ds(128, CY)] for ref in (xs, ys)]
    fld[...] = split_fields(*(field[...] for field in fields))
    acc[...] = jnp.zeros_like(acc)

    def second(t):
        def make():
            return lambda start, size: product_ref[start : start + size, tile_rows(t)]

        save_state(state, t, tile_step(t, cells_ref, fld[...], make, acc, True))

    sweep(0, count, second)

    x = xs[...]
    y = ys[...]
    xl, yl = x[:, 0:128], y[:, 0:128]
    xr, yr = x[:, 384:512], y[:, 384:512]
    edge = jnp.where(
        lane == 127,
        xl,
        jnp.where(
            lane == 126,
            pltpu.roll(yl, 127, 1),
            jnp.where(lane == 0, xr, jnp.where(lane == 1, pltpu.roll(yr, 1, 1), 0.0)),
        ),
    )
    rows = turned(edge)
    ends_l = quadratic(lc, lx0, ly0, rows[127:128], rows[126:127])
    ends_r = quadratic(rc, rx0, ry0, rows[0:1], rows[1:2])
    columns = turned(
        jnp.concatenate([ends_l[0], ends_l[1], ends_r[0], ends_r[1], jnp.zeros((4, CY), F32)], axis=0)
    )[0:TALL]
    lines = []
    for (x0, y0), lines_of, near, at in (
        (starts[0], tops, 7, 7),
        (starts[1], bottoms, 0, 8 + CX),
    ):
        ends = quadratic(
            lines_of[24:48, :], x0, y0, x[at : at + 1, OWN], y[at : at + 1, OWN]
        )
        lines.append([jnp.where(line == near, ends[k], zero_line) for k in range(2)])
    sources = []
    for k in range(2):
        before = jnp.where(lane == 127, pltpu.roll(columns, 127 - k, 1), 0.0)
        after = jnp.where(lane == 0, pltpu.roll(columns, 126 - k, 1), 0.0)
        sources.append(assembled(lines[0][k], own(acc, k), lines[1][k], before, after))
    x, y, z = advance(x, y, zs[...], *sources)
    xs[...] = x
    ys[...] = y
    zs[...] = z
    acc[...] = jnp.zeros_like(acc)

    def third(t):
        def make():
            return rows_of(stored_product(table_ref, state, t))

        updated = tile_step(t, cells_ref, fields, make, acc)
        for c in range(TILE // PART):
            rows = pl.ds(pl.multiple_of(t * TILE + c * PART, PART), PART)
            buf[rows, :] = updated[:, c * PART : (c + 1) * PART].T
            write(t, c).start()

    sweep(0, count, third)
    blank = jnp.zeros((TALL, 128), F32)
    sources = [assembled(zero_line, own(acc, k), zero_line, blank, blank) for k in range(2)]
    x, y, z = advance(xs[...], ys[...], zs[...], *sources)
    xs[8 : 8 + CX, OWN] = x[8 : 8 + CX, OWN]
    ys[8 : 8 + CX, OWN] = y[8 : 8 + CX, OWN]
    zs[8 : 8 + CX, OWN] = z[8 : 8 + CX, OWN]
    saves = [
        pltpu.make_async_copy(src.at[pl.ds(8, CX), pl.ds(128, CY)], dst, sems.at[total + k])
        for k, (src, dst) in enumerate(((xs, out_x), (ys, out_y), (zs, out_z)))
    ]
    for save in saves:
        save.start()
    sweep(0, total, finish_all)
    for save in saves:
        save.wait()


VMEM = pl.BlockSpec(memory_space=pltpu.VMEM)
SMEM = pl.BlockSpec(memory_space=pltpu.SMEM)
ANY = pl.BlockSpec(memory_space=pl.ANY)
LIMITS = pltpu.CompilerParams(vmem_limit_bytes=40 << 20)


def shaped(shape, dtype=F32):
    return jax.ShapeDtypeStruct(shape, dtype)


def pairs(axis, first):
    count = lax.axis_size(axis)
    swaps = [(i % count, (i + 1) % count) for i in range(first, first + count, 2)]
    return swaps + [(b, a) for a, b in swaps]


def pinned(value):
    return pltpu.with_memory_space_constraint(value, pltpu.VMEM)


def streamed(value):
    return pltpu.with_memory_space_constraint(value, pltpu.HBM)


def held(shape, dtype=F32):
    return pltpu.VMEM(shape, dtype)


def shards(density, cell_index, live_batches, propagator, dipoles, ex, ey, mz):
    slots = density.shape[0]
    tiles = slots // TILE
    cells = cell_index.reshape(slots // 128, 128)
    buffer = pltpu.VMEM((slots, S2), F32)
    sems = pltpu.SemaphoreType.DMA((tiles + 3,))
    sums = (4 * CX, CY)
    half = held((slots, S2), BF16)
    readout, one, two, west, east, hi, lo, fetched, places = pl.pallas_call(
        coefficient_kernel,
        out_shape=(
            shaped((8, S2)),
            shaped((LINES, CY)),
            shaped((LINES, CY)),
            shaped((32, CX)),
            shaped((32, CX)),
            half,
            half,
            held(propagator.shape),
            held(cells.shape, jnp.int32),
        ),
        in_specs=[SMEM] + [ANY] * 7,
        out_specs=(VMEM,) * 9,
        scratch_shapes=[
            buffer,
            pltpu.VMEM((128, CY), F32),
            pltpu.VMEM((128, CX), F32),
            pltpu.VMEM(dipoles.shape, F32),
            pltpu.SemaphoreType.DMA((slots // SMALL,)),
            pltpu.SemaphoreType.DMA((9,)),
        ],
        compiler_params=LIMITS,
        name="coefficients",
    )(
        live_batches,
        *(streamed(value) for value in (cells, ex, ey, mz, propagator, dipoles, density)),
    )
    row_one = lax.ppermute(one, "gx", pairs("gx", 0))
    row_two = lax.ppermute(two, "gx", pairs("gx", 1))
    table = pl.pallas_call(
        table_kernel,
        out_shape=held((ROWS, 3 * S2), BF16),
        in_specs=[VMEM] * 2,
        out_specs=VMEM,
        compiler_params=LIMITS,
        name="table",
    )(pinned(fetched), readout)
    state, source = pl.pallas_call(
        first_kernel,
        out_shape=(held((slots, 2 * S2), BF16), held(sums)),
        in_specs=[SMEM] + [VMEM] * 6,
        out_specs=(VMEM,) * 2,
        compiler_params=LIMITS,
        name="first",
    )(live_batches, pinned(places), ex, ey, pinned(table), pinned(hi), pinned(lo))
    package = held((LINES, CY))
    to_one, to_two = pl.pallas_call(
        corner_kernel,
        out_shape=(package, package),
        in_specs=[VMEM] * 5 + [VMEM] * 2 + [ANY],
        out_specs=(VMEM,) * 2,
        compiler_params=LIMITS,
        name="corners",
    )(ex, ey, mz, west, east, pinned(row_one), pinned(row_two), pinned(source))
    col_one = lax.ppermute(to_one, "gy", pairs("gy", 0))
    col_two = lax.ppermute(to_two, "gy", pairs("gy", 1))
    product = pl.pallas_call(
        ahead_kernel,
        out_shape=held((ROWS, slots)),
        in_specs=[SMEM] + [VMEM] * 2 + [ANY],
        out_specs=VMEM,
        compiler_params=LIMITS,
        name="ahead",
    )(live_batches, pinned(table), pinned(state), pinned(to_two))
    field = shaped((CX, CY))
    tall = pltpu.VMEM((TALL, WIDE), F32)
    return pl.pallas_call(
        main_kernel,
        out_shape=(shaped((slots, S2)), field, field, field),
        in_specs=[SMEM] + [VMEM] * 11 + [ANY],
        out_specs=(ANY,) * 4,
        scratch_shapes=[
            pltpu.VMEM((slots, 2 * S2), BF16), buffer, pltpu.VMEM(sums, F32), pltpu.VMEM(sums, BF16),
            tall, tall, tall, sems, pltpu.SemaphoreType.DMA((tiles, TILE // PART)),
        ],
        compiler_params=LIMITS,
        name="main",
    )(
        live_batches, pinned(places), ex, ey, mz, pinned(source), pinned(table), pinned(product),
        pinned(row_one), pinned(row_two), pinned(col_one), pinned(col_two), streamed(density),
    )


def solution(mesh):
    placed = (
        P(("gx", "gy"), None),
        P(("gx", "gy")),
        P(("gx", "gy")),
        P(),
        P(),
        P("gx", "gy"),
        P("gx", "gy"),
        P("gx", "gy"),
    )
    return jax.shard_map(
        shards,
        mesh=mesh,
        in_specs=placed,
        out_specs=(P(("gx", "gy"), None), P("gx", "gy"), P("gx", "gy"), P("gx", "gy")),
        check_vma=False,
    )
```
